256 devices in a mesh: river: 8 (over y, core), leaf: 32 (over z, x).
Axes of the slice: x: 4, y: 4, z: 8, core: 2. Of those that a mesh axis runs over, the one named last changes fastest.
Arguments:
- range_zero: float32 [16, 1344], P(None, 'leaf'), may hold values from 0.0001 to 0.001
- range_one: float32 [16, 1344], P(None, 'leaf'), may hold values from 0.0001 to 0.001
- turn_regret: float32 [8, 16, 1344], P('river', None, 'leaf'), may hold values from 0.05 to 5
- river_regret_zero: float32 [8, 1344, 3072], P('river', 'leaf'), may hold values from 0.05 to 5
- river_regret_one: float32 [8, 1344, 9216], P('river', 'leaf'), may hold values from 0.05 to 5
- hand_cards: int32 [1344, 2], replicated, may hold values from 0 to 52, as said below
- dealt_cards: int32 [52], replicated, may hold values from 0 to 51, as said below
- hand_ranks: int32 [48, 1344], replicated, may hold values from 0 to 7461
- leaf_pots: int32 [8, 12], P('river'), may hold values from 2 to 64
- leaf_kinds: int32 [8, 12], P('river'), may hold values from 0 to 2
Outputs:
- new_turn_regret: float32 [8, 16, 1344], P('river', None, 'leaf')
- new_river_zero: float32 [8, 1344, 3072], P('river', 'leaf')
- new_river_one: float32 [8, 1344, 9216], P('river', 'leaf')
- root_values: float32 [2, 16, 1344], P(None, None, 'leaf')
The draws below stay inside these ranges and needn't reach their ends.
Inputs may be any that keep to these rules, and one draw needn't show every extreme that they name: `hand_cards`: each slot holds the two card numbers of a distinct two-card hand; every one of the 1,326 hands has a slot; empty slots hold 52 twice. `dealt_cards`: all entries are distinct card numbers. `hand_ranks`: A higher rank wins the showdown, equal ranks split it. `leaf_kinds`: 0 is a showdown, 1 a fold by player one, 2 a fold by player zero.
All inputs are finite; a program needn't handle non-finite values.
Results may differ from the reference program's by a relative error of at most 0.0003.
Values may be sent and summed in bfloat16 or wider, within the bound.
A program may use at most 128 MiB of HBM per device.

```python
import math
import jax
import jax.numpy as jnp
import numpy as np
from jax import lax

HANDS = 1344
RIVERS = 48
MOVES_ZERO = 4
MOVES_ONE = 3
SUBGAMES = 16
LEAVES = 12
LINES = 8


def draw_hand_cards(key, part):
    first_table, second_table = np.triu_indices(52, 1)
    hand_count = min(HANDS, 1326)
    shuffled = jax.random.permutation(jax.random.fold_in(key, 11), 1326)[:hand_count]
    first_card = jnp.asarray(first_table, dtype=jnp.int32)[shuffled]
    second_card = jnp.asarray(second_table, dtype=jnp.int32)[shuffled]
    hand_pairs = jnp.stack([first_card, second_card], axis=1)
    return jnp.pad(hand_pairs, ((0, HANDS - hand_count), (0, 0)), constant_values=52)


def draw_dealt_cards(key, part):
    shuffled = jax.random.permutation(jax.random.fold_in(key, 17), 52)
    return shuffled[:RIVERS + 4].astype(jnp.int32)


def touch_ends(entries, rng, smallest, largest):
    longest = entries.shape.index(max(entries.shape))
    spots = []
    for shift in (0, 1):
        where = [jax.random.randint(jax.random.fold_in(rng, axis), (), 0, length) for axis, length in enumerate(entries.shape)]
        where[longest] = (where[longest] + shift) % entries.shape[longest]
        spots.append(tuple(where))
    return entries.at[spots[0]].set(smallest).at[spots[1]].set(largest)


def block_scale(rng, shape, split, low, top_value):
    def one(position, parts):
        draws = jax.random.uniform(jax.random.fold_in(jax.random.fold_in(rng, 6), position), (parts,), jnp.float32, low / len(split), top_value / len(split))
        return jnp.repeat(jnp.exp(draws), shape[position] // parts).reshape((-1,) + (1,) * (len(shape) - position - 1))

    level = one(*split[0])
    for cut in split[1:]:
        level = level * one(*cut)
    return level


def setup_inputs(seed: int = 0) -> dict:
    key_of = jax.random.split(jax.random.key(seed), 11)
    return {
        "range_zero": jnp.clip(jnp.exp(math.log(0.001) - 2.3025852 * jax.random.uniform(key_of[0], (SUBGAMES, HANDS), jnp.float32) ** block_scale(key_of[0], (SUBGAMES, HANDS), ((1, 32),), -0.2, 0.2)), 0.0001, 0.001),
        "range_one": jnp.clip(jnp.exp(math.log(0.001) - 2.3025852 * jax.random.uniform(key_of[1], (SUBGAMES, HANDS), jnp.float32) ** block_scale(key_of[1], (SUBGAMES, HANDS), ((1, 32),), -0.2, 0.2)), 0.0001, 0.001),
        "turn_regret": jnp.clip(jnp.exp(math.log(5.0) - 4.6051702 * jax.random.uniform(key_of[2], (LINES, SUBGAMES, HANDS), jnp.float32) ** block_scale(key_of[2], (LINES, SUBGAMES, HANDS), ((0, 8), (2, 32)), -0.2, 0.2)), 0.05, 5.0),
        "river_regret_zero": jnp.clip(jnp.exp(math.log(5.0) - 4.6051702 * jax.random.uniform(key_of[3], (LINES, HANDS, RIVERS * MOVES_ZERO * SUBGAMES), jnp.float32) ** block_scale(key_of[3], (LINES, HANDS, RIVERS * MOVES_ZERO * SUBGAMES), ((0, 8), (1, 32)), -0.2, 0.2)), 0.05, 5.0),
        "river_regret_one": jnp.clip(jnp.exp(math.log(5.0) - 4.6051702 * jax.random.uniform(key_of[4], (LINES, HANDS, RIVERS * MOVES_ZERO * MOVES_ONE * SUBGAMES), jnp.float32) ** block_scale(key_of[4], (LINES, HANDS, RIVERS * MOVES_ZERO * MOVES_ONE * SUBGAMES), ((0, 8), (1, 32)), -0.2, 0.2)), 0.05, 5.0),
        "hand_cards": draw_hand_cards(jax.random.fold_in(key_of[10], 71), 0),
        "dealt_cards": draw_dealt_cards(jax.random.fold_in(key_of[10], 71), 0),
        "hand_ranks": touch_ends(jax.random.randint(key_of[7], (RIVERS, HANDS), 0, 7462), jax.random.fold_in(key_of[7], 1), 0, 7461).astype(jnp.int32),
        "leaf_pots": touch_ends(jax.random.randint(key_of[8], (LINES, LEAVES), 2, 65), jax.random.fold_in(key_of[8], 1), 2, 64).astype(jnp.int32),
        "leaf_kinds": touch_ends(jax.random.randint(key_of[9], (LINES, LEAVES), 0, 3), jax.random.fold_in(key_of[9], 1), 0, 2).astype(jnp.int32),
    }


chance_weight = 1.0 / 44.0


def hand_validity(hand_cards, dealt_cards):
    first_card = hand_cards[:, 0]
    second_card = hand_cards[:, 1]
    board_cards = dealt_cards[:4]
    river_cards = dealt_cards[4:]
    on_board = jnp.any(first_card[:, None] == board_cards[None, :], axis=1) | jnp.any(second_card[:, None] == board_cards[None, :], axis=1)
    usable = (first_card < 52) & (second_card < 52) & jnp.logical_not(on_board)
    blocked = (first_card[None, :] == river_cards[:, None]) | (second_card[None, :] == river_cards[:, None])
    return (usable[None, :] & jnp.logical_not(blocked)).astype(jnp.float32)


def card_intersection(hand_cards):
    first_card = hand_cards[:, 0]
    second_card = hand_cards[:, 1]
    shared = (first_card[:, None] == first_card[None, :]) | (first_card[:, None] == second_card[None, :])
    shared = shared | (second_card[:, None] == first_card[None, :]) | (second_card[:, None] == second_card[None, :])
    return jnp.logical_not(shared).astype(jnp.float32)


def payoff_block(validity, disjoint, ranking, pot_value, kind_value):
    showdown = jnp.sign(ranking[:, None] - ranking[None, :]).astype(jnp.float32)
    outcome = jnp.where(kind_value == 0, showdown, jnp.where(kind_value == 1, 1.0, -1.0))
    scaled = pot_value.astype(jnp.float32) * outcome * disjoint * validity[:, None] * validity[None, :]
    return scaled.astype(jnp.bfloat16)


def reference(range_zero, range_one, turn_regret, river_regret_zero, river_regret_one, hand_cards, dealt_cards, hand_ranks, leaf_pots, leaf_kinds):
    regret_zero = river_regret_zero.reshape(LINES, HANDS, RIVERS, MOVES_ZERO, SUBGAMES).transpose(0, 2, 3, 4, 1)
    regret_one = river_regret_one.reshape(LINES, HANDS, RIVERS, MOVES_ZERO, MOVES_ONE, SUBGAMES).transpose(0, 2, 3, 4, 5, 1)
    validity = hand_validity(hand_cards, dealt_cards)
    disjoint = card_intersection(hand_cards)
    turn_share = turn_regret / jnp.sum(turn_regret, axis=0, keepdims=True)
    zero_share = regret_zero / jnp.sum(regret_zero, axis=2, keepdims=True)
    one_share = regret_one / jnp.sum(regret_one, axis=3, keepdims=True)
    weighted = range_zero[None] * turn_share
    zero_reach = (weighted[:, None, None] * zero_share).astype(jnp.bfloat16)
    one_reach = (range_one[None, None, None, None] * one_share).astype(jnp.bfloat16)

    def river_node(node_items):
        zero_node, one_node, river_index, pots_row, kinds_row = node_items
        zero_leaf = jnp.repeat(zero_node, MOVES_ONE, axis=0).astype(jnp.float32)
        one_leaf = one_node.reshape(LEAVES, SUBGAMES, HANDS).astype(jnp.float32)
        payoffs = jax.vmap(payoff_block, in_axes=(None, None, None, 0, 0))(validity[river_index], disjoint, hand_ranks[river_index], pots_row, kinds_row)
        payoffs_wide = payoffs.astype(jnp.float32)
        zero_value = jnp.einsum("lsj,lij->lsi", one_leaf, payoffs_wide, precision=lax.Precision.HIGHEST)
        one_value = -jnp.einsum("lsi,lij->lsj", zero_leaf, payoffs_wide, precision=lax.Precision.HIGHEST)
        return zero_value, one_value

    node_count = LINES * RIVERS
    river_index_all = jnp.tile(jnp.arange(RIVERS, dtype=jnp.int32), LINES)
    zero_values, one_values = lax.map(river_node, (
        zero_reach.reshape(node_count, MOVES_ZERO, SUBGAMES, HANDS),
        one_reach.reshape(node_count, MOVES_ZERO, MOVES_ONE, SUBGAMES, HANDS),
        river_index_all,
        jnp.repeat(leaf_pots, RIVERS, axis=0),
        jnp.repeat(leaf_kinds, RIVERS, axis=0)))
    action_zero = jnp.sum(zero_values.reshape(LINES, RIVERS, MOVES_ZERO, MOVES_ONE, SUBGAMES, HANDS), axis=3)
    leaf_one = one_values.reshape(LINES, RIVERS, MOVES_ZERO, MOVES_ONE, SUBGAMES, HANDS)
    node_zero = jnp.sum(zero_share * action_zero, axis=2)
    new_zero = jnp.maximum(regret_zero + action_zero - node_zero[:, :, None], 0.0)
    node_one = jnp.sum(one_share * leaf_one, axis=3)
    new_one = jnp.maximum(regret_one + leaf_one - node_one[:, :, :, None], 0.0)
    line_zero = chance_weight * jnp.sum(node_zero, axis=1)
    line_one = chance_weight * jnp.sum(node_one, axis=(1, 2))
    root_zero = jnp.sum(turn_share * line_zero, axis=0)
    root_one = jnp.sum(line_one, axis=0)
    new_turn = jnp.maximum(turn_regret + line_zero - root_zero[None], 0.0)
    new_zero_out = new_zero.transpose(0, 4, 1, 2, 3).reshape(LINES, HANDS, RIVERS * MOVES_ZERO * SUBGAMES)
    new_one_out = new_one.transpose(0, 5, 1, 2, 3, 4).reshape(LINES, HANDS, RIVERS * MOVES_ZERO * MOVES_ONE * SUBGAMES)
    return new_turn, new_zero_out, new_one_out, jnp.stack([root_zero, root_one])
```

```python
import jax
import jax.numpy as jnp
from jax import lax
from jax.experimental import pallas as pl
from jax.experimental.pallas import tpu as pltpu
from jax.sharding import PartitionSpec as P

MESH = pl.DeviceIdType.MESH
F32 = jnp.float32
BF16 = jnp.bfloat16
RIVERS = 48
MOVES_ZERO = 4
MOVES_ONE = 3
SUBGAMES = 16
WORKERS = 24
PEERS = 32
HP = 48
KP = PEERS * HP
MB = 384
CHANCE = 1.0 / 44.0


def worker_leaf(w):
    z = w // 3
    x = lax.rem(w - 3 * z + 1 + z, 4)
    return 4 * z + x


def leaf_worker(leaf):
    z = leaf // 4
    x = leaf - 4 * z
    k = lax.rem(x - 1 - z + 12, 4)
    return k, 3 * z + k


def lanes(rows):
    return lax.broadcasted_iota(jnp.int32, (rows, 128), 1)


def gather_lanes(x, index):
    return jnp.take_along_axis(x, index, axis=1, mode="promise_in_bounds")


def roll_half(x):
    return pltpu.roll(x, 64, 1)


def action_sum(x, lane):
    x = x + gather_lanes(x, (lane & 64) | ((lane + 16) & 63))
    return x + gather_lanes(x, (lane & 64) | ((lane + 32) & 63))


def split_moves(tiles, lane):
    slot, sub = lane // 16, lane % 16
    out = []
    for b in range(MOVES_ONE):
        group = (3 * (slot - b + 8)) % 8
        tile = (3 * group + b) // 8
        picked = jnp.where(tile == 0, tiles[0], jnp.where(tile == 1, tiles[1], tiles[2]))
        out.append(gather_lanes(picked, ((3 * slot + b) % 8) * 16 + sub))
    return out


def join_moves(parts, lane):
    slot, sub = lane // 16, lane % 16
    moved = []
    for b in range(MOVES_ONE):
        group = (3 * (slot - b + 8)) % 8
        moved.append(gather_lanes(parts[b], group * 16 + sub))
    out = []
    for v in range(3):
        b = (8 * v + slot) % 3
        out.append(jnp.where(b == 0, moved[0], jnp.where(b == 1, moved[1], moved[2])))
    return out


def tile_selector():
    sub = lax.broadcasted_iota(jnp.int32, (SUBGAMES, 128), 0)
    lane = lanes(SUBGAMES)
    return (lane % SUBGAMES == sub).astype(F32)


def to_lanes(x):
    return lax.dot_general(
        x,
        tile_selector(),
        (((0,), (0,)), ((), ())),
        precision=lax.Precision.HIGHEST,
        preferred_element_type=F32,
    )


def zero_shares(rz, w, lane):
    x = rz[:, pl.ds(128 * w, 128)]
    return x, x / action_sum(x, lane)


def one_shares(ro, w, lane):
    tiles = [ro[:, pl.ds(384 * w + 128 * v, 128)] for v in range(3)]
    regrets = split_moves(tiles, lane)
    scale = 1.0 / (regrets[0] + regrets[1] + regrets[2])
    return regrets, [r * scale for r in regrets]


def prep_kernel(rz, ro, range_zero, range_one, turn_regret, turn_total, y):
    hands = rz.shape[0]
    lane = lanes(hands)
    low = lane < 64
    weight_zero = to_lanes(range_zero[...] * (turn_regret[...] / turn_total[...]))
    weight_one = to_lanes(range_one[...])

    def step(w, carry):
        _, zs = zero_shares(rz, w, lane)
        _, os = one_shares(ro, w, lane)
        z = weight_zero * zs
        o = [weight_one * s for s in os]
        packed = (
            jnp.where(low, z, roll_half(o[0])),
            jnp.where(low, o[1], roll_half(o[2])),
            jnp.where(low, roll_half(z), o[0]),
            jnp.where(low, roll_half(o[1]), o[2]),
        )
        for k in range(4):
            y[w, k, 32:48] = jnp.zeros((16, 128), BF16)
            y[w, k, 0:hands] = packed[k].astype(BF16)
        return carry

    lax.fori_loop(0, WORKERS, step, 0)


def entry_barrier(line, leaf):
    barrier = pltpu.get_barrier_semaphore()

    def greet(k, carry):
        peer = lax.rem(leaf + k, PEERS)
        pl.semaphore_signal(barrier, inc=1, device_id=(line, peer), device_id_type=MESH)
        return carry

    lax.fori_loop(1, PEERS, greet, 0)
    pl.semaphore_wait(barrier, PEERS - 1)


def forward_kernel(y, recv, send_sem, recv_sem, local_sem):
    line, leaf = lax.axis_index("river"), lax.axis_index("leaf")
    k_self, w_self = leaf_worker(leaf)
    is_worker = k_self < 3
    entry_barrier(line, leaf)
    first = 3 * (leaf // 4)

    def copy(w, peer):
        return pltpu.make_async_remote_copy(
            src_ref=y.at[w],
            dst_ref=recv.at[leaf],
            send_sem=send_sem.at[w],
            recv_sem=recv_sem.at[leaf],
            device_id=(line, peer),
            device_id_type=MESH,
        )

    def start(k, carry):
        w = lax.rem(first + k, WORKERS)
        peer = worker_leaf(w)

        @pl.when(peer != leaf)
        def _():
            copy(w, peer).start()

        return carry

    lax.fori_loop(0, WORKERS, start, 0)

    @pl.when(is_worker)
    def _():
        own = pltpu.make_async_copy(y.at[w_self], recv.at[leaf], local_sem)
        own.start()
        own.wait()

        def arrive(k, carry):
            source = lax.rem(leaf + k, PEERS)
            pltpu.make_async_remote_copy(
                src_ref=y.at[0],
                dst_ref=recv.at[source],
                send_sem=send_sem.at[0],
                recv_sem=recv_sem.at[source],
                device_id=(line, source),
                device_id_type=MESH,
            ).wait_recv()
            return carry

        lax.fori_loop(1, PEERS, arrive, 0)

    def sent(k, carry):
        w = lax.rem(first + k, WORKERS)
        peer = worker_leaf(w)

        @pl.when(peer != leaf)
        def _():
            copy(w, peer).wait_send()

        return carry

    lax.fori_loop(0, WORKERS, sent, 0)


def backward_kernel(out, back, send_sem, recv_sem, local_sem):
    line, leaf = lax.axis_index("river"), lax.axis_index("leaf")
    k_self, w_self = leaf_worker(leaf)
    is_worker = k_self < 3
    entry_barrier(line, leaf)
    first = 3 * (leaf // 4)

    def copy(peer):
        return pltpu.make_async_remote_copy(
            src_ref=out.at[peer],
            dst_ref=back.at[w_self],
            send_sem=send_sem.at[peer],
            recv_sem=recv_sem.at[w_self],
            device_id=(line, peer),
            device_id_type=MESH,
        )

    @pl.when(is_worker)
    def _():
        def start(k, carry):
            copy(lax.rem(leaf + k, PEERS)).start()
            return carry

        lax.fori_loop(1, PEERS, start, 0)
        own = pltpu.make_async_copy(out.at[leaf], back.at[w_self], local_sem)
        own.start()
        own.wait()

    def arrive(k, carry):
        w = lax.rem(first + k, WORKERS)
        peer = worker_leaf(w)

        @pl.when(peer != leaf)
        def _():
            pltpu.make_async_remote_copy(
                src_ref=out.at[0],
                dst_ref=back.at[w],
                send_sem=send_sem.at[0],
                recv_sem=recv_sem.at[w],
                device_id=(line, peer),
                device_id_type=MESH,
            ).wait_recv()

        return carry

    lax.fori_loop(0, WORKERS, arrive, 0)

    @pl.when(is_worker)
    def _():
        def sent(k, carry):
            copy(lax.rem(leaf + k, PEERS)).wait_send()
            return carry

        lax.fori_loop(1, PEERS, sent, 0)


def leaf_scales(pots, kinds, rows):
    action = (lanes(rows) // SUBGAMES) % MOVES_ZERO
    show, fold = [], []
    for b in range(MOVES_ONE):
        s = jnp.zeros((rows, 128), F32)
        f = jnp.zeros((rows, 128), F32)
        for a in range(MOVES_ZERO):
            pot = pots[0, a * MOVES_ONE + b].astype(F32)
            kind = kinds[0, a * MOVES_ONE + b]
            here = action == a
            s = jnp.where(here, jnp.where(kind == 0, pot, 0.0), s)
            f = jnp.where(here, jnp.where(kind == 0, 0.0, jnp.where(kind == 1, pot, -pot)), f)
        show.append(s)
        fold.append(f)
    return show, fold


def column(rows, select):
    return lax.dot_general(
        rows, select, (((0,), (0,)), ((), ())), preferred_element_type=F32
    )


def blocks_kernel(recv, cards, ranks, dealt, pots, kinds, out, x, mat, dis, col, inc):
    leaf = lax.axis_index("leaf")
    k_self, w_self = leaf_worker(leaf)

    @pl.when(k_self < 3)
    def _():
        low = lanes(8) < 64
        one_row = (lax.broadcasted_iota(jnp.int32, (8, 128), 0))
        pick = lambda r, scale: jnp.where(one_row == r, scale, 0.0).astype(BF16)
        card_rows = cards[...].astype(BF16)
        first = column(card_rows, pick(0, 1.0))
        second = column(card_rows, pick(1, 1.0))
        board = [dealt[k].astype(F32) for k in range(4)]
        usable = (first < 52.0) & (second < 52.0)
        for k in range(4):
            usable = usable & (first != board[k]) & (second != board[k])
        valid = []
        for c in range(2):
            river = dealt[4 + 2 * w_self + c].astype(F32)
            ok = usable & (first != river) & (second != river)
            valid.append(ok.astype(F32))
        card = lanes(KP).astype(F32)
        inc[...] = ((first == card) | (second == card)).astype(BF16)
        rank_rows = ranks[...]
        high_rows = jnp.floor(rank_rows * (1.0 / 64.0))
        low_rows = rank_rows - 64.0 * high_rows
        for c in range(2):
            col[c] = column(high_rows.astype(BF16), pick(c, 64.0)) + column(
                low_rows.astype(BF16), pick(c, 1.0)
            )
            col[2 + c] = valid[c]
            vb = valid[c].astype(BF16)
            for k in range(2):
                x[:, pl.ds(256 * c + 128 * k, 128)] = (
                    recv[:, 2 * c + k].reshape(KP, 128) * vb
                )
        show, fold = leaf_scales(pots, kinds, 8)
        show = [s[0:1] for s in show]
        fold = [f[0:1] for f in fold]
        low_row = low[0:1]
        show_mix = jnp.where(low_row, show[1], show[2])
        fold_mix = jnp.where(low_row, fold[1], fold[2])

        def block(i, carry):
            rows = pl.ds(pl.multiple_of(i * MB, MB), MB)
            for j in range(KP // 128):
                js = pl.ds(128 * j, 128)
                shared = lax.dot_general(
                    inc[rows], inc[js], (((1,), (1,)), ((), ())), preferred_element_type=F32
                )
                apart = jnp.maximum(1.0 - shared, 0.0)
                dis[:, js] = apart.astype(BF16)
                for c in range(2):
                    gap = col[c, rows] - rank_rows[c : c + 1, 128 * j : 128 * j + 128]
                    sign = jnp.minimum(jnp.maximum(gap, -1.0), 1.0)
                    mat[c, :, js] = (sign * apart).astype(BF16)
            acts, shows, folds = [], [], []
            for c in range(2):
                xc = x[:, pl.ds(256 * c, 256)]
                s = jnp.dot(mat[c], xc, preferred_element_type=F32)
                d = jnp.dot(dis[...], xc, preferred_element_type=F32)
                v = col[2 + c, rows]
                s0, s1 = s[:, :128] * v, s[:, 128:] * v
                d0, d1 = d[:, :128] * v, d[:, 128:] * v
                mixed = s1 * show_mix + d1 * fold_mix
                act = s0 * show[0] + d0 * fold[0] + mixed + roll_half(mixed)
                acts.append(jnp.where(low_row, s0, act))
                folds.append(d0)
            tiles = (acts[0], acts[1], jnp.where(low_row, folds[0], roll_half(folds[1])))
            for k in range(3):
                out[pl.ds(i * (MB // HP), MB // HP), k] = tiles[k].reshape(MB // HP, HP, 128)
            return carry

        lax.fori_loop(0, KP // MB, block, 0)


def update_kernel(rz, ro, back, pots, kinds, new_rz, new_ro, lines):
    hands = rz.shape[0]
    lane = lanes(hands)
    low = lane < 64
    show, fold = leaf_scales(pots, kinds, hands)

    def step(w, carry):
        sum_zero, sum_one = carry
        r, zs = zero_shares(rz, w, lane)
        regrets, os = one_shares(ro, w, lane)
        t0, t1, dz = back[w, 0, 0:hands], back[w, 1, 0:hands], back[w, 2, 0:hands]
        act = jnp.where(low, roll_half(t0), t1)
        sz = jnp.where(low, t0, roll_half(t1))
        node = action_sum(zs * act, lane)
        new_rz[:, pl.ds(128 * w, 128)] = jnp.maximum(r + act - node, 0.0)
        leaf_one = [show[b] * sz - fold[b] * dz for b in range(MOVES_ONE)]
        node_one = os[0] * leaf_one[0] + os[1] * leaf_one[1] + os[2] * leaf_one[2]
        new = [jnp.maximum(regrets[b] + leaf_one[b] - node_one, 0.0) for b in range(MOVES_ONE)]
        native = join_moves(new, lane)
        for v in range(3):
            new_ro[:, pl.ds(384 * w + 128 * v, 128)] = native[v]
        return (sum_zero + node, sum_one + node_one)

    zero = jnp.zeros((hands, 128), F32)
    sum_zero, sum_one = lax.fori_loop(0, WORKERS, step, (zero, zero))
    sum_zero = jnp.where(lane % 64 < SUBGAMES, sum_zero, 0.0)
    for k, total in enumerate((sum_zero, sum_one)):
        lines[k] = CHANCE * lax.dot_general(
            tile_selector(),
            total,
            (((1,), (1,)), ((), ())),
            precision=lax.Precision.HIGHEST,
            preferred_element_type=F32,
        )


VM = pl.BlockSpec(memory_space=pltpu.VMEM)
SM = pl.BlockSpec(memory_space=pltpu.SMEM)
LIMIT = 48 << 20


def exchange(kernel, identity, operand, shape, dtype, sends, recvs):
    return pl.pallas_call(
        kernel,
        out_shape=jax.ShapeDtypeStruct(shape, dtype),
        in_specs=[VM],
        out_specs=VM,
        scratch_shapes=[
            pltpu.SemaphoreType.DMA((sends,)),
            pltpu.SemaphoreType.DMA((recvs,)),
            pltpu.SemaphoreType.DMA,
        ],
        compiler_params=pltpu.CompilerParams(
            collective_id=identity, has_side_effects=True, vmem_limit_bytes=LIMIT
        ),
    )(operand)


def local(
    range_zero,
    range_one,
    turn_regret,
    river_regret_zero,
    river_regret_one,
    hand_cards,
    dealt_cards,
    hand_ranks,
    leaf_pots,
    leaf_kinds,
):
    hands = range_zero.shape[1]
    rz = river_regret_zero[0]
    ro = river_regret_one[0]
    tr = turn_regret[0]
    params = pltpu.CompilerParams(vmem_limit_bytes=LIMIT)
    turn_total = lax.psum(tr, "river")
    y = pl.pallas_call(
        prep_kernel,
        out_shape=jax.ShapeDtypeStruct((WORKERS, 4, HP, 128), BF16),
        in_specs=[VM] * 6,
        out_specs=VM,
        compiler_params=params,
    )(rz, ro, range_zero, range_one, tr, turn_total)
    recv = exchange(
        forward_kernel, 1, y, (PEERS, 4, HP, 128), BF16, WORKERS, PEERS
    )
    cards = jnp.pad(
        hand_cards.T.reshape(2, PEERS, hands), ((0, 0), (0, 0), (0, HP - hands)), constant_values=52
    ).reshape(2, KP)
    cards = jnp.pad(cards.astype(F32), ((0, 6), (0, 0)))
    _, w_self = leaf_worker(lax.axis_index("leaf"))
    w_self = jnp.minimum(w_self, WORKERS - 1)
    ranks = lax.dynamic_slice_in_dim(hand_ranks, 2 * w_self, 2, 0)
    ranks = jnp.pad(ranks.reshape(2, PEERS, hands), ((0, 0), (0, 0), (0, HP - hands))).reshape(2, KP)
    ranks = jnp.pad(ranks.astype(F32), ((0, 6), (0, 0)))
    out = pl.pallas_call(
        blocks_kernel,
        out_shape=jax.ShapeDtypeStruct((PEERS, 3, HP, 128), F32),
        in_specs=[VM, VM, VM, SM, SM, SM],
        out_specs=VM,
        scratch_shapes=[
            pltpu.VMEM((KP, 512), BF16),
            pltpu.VMEM((2, MB, KP), BF16),
            pltpu.VMEM((MB, KP), BF16),
            pltpu.VMEM((4, KP, 128), F32),
            pltpu.VMEM((KP, 128), BF16),
        ],
        compiler_params=params,
    )(recv, cards, ranks, dealt_cards, leaf_pots, leaf_kinds)
    back = exchange(
        backward_kernel, 2, out, (WORKERS, 3, HP, 128), F32, PEERS, WORKERS
    )
    new_rz, new_ro, lines = pl.pallas_call(
        update_kernel,
        out_shape=(
            jax.ShapeDtypeStruct(rz.shape, F32),
            jax.ShapeDtypeStruct(ro.shape, F32),
            jax.ShapeDtypeStruct((2, SUBGAMES, hands), F32),
        ),
        in_specs=[VM, VM, VM, SM, SM],
        out_specs=(VM, VM, VM),
        compiler_params=params,
    )(rz, ro, back, leaf_pots, leaf_kinds)
    line_zero = lines[0]
    share = tr / turn_total
    roots = lax.psum(jnp.stack([share * line_zero, lines[1]]), "river")
    new_turn = jnp.maximum(tr + line_zero - roots[0], 0.0)
    return (new_turn[None], new_rz[None], new_ro[None], roots)


def solution(mesh):
    placed = (
        P(None, "leaf"),
        P(None, "leaf"),
        P("river", None, "leaf"),
        P("river", "leaf", None),
        P("river", "leaf", None),
        P(),
        P(),
        P(),
        P("river", None),
        P("river", None),
    )
    return jax.shard_map(
        local,
        mesh=mesh,
        in_specs=placed,
        out_specs=(
            P("river", None, "leaf"),
            P("river", "leaf", None),
            P("river", "leaf", None),
            P(None, None, "leaf"),
        ),
        check_vma=False,
    )
```

```python
import jax
import jax.numpy as jnp
from jax import lax
from jax.experimental import pallas as pl
from jax.experimental.pallas import tpu as pltpu
from jax.sharding import PartitionSpec as P

MESH = pl.DeviceIdType.MESH
F32 = jnp.float32
BF16 = jnp.bfloat16
RIVERS = 48
MOVES_ZERO = 4
MOVES_ONE = 3
SUBGAMES = 16
WORKERS = 24
PEERS = 32
HP = 48
KP = PEERS * HP
MB = 384
CHANCE = 1.0 / 44.0


def worker_leaf(w):
    z = w // 3
    x = lax.rem(w - 3 * z + 1 + z, 4)
    return 4 * z + x


def leaf_worker(leaf):
    z = leaf // 4
    x = leaf - 4 * z
    k = lax.rem(x - 1 - z + 12, 4)
    return k, 3 * z + k


def lanes(rows):
    return lax.broadcasted_iota(jnp.int32, (rows, 128), 1)


def gather_lanes(x, index):
    return jnp.take_along_axis(x, index, axis=1, mode="promise_in_bounds")


def roll_half(x):
    return pltpu.roll(x, 64, 1)


def action_sum(x, lane):
    x = x + gather_lanes(x, (lane & 64) | ((lane + 16) & 63))
    return x + gather_lanes(x, (lane & 64) | ((lane + 32) & 63))


def split_moves(tiles, lane):
    slot, sub = lane // 16, lane % 16
    out = []
    for b in range(MOVES_ONE):
        group = (3 * (slot - b + 8)) % 8
        tile = (3 * group + b) // 8
        picked = jnp.where(tile == 0, tiles[0], jnp.where(tile == 1, tiles[1], tiles[2]))
        out.append(gather_lanes(picked, ((3 * slot + b) % 8) * 16 + sub))
    return out


def join_moves(parts, lane):
    slot, sub = lane // 16, lane % 16
    moved = []
    for b in range(MOVES_ONE):
        group = (3 * (slot - b + 8)) % 8
        moved.append(gather_lanes(parts[b], group * 16 + sub))
    out = []
    for v in range(3):
        b = (8 * v + slot) % 3
        out.append(jnp.where(b == 0, moved[0], jnp.where(b == 1, moved[1], moved[2])))
    return out


def tile_selector():
    sub = lax.broadcasted_iota(jnp.int32, (SUBGAMES, 128), 0)
    lane = lanes(SUBGAMES)
    return (lane % SUBGAMES == sub).astype(F32)


def to_lanes(x):
    return lax.dot_general(
        x,
        tile_selector(),
        (((0,), (0,)), ((), ())),
        precision=lax.Precision.HIGHEST,
        preferred_element_type=F32,
    )


def zero_shares(rz, w, lane):
    x = rz[:, pl.ds(128 * w, 128)]
    return x, x / action_sum(x, lane)


def one_shares(ro, w, lane):
    tiles = [ro[:, pl.ds(384 * w + 128 * v, 128)] for v in range(3)]
    regrets = split_moves(tiles, lane)
    scale = 1.0 / (regrets[0] + regrets[1] + regrets[2])
    return regrets, [r * scale for r in regrets]


def leaf_scales(pots, kinds, rows):
    action = (lanes(rows) // SUBGAMES) % MOVES_ZERO
    show, fold = [], []
    for b in range(MOVES_ONE):
        s = jnp.zeros((rows, 128), F32)
        f = jnp.zeros((rows, 128), F32)
        for a in range(MOVES_ZERO):
            pot = pots[0, a * MOVES_ONE + b].astype(F32)
            kind = kinds[0, a * MOVES_ONE + b]
            here = action == a
            s = jnp.where(here, jnp.where(kind == 0, pot, 0.0), s)
            f = jnp.where(here, jnp.where(kind == 0, 0.0, jnp.where(kind == 1, pot, -pot)), f)
        show.append(s)
        fold.append(f)
    return show, fold


ONE_TOP = 64.0 * 0.001 * 1.005
CODE = 32760.0


def column(rows, select):
    return lax.dot_general(
        rows, select, (((0,), (0,)), ((), ())), preferred_element_type=F32
    )


def code(x):
    return x.astype(jnp.int32).astype(jnp.int16)


def nearest(x):
    return jnp.floor(x + 0.5)


def lead_kernel(
    rz_hbm,
    ro_hbm,
    range_zero,
    range_one,
    turn_regret,
    cards,
    ranks,
    dealt,
    pots,
    kinds,
    back,
    turn_total,
    rz,
    ro,
    turns,
    yz,
    yw,
    recv_z,
    recv_w,
    x,
    mat,
    col,
    inc,
    out,
    load_sem,
    turn_send,
    turn_recv,
    z_send,
    z_recv,
    w_send,
    w_recv,
    out_send,
    out_recv,
):
    line, leaf = lax.axis_index("river"), lax.axis_index("leaf")
    lines = turns.shape[0]
    k_self, w_self = leaf_worker(leaf)
    is_worker = k_self < 3
    hands = rz.shape[0]
    first_worker = 3 * (leaf // 4)

    loads = [
        pltpu.make_async_copy(rz_hbm, rz, load_sem.at[0]),
        pltpu.make_async_copy(ro_hbm, ro, load_sem.at[1]),
    ]
    for load in loads:
        load.start()

    barrier = pltpu.get_barrier_semaphore()

    def greet_leaf(k, carry):
        peer = lax.rem(leaf + k, PEERS)
        pl.semaphore_signal(barrier, inc=1, device_id=(line, peer), device_id_type=MESH)
        return carry

    def greet_line(k, carry):
        peer = lax.rem(line + k, lines)
        pl.semaphore_signal(barrier, inc=1, device_id=(peer, leaf), device_id_type=MESH)
        return carry

    lax.fori_loop(1, lines, greet_line, 0)
    lax.fori_loop(1, PEERS, greet_leaf, 0)
    pl.semaphore_wait(barrier, PEERS - 1 + lines - 1)

    def turn_copy(peer, slot):
        return pltpu.make_async_remote_copy(
            src_ref=turn_regret,
            dst_ref=turns.at[slot],
            send_sem=turn_send.at[peer],
            recv_sem=turn_recv.at[slot],
            device_id=(peer, leaf),
            device_id_type=MESH,
        )

    def turn_start(k, carry):
        turn_copy(lax.rem(line + k, lines), line).start()
        return carry

    lax.fori_loop(1, lines, turn_start, 0)
    turns[line] = turn_regret[...]

    def turn_wait(k, carry):
        peer = lax.rem(line + k, lines)
        turn_copy(peer, peer).wait_recv()
        return carry

    lax.fori_loop(1, lines, turn_wait, 0)
    total = turns[0]
    for t in range(1, lines):
        total = total + turns[t]
    turn_total[...] = total

    lane = lanes(hands)
    weight_zero = to_lanes(range_zero[...] * (turn_regret[...] / total))
    weight_one = to_lanes(range_one[...])
    show, fold = leaf_scales(pots, kinds, 8)
    show = [s[0:1] * (CODE / ONE_TOP) for s in show]
    fold = [f[0:1] * (CODE / ONE_TOP) for f in fold]
    for load in loads:
        load.wait()

    def z_copy(w, peer):
        return pltpu.make_async_remote_copy(
            src_ref=yz.at[w],
            dst_ref=recv_z.at[leaf],
            send_sem=z_send.at[w],
            recv_sem=z_recv.at[leaf],
            device_id=(line, peer),
            device_id_type=MESH,
        )

    def w_copy(w, peer):
        return pltpu.make_async_remote_copy(
            src_ref=yw.at[w],
            dst_ref=recv_w.at[leaf],
            send_sem=w_send.at[w],
            recv_sem=w_recv.at[leaf],
            device_id=(line, peer),
            device_id_type=MESH,
        )

    def prepare(k, carry):
        w = lax.rem(first_worker + k, WORKERS)
        _, zs = zero_shares(rz, w, lane)
        _, os = one_shares(ro, w, lane)
        yz[w, 32:48] = jnp.zeros((16, 128), BF16)
        yz[w, 0:hands] = (weight_zero * zs).astype(BF16)
        o = [(weight_one * s).astype(BF16).astype(F32) for s in os]
        for j, scale in enumerate((show, fold)):
            mixed = o[0] * scale[0] + o[1] * scale[1] + o[2] * scale[2]
            yw[w, j, 32:48] = jnp.zeros((16, 128), jnp.int16)
            yw[w, j, 0:hands] = code(nearest(mixed))
        peer = worker_leaf(w)

        @pl.when(peer != leaf)
        def _():
            z_copy(w, peer).start()
            w_copy(w, peer).start()

        @pl.when(peer == leaf)
        def _():
            recv_z[leaf] = yz[w]
            recv_w[leaf] = yw[w]

        return carry

    lax.fori_loop(0, WORKERS, prepare, 0)

    def out_copy(peer):
        return pltpu.make_async_remote_copy(
            src_ref=out.at[peer],
            dst_ref=back.at[w_self],
            send_sem=out_send.at[peer],
            recv_sem=out_recv.at[w_self],
            device_id=(line, peer),
            device_id_type=MESH,
        )

    @pl.when(is_worker)
    def _():
        low = lanes(8)[0:1] < 64
        one_row = lax.broadcasted_iota(jnp.int32, (8, 128), 0)
        pick = lambda r, scale: jnp.where(one_row == r, scale, 0.0).astype(BF16)
        card_rows = cards[...].astype(BF16)
        first = column(card_rows, pick(0, 1.0))
        second = column(card_rows, pick(1, 1.0))
        usable = (first < 52.0) & (second < 52.0)
        for k in range(4):
            board = dealt[k].astype(F32)
            usable = usable & (first != board) & (second != board)
        rivers = [dealt[4 + 2 * w_self + c].astype(F32) for c in range(2)]
        river = jnp.where(low, rivers[0], rivers[1])
        col[2] = (usable & (first != river) & (second != river)).astype(F32)
        inc[...] = ((first == lanes(KP).astype(F32)) | (second == lanes(KP).astype(F32))).astype(BF16)
        rank_rows = ranks[...]
        high_rows = jnp.floor(rank_rows * (1.0 / 64.0))
        low_rows = rank_rows - 64.0 * high_rows
        for c in range(2):
            col[c] = column(high_rows.astype(BF16), pick(c, 64.0)) + column(
                low_rows.astype(BF16), pick(c, 1.0)
            )

        def build(i, carry):
            rows = pl.ds(pl.multiple_of(i * MB, MB), MB)
            for j in range(KP // 128):
                js = pl.ds(128 * j, 128)
                shared = lax.dot_general(
                    inc[rows], inc[js], (((1,), (1,)), ((), ())), preferred_element_type=F32
                )
                apart = jnp.maximum(1.0 - shared, 0.0)
                mat[2, rows, js] = apart.astype(BF16)
                for c in range(2):
                    gap = col[c, rows] - ranks[c : c + 1, js]
                    sign = jnp.minimum(jnp.maximum(gap, -1.0), 1.0)
                    mat[c, rows, js] = (sign * apart).astype(BF16)
            return carry

        lax.fori_loop(0, KP // MB, build, 0)

        def arrive(k, carry):
            source = lax.rem(leaf + k, PEERS)
            pltpu.make_async_remote_copy(
                src_ref=yz.at[0],
                dst_ref=recv_z.at[source],
                send_sem=z_send.at[0],
                recv_sem=z_recv.at[source],
                device_id=(line, source),
                device_id_type=MESH,
            ).wait_recv()
            pltpu.make_async_remote_copy(
                src_ref=yw.at[0],
                dst_ref=recv_w.at[source],
                send_sem=w_send.at[0],
                recv_sem=w_recv.at[source],
                device_id=(line, source),
                device_id_type=MESH,
            ).wait_recv()
            return carry

        lax.fori_loop(1, PEERS, arrive, 0)

        def unpack(i, carry):
            z_sum, w_sum = carry
            rows = pl.ds(pl.multiple_of(i * MB, MB), MB)
            chunk = pl.ds(i * (MB // HP), MB // HP)
            v = col[2, rows]
            z = recv_z[chunk].reshape(MB, 128).astype(F32) * v
            ws = recv_w[chunk, 0].reshape(MB, 128).astype(jnp.int32).astype(F32) * v
            wf = recv_w[chunk, 1].reshape(MB, 128).astype(jnp.int32).astype(F32) * v
            s_high = jnp.floor(ws * (1.0 / 256.0))
            s_low = ws - 256.0 * s_high
            f_high = jnp.floor(wf * (1.0 / 256.0))
            f_low = wf - 256.0 * f_high
            x[rows, 0:128] = z.astype(BF16)
            x[rows, 128:256] = f_high.astype(BF16)
            x[rows, 256:384] = f_low.astype(BF16)
            x[rows, 384:512] = jnp.where(low, s_high, roll_half(s_low)).astype(BF16)
            x[rows, 512:640] = jnp.where(low, roll_half(s_high), s_low).astype(BF16)
            return (
                z_sum + jnp.sum(z, axis=0, keepdims=True),
                w_sum + jnp.sum(ws + jnp.abs(wf), axis=0, keepdims=True),
            )

        empty = jnp.zeros((1, 128), F32)
        z_sum, w_sum = lax.fori_loop(0, KP // MB, unpack, (empty, empty))
        unit = ONE_TOP / CODE
        z_power = jnp.floor(jnp.log2(jnp.maximum(z_sum, 1e-30))) + 1.0
        w_power = jnp.floor(jnp.log2(jnp.maximum(w_sum * unit, 1e-30))) + 1.0
        z_scale = CODE * jnp.exp2(-z_power)
        w_scale = (CODE * unit) * jnp.exp2(-w_power)
        pad = lax.rem(lax.broadcasted_iota(jnp.int32, (MB, 128), 0), HP) >= hands
        low_part = jnp.where(low, 256.0, 1.0)

        def block(k, carry):
            i = lax.rem(leaf // 8 + k, KP // MB)
            rows = pl.ds(pl.multiple_of(i * MB, MB), MB)
            d = jnp.dot(mat[2, rows], x[:, 0:384], preferred_element_type=F32)
            s0z = jnp.dot(mat[0, rows], x[:, 0:128], preferred_element_type=F32)
            s0w = jnp.dot(mat[0, rows], x[:, 384:512], preferred_element_type=F32)
            s1z = jnp.dot(mat[1, rows], x[:, 0:128], preferred_element_type=F32)
            s1w = jnp.dot(mat[1, rows], x[:, 512:640], preferred_element_type=F32)
            v = col[2, rows]
            s0w = s0w * low_part
            s1w = s1w * low_part
            s0w = s0w + roll_half(s0w)
            s1w = s1w + roll_half(s1w)
            act = jnp.where(low, s0w, s1w) + 256.0 * d[:, 128:256] + d[:, 256:384]
            tiles = (
                (act * (v * w_scale), w_power),
                (jnp.where(low, s0z, s1z) * (v * z_scale), z_power),
                (d[:, 0:128] * (v * z_scale), z_power),
            )
            for j, (value, power) in enumerate(tiles):
                value = jnp.minimum(jnp.maximum(nearest(value), -32767.0), 32767.0)
                coded = code(jnp.where(pad, power, value))
                out[pl.ds(i * (MB // HP), MB // HP), j] = coded.reshape(MB // HP, HP, 128)

            def send(m, carry):
                peer = i * (MB // HP) + m

                @pl.when(peer != leaf)
                def _():
                    out_copy(peer).start()

                @pl.when(peer == leaf)
                def _():
                    back[w_self] = out[peer]

                return carry

            lax.fori_loop(0, MB // HP, send, 0)
            return carry

        lax.fori_loop(0, KP // MB, block, 0)

    def collect(k, carry):
        w = lax.rem(first_worker + k, WORKERS)
        peer = worker_leaf(w)

        @pl.when(peer != leaf)
        def _():
            pltpu.make_async_remote_copy(
                src_ref=out.at[0],
                dst_ref=back.at[w],
                send_sem=out_send.at[0],
                recv_sem=out_recv.at[w],
                device_id=(line, peer),
                device_id_type=MESH,
            ).wait_recv()
            z_copy(w, peer).wait_send()
            w_copy(w, peer).wait_send()

        return carry

    lax.fori_loop(0, WORKERS, collect, 0)

    @pl.when(is_worker)
    def _():
        def sent(k, carry):
            out_copy(lax.rem(leaf + k, PEERS)).wait_send()
            return carry

        lax.fori_loop(1, PEERS, sent, 0)

    def turn_sent(k, carry):
        turn_copy(lax.rem(line + k, lines), line).wait_send()
        return carry

    lax.fori_loop(1, lines, turn_sent, 0)


PER_STEP = 4


def update_kernel(rz, ro, back, pots, kinds, new_rz, new_ro, lines, sums):
    hands = rz.shape[0]
    lane = lanes(hands)
    show, fold = leaf_scales(pots, kinds, hands)
    i = pl.program_id(0)

    @pl.when(i == 0)
    def _():
        sums[...] = jnp.zeros_like(sums)

    sum_zero, sum_one = sums[0], sums[1]
    for w in range(PER_STEP):
        r, zs = zero_shares(rz, w, lane)
        regrets, os = one_shares(ro, w, lane)
        values = []
        for j in range(3):
            coded = back[w, j].astype(jnp.int32).astype(F32)
            scale = jnp.exp2(coded[hands : hands + 1]) * (1.0 / CODE)
            values.append(coded[0:hands] * scale)
        act, sz, dz = values
        node = action_sum(zs * act, lane)
        new_rz[:, pl.ds(128 * w, 128)] = jnp.maximum(r + act - node, 0.0)
        leaf_one = [show[b] * sz - fold[b] * dz for b in range(MOVES_ONE)]
        node_one = os[0] * leaf_one[0] + os[1] * leaf_one[1] + os[2] * leaf_one[2]
        new = [jnp.maximum(regrets[b] + leaf_one[b] - node_one, 0.0) for b in range(MOVES_ONE)]
        native = join_moves(new, lane)
        for v in range(3):
            new_ro[:, pl.ds(384 * w + 128 * v, 128)] = native[v]
        sum_zero = sum_zero + node
        sum_one = sum_one + node_one
    sums[0] = sum_zero
    sums[1] = sum_one

    @pl.when(i == pl.num_programs(0) - 1)
    def _():
        node_once = jnp.where(lane % 64 < SUBGAMES, sum_zero, 0.0)
        for k, total in enumerate((node_once, sum_one)):
            lines[k] = CHANCE * lax.dot_general(
                tile_selector(),
                total,
                (((1,), (1,)), ((), ())),
                precision=lax.Precision.HIGHEST,
                preferred_element_type=F32,
            )


def root_kernel(values, turn_regret, turn_total, new_turn, roots, own, parts, send_sem, recv_sem):
    line, leaf = lax.axis_index("river"), lax.axis_index("leaf")
    lines = parts.shape[0]
    barrier = pltpu.get_barrier_semaphore()

    def greet(k, carry):
        peer = lax.rem(line + k, lines)
        pl.semaphore_signal(barrier, inc=1, device_id=(peer, leaf), device_id_type=MESH)
        return carry

    lax.fori_loop(1, lines, greet, 0)
    own[0] = (turn_regret[...] / turn_total[...]) * values[0]
    own[1] = values[1]
    pl.semaphore_wait(barrier, lines - 1)

    def copy(peer, slot):
        return pltpu.make_async_remote_copy(
            src_ref=own,
            dst_ref=parts.at[slot],
            send_sem=send_sem.at[peer],
            recv_sem=recv_sem.at[slot],
            device_id=(peer, leaf),
            device_id_type=MESH,
        )

    def start(k, carry):
        copy(lax.rem(line + k, lines), line).start()
        return carry

    lax.fori_loop(1, lines, start, 0)
    parts[line] = own[...]

    def wait(k, carry):
        peer = lax.rem(line + k, lines)
        copy(peer, peer).wait_recv()
        copy(peer, line).wait_send()
        return carry

    lax.fori_loop(1, lines, wait, 0)
    total = parts[0]
    for t in range(1, lines):
        total = total + parts[t]
    roots[...] = total
    new_turn[...] = jnp.maximum(turn_regret[...] + values[0] - total[0], 0.0)


VM = pl.BlockSpec(memory_space=pltpu.VMEM)
SM = pl.BlockSpec(memory_space=pltpu.SMEM)
HB = pl.BlockSpec(memory_space=pl.ANY)
LIMIT = 56 << 20


def local(
    range_zero,
    range_one,
    turn_regret,
    river_regret_zero,
    river_regret_one,
    hand_cards,
    dealt_cards,
    hand_ranks,
    leaf_pots,
    leaf_kinds,
):
    hands = range_zero.shape[1]
    lines = lax.axis_size("river")
    rz = river_regret_zero[0]
    ro = river_regret_one[0]
    tr = turn_regret[0]
    cards = jnp.pad(
        hand_cards.T.reshape(2, PEERS, hands), ((0, 0), (0, 0), (0, HP - hands)), constant_values=52
    ).reshape(2, KP)
    cards = jnp.pad(cards.astype(F32), ((0, 6), (0, 0)))
    _, w_self = leaf_worker(lax.axis_index("leaf"))
    w_self = jnp.minimum(w_self, WORKERS - 1)
    ranks = lax.dynamic_slice_in_dim(hand_ranks, 2 * w_self, 2, 0)
    ranks = jnp.pad(ranks.reshape(2, PEERS, hands), ((0, 0), (0, 0), (0, HP - hands))).reshape(2, KP)
    ranks = jnp.pad(ranks.astype(F32), ((0, 6), (0, 0)))
    dma = pltpu.SemaphoreType.DMA
    back, turn_total = pl.pallas_call(
        lead_kernel,
        out_shape=(
            jax.ShapeDtypeStruct((WORKERS, 3, HP, 128), jnp.int16),
            jax.ShapeDtypeStruct(tr.shape, F32),
        ),
        in_specs=[HB, HB, VM, VM, VM, VM, VM, SM, SM, SM],
        out_specs=(VM, VM),
        scratch_shapes=[
            pltpu.VMEM(rz.shape, F32),
            pltpu.VMEM(ro.shape, F32),
            pltpu.VMEM((lines,) + tr.shape, F32),
            pltpu.VMEM((WORKERS, HP, 128), BF16),
            pltpu.VMEM((WORKERS, 2, HP, 128), jnp.int16),
            pltpu.VMEM((PEERS, HP, 128), BF16),
            pltpu.VMEM((PEERS, 2, HP, 128), jnp.int16),
            pltpu.VMEM((KP, 640), BF16),
            pltpu.VMEM((3, KP, KP), BF16),
            pltpu.VMEM((3, KP, 128), F32),
            pltpu.VMEM((KP, 128), BF16),
            pltpu.VMEM((PEERS, 3, HP, 128), jnp.int16),
            dma((2,)),
            dma((lines,)),
            dma((lines,)),
            dma((WORKERS,)),
            dma((PEERS,)),
            dma((WORKERS,)),
            dma((PEERS,)),
            dma((PEERS,)),
            dma((WORKERS,)),
        ],
        compiler_params=pltpu.CompilerParams(
            collective_id=1, has_side_effects=True, vmem_limit_bytes=LIMIT
        ),
    )(rz, ro, range_zero, range_one, tr, cards, ranks, dealt_cards, leaf_pots, leaf_kinds)
    steps = WORKERS // PER_STEP
    new_rz, new_ro, values = pl.pallas_call(
        update_kernel,
        grid=(steps,),
        out_shape=(
            jax.ShapeDtypeStruct(rz.shape, F32),
            jax.ShapeDtypeStruct(ro.shape, F32),
            jax.ShapeDtypeStruct((2,) + tr.shape, F32),
        ),
        in_specs=[
            pl.BlockSpec((hands, 128 * PER_STEP), lambda i: (0, i)),
            pl.BlockSpec((hands, 384 * PER_STEP), lambda i: (0, i)),
            pl.BlockSpec((PER_STEP, 3, HP, 128), lambda i: (i, 0, 0, 0)),
            SM,
            SM,
        ],
        out_specs=(
            pl.BlockSpec((hands, 128 * PER_STEP), lambda i: (0, i)),
            pl.BlockSpec((hands, 384 * PER_STEP), lambda i: (0, i)),
            pl.BlockSpec((2,) + tr.shape, lambda i: (0, 0, 0)),
        ),
        scratch_shapes=[pltpu.VMEM((2, hands, 128), F32)],
        compiler_params=pltpu.CompilerParams(vmem_limit_bytes=16 << 20),
    )(rz, ro, back, leaf_pots, leaf_kinds)
    new_turn, roots = pl.pallas_call(
        root_kernel,
        out_shape=(
            jax.ShapeDtypeStruct(tr.shape, F32),
            jax.ShapeDtypeStruct((2,) + tr.shape, F32),
        ),
        in_specs=[VM, VM, VM],
        out_specs=(VM, VM),
        scratch_shapes=[
            pltpu.VMEM((2,) + tr.shape, F32),
            pltpu.VMEM((lines, 2) + tr.shape, F32),
            dma((lines,)),
            dma((lines,)),
        ],
        compiler_params=pltpu.CompilerParams(collective_id=2, has_side_effects=True),
    )(values, tr, turn_total)
    return (new_turn[None], new_rz[None], new_ro[None], roots)


def solution(mesh):
    placed = (
        P(None, "leaf"),
        P(None, "leaf"),
        P("river", None, "leaf"),
        P("river", "leaf", None),
        P("river", "leaf", None),
        P(),
        P(),
        P(),
        P("river", None),
        P("river", None),
    )
    return jax.shard_map(
        local,
        mesh=mesh,
        in_specs=placed,
        out_specs=(
            P("river", None, "leaf"),
            P("river", "leaf", None),
            P("river", "leaf", None),
            P(None, None, "leaf"),
        ),
        check_vma=False,
    )
```

```python
import jax
import jax.numpy as jnp
from jax import lax
from jax.experimental import pallas as pl
from jax.experimental.pallas import tpu as pltpu
from jax.sharding import PartitionSpec as P

MESH = pl.DeviceIdType.MESH
F32 = jnp.float32
BF16 = jnp.bfloat16
RIVERS = 48
MOVES_ZERO = 4
MOVES_ONE = 3
SUBGAMES = 16
WORKERS = 24
PEERS = 32
HP = 48
KP = PEERS * HP
MB = 384
BLOCK = 384
CHANCE = 1.0 / 44.0


def worker_leaf(w):
    z = w // 3
    x = lax.rem(w - 3 * z + 1 + z, 4)
    return 4 * z + x


def leaf_worker(leaf):
    z = leaf // 4
    x = leaf - 4 * z
    k = lax.rem(x - 1 - z + 12, 4)
    return k, 3 * z + k


def lanes(rows):
    return lax.broadcasted_iota(jnp.int32, (rows, 128), 1)


def gather_lanes(x, index):
    return jnp.take_along_axis(x, index, axis=1, mode="promise_in_bounds")


def roll_half(x):
    return pltpu.roll(x, 64, 1)


def action_sum(x, lane):
    x = x + gather_lanes(x, (lane & 64) | ((lane + 16) & 63))
    return x + gather_lanes(x, (lane & 64) | ((lane + 32) & 63))


def split_moves(tiles, lane):
    slot, sub = lane // 16, lane % 16
    out = []
    for b in range(MOVES_ONE):
        group = (3 * (slot - b + 8)) % 8
        tile = (3 * group + b) // 8
        picked = jnp.where(tile == 0, tiles[0], jnp.where(tile == 1, tiles[1], tiles[2]))
        out.append(gather_lanes(picked, ((3 * slot + b) % 8) * 16 + sub))
    return out


def join_moves(parts, lane):
    slot, sub = lane // 16, lane % 16
    moved = []
    for b in range(MOVES_ONE):
        group = (3 * (slot - b + 8)) % 8
        moved.append(gather_lanes(parts[b], group * 16 + sub))
    out = []
    for v in range(3):
        b = (8 * v + slot) % 3
        out.append(jnp.where(b == 0, moved[0], jnp.where(b == 1, moved[1], moved[2])))
    return out


def tile_selector():
    sub = lax.broadcasted_iota(jnp.int32, (SUBGAMES, 128), 0)
    lane = lanes(SUBGAMES)
    return (lane % SUBGAMES == sub).astype(F32)


def to_lanes(x):
    return lax.dot_general(
        x,
        tile_selector(),
        (((0,), (0,)), ((), ())),
        precision=lax.Precision.HIGHEST,
        preferred_element_type=F32,
    )


def leaf_scales(pots, kinds, rows):
    action = (lanes(rows) // SUBGAMES) % MOVES_ZERO
    show, fold = [], []
    for b in range(MOVES_ONE):
        s = jnp.zeros((rows, 128), F32)
        f = jnp.zeros((rows, 128), F32)
        for a in range(MOVES_ZERO):
            pot = pots[0, a * MOVES_ONE + b].astype(F32)
            kind = kinds[0, a * MOVES_ONE + b]
            here = action == a
            s = jnp.where(here, jnp.where(kind == 0, pot, 0.0), s)
            f = jnp.where(here, jnp.where(kind == 0, 0.0, jnp.where(kind == 1, pot, -pot)), f)
        show.append(s)
        fold.append(f)
    return show, fold


ONE_TOP = 64.0 * 0.001 * 1.005
CODE = 32760.0
ROWS = 128
STAGE = 136


def column(rows, select):
    return lax.dot_general(
        rows, select, (((0,), (0,)), ((), ())), preferred_element_type=F32
    )


def code(x):
    return x.astype(jnp.int32).astype(jnp.int16)


def decode(x):
    return x.astype(jnp.int32).astype(F32)


def nearest(x):
    return jnp.floor(x + 0.5)


def power_above(x):
    return jnp.floor(jnp.log2(jnp.maximum(x, 1e-30))) + 1.0


def zero_shares(rz, w, lane, hands):
    x = rz[pl.ds(w, hands, stride=WORKERS)]
    return x, x / action_sum(x, lane)


def one_shares(ro, w, lane, hands):
    tiles = [ro[pl.ds(3 * w + v, hands, stride=3 * WORKERS)] for v in range(3)]
    regrets = split_moves(tiles, lane)
    scale = 1.0 / (regrets[0] + regrets[1] + regrets[2])
    return regrets, [r * scale for r in regrets]


def kernel(
    rz_hbm,
    ro_hbm,
    range_zero,
    range_one,
    turn_regret,
    cards,
    all_ranks,
    dealt,
    pots,
    kinds,
    new_turn,
    new_rz,
    new_ro,
    roots,
    rz,
    ro,
    turns,
    yq,
    recv,
    stage,
    spread,
    card_pad,
    rank_row,
    x,
    mat,
    col,
    inc,
    out,
    back,
    own,
    parts,
    load_sem,
    turn_send,
    turn_recv,
    y_send,
    y_recv,
    out_send,
    out_recv,
    root_send,
    root_recv,
):
    line, leaf = lax.axis_index("river"), lax.axis_index("leaf")
    lines = turns.shape[0]
    k_self, w_self = leaf_worker(leaf)
    is_worker = k_self < 3
    hands = turn_regret.shape[1]
    first_worker = 3 * (leaf // 4)

    loads = [
        pltpu.make_async_copy(rz_hbm, rz, load_sem.at[0]),
        pltpu.make_async_copy(ro_hbm, ro, load_sem.at[1]),
    ]
    for load in loads:
        load.start()

    barrier = pltpu.get_barrier_semaphore()

    def greet_leaf(k, carry):
        peer = lax.rem(leaf + k, PEERS)
        pl.semaphore_signal(barrier, inc=1, device_id=(line, peer), device_id_type=MESH)
        return carry

    def greet_line(k, carry):
        peer = lax.rem(line + k, lines)
        pl.semaphore_signal(barrier, inc=1, device_id=(peer, leaf), device_id_type=MESH)
        return carry

    lax.fori_loop(1, lines, greet_line, 0)
    lax.fori_loop(1, PEERS, greet_leaf, 0)

    lane = lanes(hands)
    weight_one = to_lanes(range_one[...])
    show, fold = leaf_scales(pots, kinds, 8)
    show = [s[0:1] for s in show]
    fold = [f[0:1] for f in fold]
    unit = CODE / ONE_TOP
    stage[...] = jnp.zeros_like(stage)
    for load in loads:
        load.wait()
    pl.semaphore_wait(barrier, PEERS - 1 + lines - 1)

    def line_copy(src, dst, sends, recvs, peer, slot):
        return pltpu.make_async_remote_copy(
            src_ref=src,
            dst_ref=dst.at[slot],
            send_sem=sends.at[peer],
            recv_sem=recvs.at[slot],
            device_id=(peer, leaf),
            device_id_type=MESH,
        )

    def line_sum(src, dst, sends, recvs):
        def start(k, carry):
            line_copy(src, dst, sends, recvs, lax.rem(line + k, lines), line).start()
            return carry

        lax.fori_loop(1, lines, start, 0)
        dst[line] = src[...]

        def wait(k, carry):
            peer = lax.rem(line + k, lines)
            line_copy(src, dst, sends, recvs, peer, peer).wait_recv()
            return carry

        lax.fori_loop(1, lines, wait, 0)
        total = dst[0]
        for t in range(1, lines):
            total = total + dst[t]
        return total

    def line_sent(src, dst, sends, recvs):
        def wait(k, carry):
            line_copy(src, dst, sends, recvs, lax.rem(line + k, lines), line).wait_send()
            return carry

        lax.fori_loop(1, lines, wait, 0)

    turn_share = turn_regret[...] / line_sum(turn_regret, turns, turn_send, turn_recv)
    weight_zero = to_lanes(range_zero[...] * turn_share)

    def y_copy(w, peer):
        return pltpu.make_async_remote_copy(
            src_ref=yq.at[w],
            dst_ref=recv.at[leaf],
            send_sem=y_send.at[w],
            recv_sem=y_recv.at[leaf],
            device_id=(line, peer),
            device_id_type=MESH,
        )

    def prepare(k, carry):
        w = lax.rem(first_worker + k, WORKERS)
        slot = lax.rem(k, 2)
        _, zs = zero_shares(rz, w, lane, hands)
        _, os = one_shares(ro, w, lane, hands)
        z = (weight_zero * zs).astype(BF16).astype(F32)
        power = power_above(jnp.max(z, axis=0, keepdims=True))
        o = [(weight_one * s).astype(BF16).astype(F32) for s in os]
        stage[slot, 0:hands] = nearest(z * (CODE * jnp.exp2(-power)))
        for j, scale in enumerate((show, fold)):
            mixed = o[0] * scale[0] + o[1] * scale[1] + o[2] * scale[2]
            stage[slot, (j + 1) * hands : (j + 2) * hands] = nearest(mixed * unit)
        stage[slot, 3 * hands : 3 * hands + 1] = power
        yq[w] = code(stage[slot, 0:ROWS])
        peer = worker_leaf(w)

        @pl.when(peer != leaf)
        def _():
            y_copy(w, peer).start()

        @pl.when(peer == leaf)
        def _():
            recv[leaf] = yq[w]

        return carry

    lax.fori_loop(0, WORKERS, prepare, 0)

    def out_copy(peer):
        return pltpu.make_async_remote_copy(
            src_ref=out.at[peer],
            dst_ref=back.at[w_self],
            send_sem=out_send.at[peer],
            recv_sem=out_recv.at[w_self],
            device_id=(line, peer),
            device_id_type=MESH,
        )

    @pl.when(is_worker)
    def _():
        low = lanes(8)[0:1] < 64
        source_hand = lax.broadcasted_iota(jnp.int32, (PEERS * hands, 128), 0)
        place = source_hand + (HP - hands) * (source_hand // hands)
        for j in range(KP // 128):
            here = lanes(PEERS * hands) + 128 * j
            spread[:, pl.ds(128 * j, 128)] = (place == here).astype(F32).astype(BF16)
        card_pad[...] = jnp.zeros_like(card_pad)
        card_pad[0:2] = (cards[...] + 1).astype(F32)
        eight = pl.ds(pl.multiple_of(8 * (w_self // 4), 8), 8)
        ranks = all_ranks[eight].astype(F32)
        high = jnp.floor(ranks * (1.0 / 64.0))
        rest = ranks - 64.0 * high

        def spread_rows(v):
            return jnp.dot(v.astype(BF16), spread[...], preferred_element_type=F32)

        card_rows = spread_rows(card_pad[...]).astype(BF16)
        high_rows = spread_rows(high)
        rest_rows = spread_rows(rest)
        one_row = lax.broadcasted_iota(jnp.int32, (8, 128), 0)
        pick = lambda r, scale: jnp.where(one_row == r, scale, 0.0).astype(BF16)
        first = column(card_rows, pick(0, 1.0)) - 1.0
        second = column(card_rows, pick(1, 1.0)) - 1.0
        usable = (first < 52.0) & (second < 52.0) & (first >= 0.0)
        for k in range(4):
            board = dealt[k].astype(F32)
            usable = usable & (first != board) & (second != board)
        rivers = [dealt[4 + 2 * w_self + c].astype(F32) for c in range(2)]
        river = jnp.where(low, rivers[0], rivers[1])
        col[2] = (usable & (first != river) & (second != river)).astype(F32)
        card = lanes(KP).astype(F32)
        inc[...] = ((first == card) | (second == card)).astype(F32).astype(BF16)
        rank_rows = 64.0 * high_rows + rest_rows
        wide_row = lax.broadcasted_iota(jnp.int32, (8, KP), 0)
        for c in range(2):
            r = 2 * lax.rem(w_self, 4) + c
            rank_row[c : c + 1] = jnp.sum(
                jnp.where(wide_row == r, rank_rows, 0.0), axis=0, keepdims=True
            )
            col[c] = column(high_rows.astype(BF16), pick(r, 64.0)) + column(
                rest_rows.astype(BF16), pick(r, 1.0)
            )

        def build(i, carry):
            rows = pl.ds(pl.multiple_of(i * MB, MB), MB)
            for j in range(KP // 128):
                js = pl.ds(128 * j, 128)
                shared = lax.dot_general(
                    inc[rows], inc[js], (((1,), (1,)), ((), ())), preferred_element_type=F32
                )
                apart = jnp.maximum(1.0 - shared, 0.0)
                mat[2, rows, js] = apart.astype(BF16)
                for c in range(2):
                    gap = col[c, rows] - rank_row[c : c + 1, js]
                    sign = jnp.minimum(jnp.maximum(gap, -1.0), 1.0)
                    mat[c, rows, js] = (sign * apart).astype(BF16)
            return carry

        lax.fori_loop(0, KP // MB, build, 0)

        def arrive(k, carry):
            z_sum, w_sum = carry
            source = lax.rem(leaf + k, PEERS)
            slot = lax.rem(k, 2)

            @pl.when(k > 0)
            def _():
                pltpu.make_async_remote_copy(
                    src_ref=yq.at[0],
                    dst_ref=recv.at[source],
                    send_sem=y_send.at[0],
                    recv_sem=y_recv.at[source],
                    device_id=(line, source),
                    device_id_type=MESH,
                ).wait_recv()

            rows = pl.ds(pl.multiple_of(source * HP, HP), HP)
            v = col[2, rows]
            coded = decode(recv[source])
            stage[slot, 0:ROWS] = coded
            scale = jnp.exp2(stage[slot, 3 * hands : 3 * hands + 1]) * (1.0 / CODE)
            z = (stage[slot, 0:HP] * (v * scale)).astype(BF16)
            ws = stage[slot, hands : hands + HP] * v
            wf = stage[slot, 2 * hands : 2 * hands + HP] * v
            s_high = jnp.floor(ws * (1.0 / 256.0))
            s_low = ws - 256.0 * s_high
            f_high = jnp.floor(wf * (1.0 / 256.0))
            f_low = wf - 256.0 * f_high
            x[rows, 0:128] = z
            x[rows, 128:256] = f_high.astype(BF16)
            x[rows, 256:384] = f_low.astype(BF16)
            x[rows, 384:512] = jnp.where(low, s_high, roll_half(s_low)).astype(BF16)
            x[rows, 512:640] = jnp.where(low, roll_half(s_high), s_low).astype(BF16)
            return (z_sum + z.astype(F32), w_sum + ws + jnp.abs(wf))

        empty = jnp.zeros((HP, 128), F32)
        z_sum, w_sum = lax.fori_loop(0, PEERS, arrive, (empty, empty))
        z_power = power_above(jnp.sum(z_sum, axis=0, keepdims=True))
        w_power = power_above(jnp.sum(w_sum, axis=0, keepdims=True) * (1.0 / unit))
        z_scale = CODE * jnp.exp2(-z_power)
        w_scale = (CODE / unit) * jnp.exp2(-w_power)
        low_part = jnp.where(low, 256.0, 1.0)

        def block(k, carry):
            i = lax.rem(leaf // (BLOCK // HP) + k, KP // BLOCK)
            rows = pl.ds(pl.multiple_of(i * BLOCK, BLOCK), BLOCK)
            d = jnp.dot(mat[2, rows], x[:, 0:384], preferred_element_type=F32)
            s0z = jnp.dot(mat[0, rows], x[:, 0:128], preferred_element_type=F32)
            s0w = jnp.dot(mat[0, rows], x[:, 384:512], preferred_element_type=F32)
            s1z = jnp.dot(mat[1, rows], x[:, 0:128], preferred_element_type=F32)
            s1w = jnp.dot(mat[1, rows], x[:, 512:640], preferred_element_type=F32)
            v = col[2, rows]
            s0w = s0w * low_part
            s1w = s1w * low_part
            s0w = s0w + roll_half(s0w)
            s1w = s1w + roll_half(s1w)
            act = jnp.where(low, s0w, s1w) + 256.0 * d[:, 128:256] + d[:, 256:384]
            tiles = (
                act * (v * w_scale),
                jnp.where(low, s0z, s1z) * (v * z_scale),
                d[:, 0:128] * (v * z_scale),
            )
            tiles = [nearest(jnp.minimum(jnp.maximum(t, -CODE), CODE)) for t in tiles]
            for m in range(BLOCK // HP):
                for j in range(3):
                    stage[m, j * hands : j * hands + HP] = tiles[j][m * HP : (m + 1) * HP]
                stage[m, 3 * hands : 3 * hands + 1] = w_power
                stage[m, 3 * hands + 1 : 3 * hands + 2] = z_power
                peer = i * (BLOCK // HP) + m
                out[peer] = code(stage[m, 0:ROWS])

                @pl.when(peer != leaf)
                def _():
                    out_copy(peer).start()

                @pl.when(peer == leaf)
                def _():
                    back[w_self] = out[peer]

            return carry

        lax.fori_loop(0, KP // BLOCK, block, 0)

    def update(k, carry):
        sum_zero, sum_one = carry
        w = lax.rem(first_worker + k, WORKERS)
        slot = lax.rem(k, 2)
        peer = worker_leaf(w)

        @pl.when(peer != leaf)
        def _():
            pltpu.make_async_remote_copy(
                src_ref=out.at[0],
                dst_ref=back.at[w],
                send_sem=out_send.at[0],
                recv_sem=out_recv.at[w],
                device_id=(line, peer),
                device_id_type=MESH,
            ).wait_recv()

        r, zs = zero_shares(rz, w, lane, hands)
        regrets, os = one_shares(ro, w, lane, hands)
        stage[slot, 0:ROWS] = decode(back[w])
        w_scale = jnp.exp2(stage[slot, 3 * hands : 3 * hands + 1]) * (1.0 / CODE)
        z_scale = jnp.exp2(stage[slot, 3 * hands + 1 : 3 * hands + 2]) * (1.0 / CODE)
        act = stage[slot, 0:hands] * w_scale
        sz = stage[slot, hands : 2 * hands] * z_scale
        dz = stage[slot, 2 * hands : 3 * hands] * z_scale
        node = action_sum(zs * act, lane)
        new_rz[pl.ds(w, hands, stride=WORKERS)] = jnp.maximum(r + act - node, 0.0)
        leaf_one = [show[b] * sz - fold[b] * dz for b in range(MOVES_ONE)]
        node_one = os[0] * leaf_one[0] + os[1] * leaf_one[1] + os[2] * leaf_one[2]
        new = [jnp.maximum(regrets[b] + leaf_one[b] - node_one, 0.0) for b in range(MOVES_ONE)]
        native = join_moves(new, lane)
        for v in range(3):
            new_ro[pl.ds(3 * w + v, hands, stride=3 * WORKERS)] = native[v]
        return (sum_zero + node, sum_one + node_one)

    zero = jnp.zeros((hands, 128), F32)
    sum_zero, sum_one = lax.fori_loop(0, WORKERS, update, (zero, zero))
    sum_zero = jnp.where(lane % 64 < SUBGAMES, sum_zero, 0.0)
    values = [
        CHANCE
        * lax.dot_general(
            tile_selector(),
            total,
            (((1,), (1,)), ((), ())),
            precision=lax.Precision.HIGHEST,
            preferred_element_type=F32,
        )
        for total in (sum_zero, sum_one)
    ]
    own[0] = turn_share * values[0]
    own[1] = values[1]
    total = line_sum(own, parts, root_send, root_recv)
    roots[...] = total
    new_turn[...] = jnp.maximum(turn_regret[...] + values[0] - total[0], 0.0)

    def y_sent(k, carry):
        w = lax.rem(first_worker + k, WORKERS)
        peer = worker_leaf(w)

        @pl.when(peer != leaf)
        def _():
            y_copy(w, peer).wait_send()

        return carry

    lax.fori_loop(0, WORKERS, y_sent, 0)

    @pl.when(is_worker)
    def _():
        def sent(k, carry):
            out_copy(lax.rem(leaf + k, PEERS)).wait_send()
            return carry

        lax.fori_loop(1, PEERS, sent, 0)

    line_sent(turn_regret, turns, turn_send, turn_recv)
    line_sent(own, parts, root_send, root_recv)


VM = pl.BlockSpec(memory_space=pltpu.VMEM)
SM = pl.BlockSpec(memory_space=pltpu.SMEM)
HB = pl.BlockSpec(memory_space=pl.ANY)
LIMIT = 56 << 20


def local(
    range_zero,
    range_one,
    turn_regret,
    river_regret_zero,
    river_regret_one,
    hand_cards,
    dealt_cards,
    hand_ranks,
    leaf_pots,
    leaf_kinds,
):
    hands = range_zero.shape[1]
    lines = lax.axis_size("river")
    tr = turn_regret[0]
    rz = river_regret_zero.reshape(hands * WORKERS, 128)
    ro = river_regret_one.reshape(hands * 3 * WORKERS, 128)
    dma = pltpu.SemaphoreType.DMA
    i16 = jnp.int16
    new_turn, new_rz, new_ro, roots = pl.pallas_call(
        kernel,
        out_shape=(
            jax.ShapeDtypeStruct(tr.shape, F32),
            jax.ShapeDtypeStruct(rz.shape, F32),
            jax.ShapeDtypeStruct(ro.shape, F32),
            jax.ShapeDtypeStruct((2,) + tr.shape, F32),
        ),
        in_specs=[HB, HB, VM, VM, VM, VM, VM, SM, SM, SM],
        out_specs=(VM, VM, VM, VM),
        scratch_shapes=[
            pltpu.VMEM(rz.shape, F32),
            pltpu.VMEM(ro.shape, F32),
            pltpu.VMEM((lines,) + tr.shape, F32),
            pltpu.VMEM((WORKERS, ROWS, 128), i16),
            pltpu.VMEM((PEERS, ROWS, 128), i16),
            pltpu.VMEM((BLOCK // HP, STAGE, 128), F32),
            pltpu.VMEM((PEERS * hands, KP), BF16),
            pltpu.VMEM((8, PEERS * hands), F32),
            pltpu.VMEM((8, KP), F32),
            pltpu.VMEM((KP, 640), BF16),
            pltpu.VMEM((3, KP, KP), BF16),
            pltpu.VMEM((3, KP, 128), F32),
            pltpu.VMEM((KP, 128), BF16),
            pltpu.VMEM((PEERS, ROWS, 128), i16),
            pltpu.VMEM((WORKERS, ROWS, 128), i16),
            pltpu.VMEM((2,) + tr.shape, F32),
            pltpu.VMEM((lines, 2) + tr.shape, F32),
            dma((2,)),
            dma((lines,)),
            dma((lines,)),
            dma((WORKERS,)),
            dma((PEERS,)),
            dma((PEERS,)),
            dma((WORKERS,)),
            dma((lines,)),
            dma((lines,)),
        ],
        compiler_params=pltpu.CompilerParams(
            collective_id=1, has_side_effects=True, vmem_limit_bytes=LIMIT
        ),
    )(
        rz,
        ro,
        range_zero,
        range_one,
        tr,
        hand_cards.T,
        hand_ranks,
        dealt_cards,
        leaf_pots,
        leaf_kinds,
    )
    return (
        new_turn[None],
        new_rz.reshape(river_regret_zero.shape),
        new_ro.reshape(river_regret_one.shape),
        roots,
    )


def solution(mesh):
    placed = (
        P(None, "leaf"),
        P(None, "leaf"),
        P("river", None, "leaf"),
        P("river", "leaf", None),
        P("river", "leaf", None),
        P(),
        P(),
        P(),
        P("river", None),
        P("river", None),
    )
    return jax.shard_map(
        local,
        mesh=mesh,
        in_specs=placed,
        out_specs=(
            P("river", None, "leaf"),
            P("river", "leaf", None),
            P("river", "leaf", None),
            P(None, None, "leaf"),
        ),
        check_vma=False,
    )
```

```python
import jax
import jax.numpy as jnp
from jax import lax
from jax.experimental import pallas as pl
from jax.experimental.pallas import tpu as pltpu
from jax.sharding import PartitionSpec as P

MESH = pl.DeviceIdType.MESH
F32 = jnp.float32
BF16 = jnp.bfloat16
RIVERS = 48
MOVES_ZERO = 4
MOVES_ONE = 3
SUBGAMES = 16
WORKERS = 24
PEERS = 32
HP = 48
KP = PEERS * HP
MB = 384
BLOCK = 384
CHANCE = 1.0 / 44.0


def worker_leaf(w, line):
    z = w // 3
    x = lax.rem(w - 3 * z + 1 + z + 2 * lax.rem(line, 2), 4)
    return 4 * z + x


def leaf_worker(leaf, line):
    z = leaf // 4
    x = leaf - 4 * z
    k = lax.rem(x - 1 - z - 2 * lax.rem(line, 2) + 16, 4)
    return k, 3 * z + k


def far_first(k, half):
    h = (k + 1) // 2
    return half + h * (1 - 2 * lax.rem(k, 2))


def lanes(rows):
    return lax.broadcasted_iota(jnp.int32, (rows, 128), 1)


def gather_lanes(x, index):
    return jnp.take_along_axis(x, index, axis=1, mode="promise_in_bounds")


def roll_half(x):
    return pltpu.roll(x, 64, 1)


def action_sum(x, lane):
    x = x + gather_lanes(x, (lane & 64) | ((lane + 16) & 63))
    return x + gather_lanes(x, (lane & 64) | ((lane + 32) & 63))


def split_moves(tiles, lane):
    slot, sub = lane // 16, lane % 16
    out = []
    for b in range(MOVES_ONE):
        group = (3 * (slot - b + 8)) % 8
        tile = (3 * group + b) // 8
        picked = jnp.where(tile == 0, tiles[0], jnp.where(tile == 1, tiles[1], tiles[2]))
        out.append(gather_lanes(picked, ((3 * slot + b) % 8) * 16 + sub))
    return out


def join_moves(parts, lane):
    slot, sub = lane // 16, lane % 16
    moved = []
    for b in range(MOVES_ONE):
        group = (3 * (slot - b + 8)) % 8
        moved.append(gather_lanes(parts[b], group * 16 + sub))
    out = []
    for v in range(3):
        b = (8 * v + slot) % 3
        out.append(jnp.where(b == 0, moved[0], jnp.where(b == 1, moved[1], moved[2])))
    return out


def tile_selector():
    sub = lax.broadcasted_iota(jnp.int32, (SUBGAMES, 128), 0)
    lane = lanes(SUBGAMES)
    return (lane % SUBGAMES == sub).astype(F32)


def to_lanes(x):
    return lax.dot_general(
        x,
        tile_selector(),
        (((0,), (0,)), ((), ())),
        precision=lax.Precision.HIGHEST,
        preferred_element_type=F32,
    )


def leaf_scales(pots, kinds, rows):
    action = (lanes(rows) // SUBGAMES) % MOVES_ZERO
    show, fold = [], []
    for b in range(MOVES_ONE):
        s = jnp.zeros((rows, 128), F32)
        f = jnp.zeros((rows, 128), F32)
        for a in range(MOVES_ZERO):
            pot = pots[0, a * MOVES_ONE + b].astype(F32)
            kind = kinds[0, a * MOVES_ONE + b]
            here = action == a
            s = jnp.where(here, jnp.where(kind == 0, pot, 0.0), s)
            f = jnp.where(here, jnp.where(kind == 0, 0.0, jnp.where(kind == 1, pot, -pot)), f)
        show.append(s)
        fold.append(f)
    return show, fold


ONE_TOP = 64.0 * 0.001 * 1.005
CODE = 32760.0
ROWS = 128
STAGE = 136


def column(rows, select):
    return lax.dot_general(
        rows, select, (((0,), (0,)), ((), ())), preferred_element_type=F32
    )


def code(x):
    return x.astype(jnp.int32).astype(jnp.int16)


def decode(x):
    return x.astype(jnp.int32).astype(F32)


def nearest(x):
    return jnp.floor(x + 0.5)


def power_above(x):
    return jnp.floor(jnp.log2(jnp.maximum(x, 1e-30))) + 1.0


def zero_shares(rz, w, lane, hands):
    x = rz[pl.ds(w, hands, stride=WORKERS)]
    return x, x / action_sum(x, lane)


def one_shares(ro, w, lane, hands):
    tiles = [ro[pl.ds(3 * w + v, hands, stride=3 * WORKERS)] for v in range(3)]
    regrets = split_moves(tiles, lane)
    scale = 1.0 / (regrets[0] + regrets[1] + regrets[2])
    return regrets, [r * scale for r in regrets]


def kernel(
    rz_hbm,
    ro_hbm,
    range_zero,
    range_one,
    turn_regret,
    cards,
    all_ranks,
    dealt,
    pots,
    kinds,
    new_turn,
    rz_out,
    ro_out,
    roots,
    rz,
    ro,
    new_rz,
    new_ro,
    turns,
    yq,
    recv,
    y_stage,
    stage,
    spread,
    card_pad,
    rank_row,
    x,
    mat,
    col,
    inc,
    out,
    back,
    own,
    parts,
    load_sem,
    turn_send,
    turn_recv,
    y_send,
    y_recv,
    out_send,
    out_recv,
    root_send,
    root_recv,
):
    line, leaf = lax.axis_index("river"), lax.axis_index("leaf")
    lines = turns.shape[0]
    k_self, w_self = leaf_worker(leaf, line)
    is_worker = k_self < 3
    hands = turn_regret.shape[1]
    z_self = leaf // 4
    x_self = leaf - 4 * z_self

    def forward_worker(k):
        step = far_first(k // 3, 4)
        return 3 * lax.rem(z_self + step, 8) + lax.rem(k + x_self, 3)

    loads = [
        pltpu.make_async_copy(rz_hbm, rz, load_sem.at[0]),
        pltpu.make_async_copy(ro_hbm, ro, load_sem.at[1]),
    ]
    for load in loads:
        load.start()

    barrier = pltpu.get_barrier_semaphore()

    def greet_leaf(k, carry):
        peer = lax.rem(leaf + k, PEERS)
        pl.semaphore_signal(barrier, inc=1, device_id=(line, peer), device_id_type=MESH)
        return carry

    def greet_line(k, carry):
        peer = lax.rem(line + k, lines)
        pl.semaphore_signal(barrier, inc=1, device_id=(peer, leaf), device_id_type=MESH)
        return carry

    lax.fori_loop(1, lines, greet_line, 0)
    lax.fori_loop(1, PEERS, greet_leaf, 0)

    lane = lanes(hands)
    weight_one = to_lanes(range_one[...])
    show, fold = leaf_scales(pots, kinds, 8)
    show = [s[0:1] for s in show]
    fold = [f[0:1] for f in fold]
    unit = CODE / ONE_TOP
    stage[...] = jnp.zeros_like(stage)
    y_stage[:, 120:ROWS] = jnp.zeros((WORKERS, ROWS - 120, 128), F32)
    for load in loads:
        load.wait()
    pl.semaphore_wait(barrier, PEERS - 1 + lines - 1)

    def line_copy(src, dst, sends, recvs, peer, slot):
        return pltpu.make_async_remote_copy(
            src_ref=src,
            dst_ref=dst.at[slot],
            send_sem=sends.at[peer],
            recv_sem=recvs.at[slot],
            device_id=(peer, leaf),
            device_id_type=MESH,
        )

    def line_start(src, dst, sends, recvs):
        def start(k, carry):
            line_copy(src, dst, sends, recvs, lax.rem(line + k, lines), line).start()
            return carry

        lax.fori_loop(1, lines, start, 0)

    def line_sum(src, dst, sends, recvs):
        dst[line] = src[...]

        def wait(k, carry):
            peer = lax.rem(line + k, lines)
            line_copy(src, dst, sends, recvs, peer, peer).wait_recv()
            return carry

        lax.fori_loop(1, lines, wait, 0)
        total = dst[0]
        for t in range(1, lines):
            total = total + dst[t]
        return total

    def line_sent(src, dst, sends, recvs):
        def wait(k, carry):
            line_copy(src, dst, sends, recvs, lax.rem(line + k, lines), line).wait_send()
            return carry

        lax.fori_loop(1, lines, wait, 0)

    line_start(turn_regret, turns, turn_send, turn_recv)

    def prepare_one(w, carry):
        _, os = one_shares(ro, w, lane, hands)
        o = [(weight_one * s).astype(BF16).astype(F32) for s in os]
        for j, scale in enumerate((show, fold)):
            mixed = o[0] * scale[0] + o[1] * scale[1] + o[2] * scale[2]
            y_stage[w, (j + 1) * hands : (j + 2) * hands] = nearest(mixed * unit)
        return carry

    lax.fori_loop(0, WORKERS, prepare_one, 0)
    turn_share = turn_regret[...] / line_sum(turn_regret, turns, turn_send, turn_recv)
    weight_zero = to_lanes(range_zero[...] * turn_share)

    def y_copy(w, peer):
        return pltpu.make_async_remote_copy(
            src_ref=yq.at[w],
            dst_ref=recv.at[leaf],
            send_sem=y_send.at[w],
            recv_sem=y_recv.at[leaf],
            device_id=(line, peer),
            device_id_type=MESH,
        )

    def prepare(k, carry):
        w = forward_worker(k)
        _, zs = zero_shares(rz, w, lane, hands)
        z = (weight_zero * zs).astype(BF16).astype(F32)
        power = power_above(jnp.max(z, axis=0, keepdims=True))
        y_stage[w, 0:hands] = nearest(z * (CODE * jnp.exp2(-power)))
        y_stage[w, 3 * hands : 3 * hands + 1] = power
        yq[w] = code(y_stage[w, 0:ROWS])
        peer = worker_leaf(w, line)

        @pl.when(peer != leaf)
        def _():
            y_copy(w, peer).start()

        @pl.when(peer == leaf)
        def _():
            recv[leaf] = yq[w]

        return carry

    lax.fori_loop(0, WORKERS, prepare, 0)

    def out_copy(peer):
        return pltpu.make_async_remote_copy(
            src_ref=out.at[peer],
            dst_ref=back.at[w_self],
            send_sem=out_send.at[peer],
            recv_sem=out_recv.at[w_self],
            device_id=(line, peer),
            device_id_type=MESH,
        )

    @pl.when(is_worker)
    def _():
        low = lanes(8)[0:1] < 64
        source_hand = lax.broadcasted_iota(jnp.int32, (PEERS * hands, 128), 0)
        place = source_hand + (HP - hands) * (source_hand // hands)
        for j in range(KP // 128):
            here = lanes(PEERS * hands) + 128 * j
            spread[:, pl.ds(128 * j, 128)] = (place == here).astype(F32).astype(BF16)
        card_pad[...] = jnp.zeros_like(card_pad)
        card_pad[0:2] = (cards[...] + 1).astype(F32)
        eight = pl.ds(pl.multiple_of(8 * (w_self // 4), 8), 8)
        ranks = all_ranks[eight].astype(F32)
        high = jnp.floor(ranks * (1.0 / 64.0))
        rest = ranks - 64.0 * high

        def spread_rows(v):
            return jnp.dot(v.astype(BF16), spread[...], preferred_element_type=F32)

        card_rows = spread_rows(card_pad[...]).astype(BF16)
        high_rows = spread_rows(high)
        rest_rows = spread_rows(rest)
        one_row = lax.broadcasted_iota(jnp.int32, (8, 128), 0)
        pick = lambda r, scale: jnp.where(one_row == r, scale, 0.0).astype(BF16)
        first = column(card_rows, pick(0, 1.0)) - 1.0
        second = column(card_rows, pick(1, 1.0)) - 1.0
        usable = (first < 52.0) & (second < 52.0) & (first >= 0.0)
        for k in range(4):
            board = dealt[k].astype(F32)
            usable = usable & (first != board) & (second != board)
        rivers = [dealt[4 + 2 * w_self + c].astype(F32) for c in range(2)]
        river = jnp.where(low, rivers[0], rivers[1])
        col[2] = (usable & (first != river) & (second != river)).astype(F32)
        card = lanes(KP).astype(F32)
        inc[...] = ((first == card) | (second == card)).astype(F32).astype(BF16)
        rank_rows = 64.0 * high_rows + rest_rows
        wide_row = lax.broadcasted_iota(jnp.int32, (8, KP), 0)
        for c in range(2):
            r = 2 * lax.rem(w_self, 4) + c
            rank_row[c : c + 1] = jnp.sum(
                jnp.where(wide_row == r, rank_rows, 0.0), axis=0, keepdims=True
            )
            col[c] = column(high_rows.astype(BF16), pick(r, 64.0)) + column(
                rest_rows.astype(BF16), pick(r, 1.0)
            )

        def build(i, carry):
            rows = pl.ds(pl.multiple_of(i * MB, MB), MB)
            for j in range(KP // 128):
                js = pl.ds(128 * j, 128)
                shared = lax.dot_general(
                    inc[rows], inc[js], (((1,), (1,)), ((), ())), preferred_element_type=F32
                )
                apart = jnp.maximum(1.0 - shared, 0.0)
                mat[2, rows, js] = apart.astype(BF16)
                for c in range(2):
                    gap = col[c, rows] - rank_row[c : c + 1, js]
                    sign = jnp.minimum(jnp.maximum(gap, -1.0), 1.0)
                    mat[c, rows, js] = (sign * apart).astype(BF16)
            return carry

        lax.fori_loop(0, KP // MB, build, 0)

        def arrive(k, carry):
            z_sum, w_sum = carry
            source_z = lax.rem(z_self - far_first(k // 4, 4) + 16, 8)
            source = 4 * source_z + lax.rem(k + x_self, 4)
            slot = lax.rem(k, 2)

            @pl.when(source != leaf)
            def _():
                pltpu.make_async_remote_copy(
                    src_ref=yq.at[0],
                    dst_ref=recv.at[source],
                    send_sem=y_send.at[0],
                    recv_sem=y_recv.at[source],
                    device_id=(line, source),
                    device_id_type=MESH,
                ).wait_recv()

            rows = pl.ds(pl.multiple_of(source * HP, HP), HP)
            v = col[2, rows]
            coded = decode(recv[source])
            stage[slot, 0:ROWS] = coded
            scale = jnp.exp2(stage[slot, 3 * hands : 3 * hands + 1]) * (1.0 / CODE)
            z = (stage[slot, 0:HP] * (v * scale)).astype(BF16)
            ws = stage[slot, hands : hands + HP] * v
            wf = stage[slot, 2 * hands : 2 * hands + HP] * v
            s_high = jnp.floor(ws * (1.0 / 256.0))
            s_low = ws - 256.0 * s_high
            f_high = jnp.floor(wf * (1.0 / 256.0))
            f_low = wf - 256.0 * f_high
            x[rows, 0:128] = z
            x[rows, 128:256] = f_high.astype(BF16)
            x[rows, 256:384] = f_low.astype(BF16)
            x[rows, 384:512] = jnp.where(low, s_high, roll_half(s_low)).astype(BF16)
            x[rows, 512:640] = jnp.where(low, roll_half(s_high), s_low).astype(BF16)
            return (z_sum + z.astype(F32), w_sum + ws + jnp.abs(wf))

        empty = jnp.zeros((HP, 128), F32)
        z_sum, w_sum = lax.fori_loop(0, PEERS, arrive, (empty, empty))
        z_power = power_above(jnp.sum(z_sum, axis=0, keepdims=True))
        w_power = power_above(jnp.sum(w_sum, axis=0, keepdims=True) * (1.0 / unit))
        z_scale = CODE * jnp.exp2(-z_power)
        w_scale = (CODE / unit) * jnp.exp2(-w_power)
        low_part = jnp.where(low, 256.0, 1.0)

        def block(k, carry):
            i = lax.rem(z_self // 2 + far_first(k, 2), 4)
            rows = pl.ds(pl.multiple_of(i * BLOCK, BLOCK), BLOCK)
            d = jnp.dot(mat[2, rows], x[:, 0:384], preferred_element_type=F32)
            s0z = jnp.dot(mat[0, rows], x[:, 0:128], preferred_element_type=F32)
            s0w = jnp.dot(mat[0, rows], x[:, 384:512], preferred_element_type=F32)
            s1z = jnp.dot(mat[1, rows], x[:, 0:128], preferred_element_type=F32)
            s1w = jnp.dot(mat[1, rows], x[:, 512:640], preferred_element_type=F32)
            v = col[2, rows]
            s0w = s0w * low_part
            s1w = s1w * low_part
            s0w = s0w + roll_half(s0w)
            s1w = s1w + roll_half(s1w)
            act = jnp.where(low, s0w, s1w) + 256.0 * d[:, 128:256] + d[:, 256:384]
            tiles = (
                act * (v * w_scale),
                jnp.where(low, s0z, s1z) * (v * z_scale),
                d[:, 0:128] * (v * z_scale),
            )
            tiles = [nearest(jnp.minimum(jnp.maximum(t, -CODE), CODE)) for t in tiles]
            for m in range(BLOCK // HP):
                for j in range(3):
                    stage[m, j * hands : j * hands + HP] = tiles[j][m * HP : (m + 1) * HP]
                stage[m, 3 * hands : 3 * hands + 1] = w_power
                stage[m, 3 * hands + 1 : 3 * hands + 2] = z_power
                peer = i * (BLOCK // HP) + m
                out[peer] = code(stage[m, 0:ROWS])

                @pl.when(peer != leaf)
                def _():
                    out_copy(peer).start()

                @pl.when(peer == leaf)
                def _():
                    back[w_self] = out[peer]

            return carry

        lax.fori_loop(0, KP // BLOCK, block, 0)

    def update(k, carry):
        sum_zero, sum_one = carry
        pair = lax.rem(z_self // 2 - far_first(k // 6, 2) + 8, 4)
        w = 6 * pair + lax.rem(k, 6)
        slot = lax.rem(k, 2)
        peer = worker_leaf(w, line)

        @pl.when(peer != leaf)
        def _():
            pltpu.make_async_remote_copy(
                src_ref=out.at[0],
                dst_ref=back.at[w],
                send_sem=out_send.at[0],
                recv_sem=out_recv.at[w],
                device_id=(line, peer),
                device_id_type=MESH,
            ).wait_recv()

        r, zs = zero_shares(rz, w, lane, hands)
        regrets, os = one_shares(ro, w, lane, hands)
        stage[slot, 0:ROWS] = decode(back[w])
        w_scale = jnp.exp2(stage[slot, 3 * hands : 3 * hands + 1]) * (1.0 / CODE)
        z_scale = jnp.exp2(stage[slot, 3 * hands + 1 : 3 * hands + 2]) * (1.0 / CODE)
        act = stage[slot, 0:hands] * w_scale
        sz = stage[slot, hands : 2 * hands] * z_scale
        dz = stage[slot, 2 * hands : 3 * hands] * z_scale
        node = action_sum(zs * act, lane)
        new_rz[pl.ds(w, hands, stride=WORKERS)] = jnp.maximum(r + act - node, 0.0)
        leaf_one = [show[b] * sz - fold[b] * dz for b in range(MOVES_ONE)]
        node_one = os[0] * leaf_one[0] + os[1] * leaf_one[1] + os[2] * leaf_one[2]
        new = [jnp.maximum(regrets[b] + leaf_one[b] - node_one, 0.0) for b in range(MOVES_ONE)]
        native = join_moves(new, lane)
        for v in range(3):
            new_ro[pl.ds(3 * w + v, hands, stride=3 * WORKERS)] = native[v]
        return (sum_zero + node, sum_one + node_one)

    zero = jnp.zeros((hands, 128), F32)
    sum_zero, sum_one = lax.fori_loop(0, WORKERS, update, (zero, zero))
    stores = [
        pltpu.make_async_copy(new_rz, rz_out, load_sem.at[2]),
        pltpu.make_async_copy(new_ro, ro_out, load_sem.at[3]),
    ]
    for store in stores:
        store.start()
    sum_zero = jnp.where(lane % 64 < SUBGAMES, sum_zero, 0.0)
    values = [
        CHANCE
        * lax.dot_general(
            tile_selector(),
            total,
            (((1,), (1,)), ((), ())),
            precision=lax.Precision.HIGHEST,
            preferred_element_type=F32,
        )
        for total in (sum_zero, sum_one)
    ]
    own[0] = turn_share * values[0]
    own[1] = values[1]
    line_start(own, parts, root_send, root_recv)
    total = line_sum(own, parts, root_send, root_recv)
    roots[...] = total
    new_turn[...] = jnp.maximum(turn_regret[...] + values[0] - total[0], 0.0)

    def y_sent(k, carry):
        w = forward_worker(k)
        peer = worker_leaf(w, line)

        @pl.when(peer != leaf)
        def _():
            y_copy(w, peer).wait_send()

        return carry

    lax.fori_loop(0, WORKERS, y_sent, 0)

    @pl.when(is_worker)
    def _():
        def sent(k, carry):
            out_copy(lax.rem(leaf + k, PEERS)).wait_send()
            return carry

        lax.fori_loop(1, PEERS, sent, 0)

    line_sent(turn_regret, turns, turn_send, turn_recv)
    line_sent(own, parts, root_send, root_recv)
    for store in stores:
        store.wait()


def place_kernel(*refs):
    count = (len(refs) - 2) // 3
    srcs, dsts, held = refs[:count], refs[count : 2 * count], refs[2 * count : 3 * count]
    load_sem, store_sem = refs[-2], refs[-1]
    loads, stores = [], []
    for k in range(count):
        loads.append(pltpu.make_async_copy(srcs[k], held[k], load_sem.at[k]))
        stores.append(pltpu.make_async_copy(held[k], dsts[k], store_sem.at[k]))
        loads[k].start()
    for k in range(count):
        loads[k].wait()
        stores[k].start()
    for k in range(count):
        stores[k].wait()


VM = pl.BlockSpec(memory_space=pltpu.VMEM)
SM = pl.BlockSpec(memory_space=pltpu.SMEM)
HB = pl.BlockSpec(memory_space=pl.ANY)
LIMIT = 56 << 20


def local(
    range_zero,
    range_one,
    turn_regret,
    river_regret_zero,
    river_regret_one,
    hand_cards,
    dealt_cards,
    hand_ranks,
    leaf_pots,
    leaf_kinds,
):
    hands = range_zero.shape[1]
    lines = lax.axis_size("river")
    tr = turn_regret[0]
    rz = river_regret_zero.reshape(hands * WORKERS, 128)
    ro = river_regret_one.reshape(hands * 3 * WORKERS, 128)
    dma = pltpu.SemaphoreType.DMA
    i16 = jnp.int16
    new_turn, new_rz, new_ro, roots = pl.pallas_call(
        kernel,
        out_shape=(
            jax.ShapeDtypeStruct(tr.shape, F32),
            jax.ShapeDtypeStruct(rz.shape, F32),
            jax.ShapeDtypeStruct(ro.shape, F32),
            jax.ShapeDtypeStruct((2,) + tr.shape, F32),
        ),
        in_specs=[HB, HB, VM, VM, VM, VM, VM, SM, SM, SM],
        out_specs=(VM, HB, HB, VM),
        scratch_shapes=[
            pltpu.VMEM(rz.shape, F32),
            pltpu.VMEM(ro.shape, F32),
            pltpu.VMEM(rz.shape, F32),
            pltpu.VMEM(ro.shape, F32),
            pltpu.VMEM((lines,) + tr.shape, F32),
            pltpu.VMEM((WORKERS, ROWS, 128), i16),
            pltpu.VMEM((PEERS, ROWS, 128), i16),
            pltpu.VMEM((WORKERS, ROWS, 128), F32),
            pltpu.VMEM((BLOCK // HP, STAGE, 128), F32),
            pltpu.VMEM((PEERS * hands, KP), BF16),
            pltpu.VMEM((8, PEERS * hands), F32),
            pltpu.VMEM((8, KP), F32),
            pltpu.VMEM((KP, 640), BF16),
            pltpu.VMEM((3, KP, KP), BF16),
            pltpu.VMEM((3, KP, 128), F32),
            pltpu.VMEM((KP, 128), BF16),
            pltpu.VMEM((PEERS, ROWS, 128), i16),
            pltpu.VMEM((WORKERS, ROWS, 128), i16),
            pltpu.VMEM((2,) + tr.shape, F32),
            pltpu.VMEM((lines, 2) + tr.shape, F32),
            dma((4,)),
            dma((lines,)),
            dma((lines,)),
            dma((WORKERS,)),
            dma((PEERS,)),
            dma((PEERS,)),
            dma((WORKERS,)),
            dma((lines,)),
            dma((lines,)),
        ],
        compiler_params=pltpu.CompilerParams(
            collective_id=1, has_side_effects=True, vmem_limit_bytes=LIMIT
        ),
    )(
        rz,
        ro,
        range_zero,
        range_one,
        tr,
        hand_cards.T,
        hand_ranks,
        dealt_cards,
        leaf_pots,
        leaf_kinds,
    )
    results = (new_turn, new_rz, new_ro, roots)
    new_turn, new_rz, new_ro, roots = pl.pallas_call(
        place_kernel,
        out_shape=tuple(jax.ShapeDtypeStruct(r.shape, F32) for r in results),
        in_specs=[HB] * 4,
        out_specs=(HB,) * 4,
        scratch_shapes=[pltpu.VMEM(r.shape, F32) for r in results] + [dma((4,)), dma((4,))],
    )(*results)
    return (
        new_turn[None],
        new_rz.reshape(river_regret_zero.shape),
        new_ro.reshape(river_regret_one.shape),
        roots,
    )


def solution(mesh):
    placed = (
        P(None, "leaf"),
        P(None, "leaf"),
        P("river", None, "leaf"),
        P("river", "leaf", None),
        P("river", "leaf", None),
        P(),
        P(),
        P(),
        P("river", None),
        P("river", None),
    )
    return jax.shard_map(
        local,
        mesh=mesh,
        in_specs=placed,
        out_specs=(
            P("river", None, "leaf"),
            P("river", "leaf", None),
            P("river", "leaf", None),
            P(None, None, "leaf"),
        ),
        check_vma=False,
    )
```

```python
import jax
import jax.numpy as jnp
from jax import lax
from jax.experimental import pallas as pl
from jax.experimental.pallas import tpu as pltpu
from jax.sharding import PartitionSpec as P

MESH = pl.DeviceIdType.MESH
F32 = jnp.float32
BF16 = jnp.bfloat16
RIVERS = 48
MOVES_ZERO = 4
MOVES_ONE = 3
SUBGAMES = 16
WORKERS = 24
PEERS = 32
HP = 48
KP = PEERS * HP
MB = 384
BLOCK = 384
CHANCE = 1.0 / 44.0


def worker_leaf(w, line):
    z = w // 3
    x = lax.rem(w - 3 * z + 1 + z + 2 * lax.rem(line, 2), 4)
    return 4 * z + x


def leaf_worker(leaf, line):
    z = leaf // 4
    x = leaf - 4 * z
    k = lax.rem(x - 1 - z - 2 * lax.rem(line, 2) + 16, 4)
    return k, 3 * z + k


def far_first(k, half):
    h = (k + 1) // 2
    return half + h * (1 - 2 * lax.rem(k, 2))


def lanes(rows):
    return lax.broadcasted_iota(jnp.int32, (rows, 128), 1)


def gather_lanes(x, index):
    return jnp.take_along_axis(x, index, axis=1, mode="promise_in_bounds")


def roll_half(x):
    return pltpu.roll(x, 64, 1)


def action_sum(x, lane):
    x = x + gather_lanes(x, (lane & 64) | ((lane + 16) & 63))
    return x + gather_lanes(x, (lane & 64) | ((lane + 32) & 63))


def split_moves(tiles, lane):
    slot, sub = lane // 16, lane % 16
    out = []
    for b in range(MOVES_ONE):
        group = (3 * (slot - b + 8)) % 8
        tile = (3 * group + b) // 8
        picked = jnp.where(tile == 0, tiles[0], jnp.where(tile == 1, tiles[1], tiles[2]))
        out.append(gather_lanes(picked, ((3 * slot + b) % 8) * 16 + sub))
    return out


def join_moves(parts, lane):
    slot, sub = lane // 16, lane % 16
    moved = []
    for b in range(MOVES_ONE):
        group = (3 * (slot - b + 8)) % 8
        moved.append(gather_lanes(parts[b], group * 16 + sub))
    out = []
    for v in range(3):
        b = (8 * v + slot) % 3
        out.append(jnp.where(b == 0, moved[0], jnp.where(b == 1, moved[1], moved[2])))
    return out


def tile_selector():
    sub = lax.broadcasted_iota(jnp.int32, (SUBGAMES, 128), 0)
    lane = lanes(SUBGAMES)
    return (lane % SUBGAMES == sub).astype(F32)


def to_lanes(x):
    return lax.dot_general(
        x,
        tile_selector(),
        (((0,), (0,)), ((), ())),
        precision=lax.Precision.HIGHEST,
        preferred_element_type=F32,
    )


def leaf_scales(pots, kinds, rows):
    action = (lanes(rows) // SUBGAMES) % MOVES_ZERO
    show, fold = [], []
    for b in range(MOVES_ONE):
        s = jnp.zeros((rows, 128), F32)
        f = jnp.zeros((rows, 128), F32)
        for a in range(MOVES_ZERO):
            pot = pots[0, a * MOVES_ONE + b].astype(F32)
            kind = kinds[0, a * MOVES_ONE + b]
            here = action == a
            s = jnp.where(here, jnp.where(kind == 0, pot, 0.0), s)
            f = jnp.where(here, jnp.where(kind == 0, 0.0, jnp.where(kind == 1, pot, -pot)), f)
        show.append(s)
        fold.append(f)
    return show, fold


ONE_TOP = 64.0 * 0.001 * 1.005
CODE = 32760.0
ROWS = 128
STAGE = 136
SPLIT = 80
EARLY = 16


def column(rows, select):
    return lax.dot_general(
        rows, select, (((0,), (0,)), ((), ())), preferred_element_type=F32
    )


def code(x):
    return x.astype(jnp.int32).astype(jnp.int16)


def decode(x):
    return x.astype(jnp.int32).astype(F32)


def nearest(x):
    return jnp.floor(x + 0.5)


def power_above(x):
    return jnp.floor(jnp.log2(jnp.maximum(x, 1e-30))) + 1.0


def zero_shares(rz, w, lane, hands):
    x = rz[pl.ds(w, hands, stride=WORKERS)]
    return x, x / action_sum(x, lane)


def one_regrets(ro, w, lane, hands):
    tiles = [ro[pl.ds(3 * w + v, hands, stride=3 * WORKERS)] for v in range(3)]
    regrets = split_moves(tiles, lane)
    return regrets, 1.0 / (regrets[0] + regrets[1] + regrets[2])


def kernel(
    rz_hbm,
    ro_hbm,
    range_zero,
    range_one,
    turn_regret,
    cards,
    all_ranks,
    dealt,
    pots,
    kinds,
    new_turn,
    rz_out,
    ro_out,
    roots,
    rz,
    ro,
    new_rz,
    new_ro,
    turns,
    yq,
    recv,
    kept,
    y_stage,
    stage,
    spread,
    card_pad,
    rank_row,
    x,
    mat,
    col,
    inc,
    out,
    back,
    own,
    parts,
    load_sem,
    turn_send,
    turn_recv,
    y_send,
    y_recv,
    out_send,
    out_recv,
    root_send,
    root_recv,
):
    line, leaf = lax.axis_index("river"), lax.axis_index("leaf")
    lines = turns.shape[0]
    k_self, w_self = leaf_worker(leaf, line)
    is_worker = k_self < 3
    hands = turn_regret.shape[1]
    z_self = leaf // 4
    x_self = leaf - 4 * z_self

    def forward_worker(k):
        step = far_first(k // 3, 4)
        return 3 * lax.rem(z_self + step, 8) + lax.rem(k + x_self, 3)

    loads = [
        pltpu.make_async_copy(rz_hbm, rz, load_sem.at[0]),
        pltpu.make_async_copy(ro_hbm, ro, load_sem.at[1]),
    ]
    for load in loads:
        load.start()

    barrier = pltpu.get_barrier_semaphore()

    def greet_leaf(k, carry):
        peer = lax.rem(leaf + k, PEERS)
        pl.semaphore_signal(barrier, inc=1, device_id=(line, peer), device_id_type=MESH)
        return carry

    def greet_line(k, carry):
        peer = lax.rem(line + k, lines)
        pl.semaphore_signal(barrier, inc=1, device_id=(peer, leaf), device_id_type=MESH)
        return carry

    lax.fori_loop(1, lines, greet_line, 0)
    lax.fori_loop(1, PEERS, greet_leaf, 0)

    lane = lanes(hands)
    weight_one = to_lanes(range_one[...])
    show, fold = leaf_scales(pots, kinds, 8)
    show = [s[0:1] for s in show]
    fold = [f[0:1] for f in fold]
    unit = CODE / ONE_TOP
    stage[...] = jnp.zeros_like(stage)
    y_stage[:, 120:ROWS] = jnp.zeros((WORKERS, ROWS - 120, 128), F32)
    for load in loads:
        load.wait()
    pl.semaphore_wait(barrier, PEERS - 1 + lines - 1)

    def line_copy(src, dst, sends, recvs, peer, slot):
        return pltpu.make_async_remote_copy(
            src_ref=src,
            dst_ref=dst.at[slot],
            send_sem=sends.at[peer],
            recv_sem=recvs.at[slot],
            device_id=(peer, leaf),
            device_id_type=MESH,
        )

    def line_start(src, dst, sends, recvs):
        def start(k, carry):
            line_copy(src, dst, sends, recvs, lax.rem(line + k, lines), line).start()
            return carry

        lax.fori_loop(1, lines, start, 0)

    def line_sum(src, dst, sends, recvs):
        dst[line] = src[...]

        def wait(k, carry):
            peer = lax.rem(line + k, lines)
            line_copy(src, dst, sends, recvs, peer, peer).wait_recv()
            return carry

        lax.fori_loop(1, lines, wait, 0)
        total = dst[0]
        for t in range(1, lines):
            total = total + dst[t]
        return total

    def line_sent(src, dst, sends, recvs):
        def wait(k, carry):
            line_copy(src, dst, sends, recvs, lax.rem(line + k, lines), line).wait_send()
            return carry

        lax.fori_loop(1, lines, wait, 0)

    line_start(turn_regret, turns, turn_send, turn_recv)

    def y_copy(part, w, peer, slot):
        rows = (pl.ds(0, SPLIT), pl.ds(SPLIT, ROWS - SPLIT))[part]
        return pltpu.make_async_remote_copy(
            src_ref=yq.at[w, rows],
            dst_ref=recv.at[slot, rows],
            send_sem=y_send.at[part, w],
            recv_sem=y_recv.at[part, slot],
            device_id=(line, peer),
            device_id_type=MESH,
        )

    def hand_over(part, w):
        peer = worker_leaf(w, line)
        rows = (pl.ds(0, SPLIT), pl.ds(SPLIT, ROWS - SPLIT))[part]
        yq[w, rows] = code(y_stage[w, rows])

        @pl.when(peer != leaf)
        def _():
            y_copy(part, w, peer, leaf).start()

        @pl.when(peer == leaf)
        def _():
            recv[leaf, rows] = yq[w, rows]

    def prepare_one(k, carry):
        w = forward_worker(k)
        regrets, scale = one_regrets(ro, w, lane, hands)
        for b in range(MOVES_ONE):
            kept[w, b, 0:hands] = regrets[b]
        kept[w, 3, 0:hands] = scale
        o = [(weight_one * (r * scale)).astype(BF16).astype(F32) for r in regrets]
        for j, pot in enumerate((show, fold)):
            mixed = o[0] * pot[0] + o[1] * pot[1] + o[2] * pot[2]
            y_stage[w, j * hands : (j + 1) * hands] = nearest(mixed * unit)
        hand_over(0, w)
        return carry

    lax.fori_loop(0, WORKERS, prepare_one, 0)
    turn_share = turn_regret[...] / line_sum(turn_regret, turns, turn_send, turn_recv)
    weight_zero = to_lanes(range_zero[...] * turn_share)

    def prepare_zero(k, carry):
        w = forward_worker(k)
        _, zs = zero_shares(rz, w, lane, hands)
        kept[w, 4, 0:hands] = zs
        z = (weight_zero * zs).astype(BF16).astype(F32)
        power = power_above(jnp.max(z, axis=0, keepdims=True))
        y_stage[w, 2 * hands : 3 * hands] = nearest(z * (CODE * jnp.exp2(-power)))
        y_stage[w, 3 * hands : 3 * hands + 1] = power
        hand_over(1, w)
        return carry

    lax.fori_loop(0, WORKERS, prepare_zero, 0)

    def out_copy(peer):
        return pltpu.make_async_remote_copy(
            src_ref=out.at[peer],
            dst_ref=back.at[w_self],
            send_sem=out_send.at[peer],
            recv_sem=out_recv.at[w_self],
            device_id=(line, peer),
            device_id_type=MESH,
        )

    @pl.when(is_worker)
    def _():
        low = lanes(8)[0:1] < 64
        source_hand = lax.broadcasted_iota(jnp.int32, (PEERS * hands, 128), 0)
        place = source_hand + (HP - hands) * (source_hand // hands)
        for j in range(KP // 128):
            here = lanes(PEERS * hands) + 128 * j
            spread[:, pl.ds(128 * j, 128)] = (place == here).astype(F32).astype(BF16)
        card_pad[...] = jnp.zeros_like(card_pad)
        card_pad[0:2] = (cards[...] + 1).astype(F32)
        eight = pl.ds(pl.multiple_of(8 * (w_self // 4), 8), 8)
        ranks = all_ranks[eight].astype(F32)
        high = jnp.floor(ranks * (1.0 / 64.0))
        rest = ranks - 64.0 * high

        def spread_rows(v):
            return jnp.dot(v.astype(BF16), spread[...], preferred_element_type=F32)

        card_rows = spread_rows(card_pad[...]).astype(BF16)
        high_rows = spread_rows(high)
        rest_rows = spread_rows(rest)
        one_row = lax.broadcasted_iota(jnp.int32, (8, 128), 0)
        pick = lambda r, scale: jnp.where(one_row == r, scale, 0.0).astype(BF16)
        first = column(card_rows, pick(0, 1.0)) - 1.0
        second = column(card_rows, pick(1, 1.0)) - 1.0
        usable = (first < 52.0) & (second < 52.0) & (first >= 0.0)
        for k in range(4):
            board = dealt[k].astype(F32)
            usable = usable & (first != board) & (second != board)
        rivers = [dealt[4 + 2 * w_self + c].astype(F32) for c in range(2)]
        river = jnp.where(low, rivers[0], rivers[1])
        col[2] = (usable & (first != river) & (second != river)).astype(F32)
        card = lanes(KP).astype(F32)
        inc[...] = ((first == card) | (second == card)).astype(F32).astype(BF16)
        rank_rows = 64.0 * high_rows + rest_rows
        wide_row = lax.broadcasted_iota(jnp.int32, (8, KP), 0)
        for c in range(2):
            r = 2 * lax.rem(w_self, 4) + c
            rank_row[c : c + 1] = jnp.sum(
                jnp.where(wide_row == r, rank_rows, 0.0), axis=0, keepdims=True
            )
            col[c] = column(high_rows.astype(BF16), pick(r, 64.0)) + column(
                rest_rows.astype(BF16), pick(r, 1.0)
            )

        def build(i, carry):
            rows = pl.ds(pl.multiple_of(i * MB, MB), MB)
            for j in range(KP // 128):
                js = pl.ds(128 * j, 128)
                shared = lax.dot_general(
                    inc[rows], inc[js], (((1,), (1,)), ((), ())), preferred_element_type=F32
                )
                apart = jnp.maximum(1.0 - shared, 0.0)
                mat[2, rows, js] = apart.astype(BF16)
                for c in range(2):
                    gap = col[c, rows] - rank_row[c : c + 1, js]
                    sign = jnp.minimum(jnp.maximum(gap, -1.0), 1.0)
                    mat[c, rows, js] = (sign * apart).astype(BF16)
            return carry

        lax.fori_loop(0, KP // MB, build, 0)

        def arrival(part, k):
            source_z = lax.rem(z_self - far_first(k // 4, 4) + 16, 8)
            source = 4 * source_z + lax.rem(k + x_self, 4)

            @pl.when(source != leaf)
            def _():
                y_copy(part, 0, source, source).wait_recv()

            rows = pl.ds(pl.multiple_of(source * HP, HP), HP)
            return source, rows, col[2, rows]

        def arrive_one(k, w_sum):
            source, rows, v = arrival(0, k)
            ws = decode(recv[source, 0:HP]) * v
            s_high = jnp.floor(ws * (1.0 / 256.0))
            s_low = ws - 256.0 * s_high
            x[rows, 384:512] = jnp.where(low, s_high, roll_half(s_low)).astype(BF16)
            x[rows, 512:640] = jnp.where(low, roll_half(s_high), s_low).astype(BF16)
            return w_sum + ws

        def arrive_two(k, carry):
            z_sum, w_sum = carry
            source, rows, v = arrival(1, k)
            slot = lax.rem(k, 2)
            stage[slot, 32:ROWS] = decode(recv[source, 32:ROWS])
            scale = jnp.exp2(stage[slot, 3 * hands : 3 * hands + 1]) * (1.0 / CODE)
            wf = stage[slot, hands : hands + HP] * v
            z = (stage[slot, 2 * hands : 2 * hands + HP] * (v * scale)).astype(BF16)
            f_high = jnp.floor(wf * (1.0 / 256.0))
            f_low = wf - 256.0 * f_high
            x[rows, 0:128] = z
            x[rows, 128:256] = f_high.astype(BF16)
            x[rows, 256:384] = f_low.astype(BF16)
            return (z_sum + z.astype(F32), w_sum + jnp.abs(wf))

        empty = jnp.zeros((HP, 128), F32)
        w_sum = lax.fori_loop(0, PEERS, arrive_one, empty)
        z_sum, w_sum = lax.fori_loop(0, PEERS, arrive_two, (empty, w_sum))
        z_power = power_above(jnp.sum(z_sum, axis=0, keepdims=True))
        w_power = power_above(jnp.sum(w_sum, axis=0, keepdims=True) * (1.0 / unit))
        z_scale = CODE * jnp.exp2(-z_power)
        w_scale = (CODE / unit) * jnp.exp2(-w_power)
        low_part = jnp.where(low, 256.0, 1.0)

        def block(k, carry):
            i = lax.rem(z_self // 2 + far_first(k, 2), 4)
            rows = pl.ds(pl.multiple_of(i * BLOCK, BLOCK), BLOCK)
            d = jnp.dot(mat[2, rows], x[:, 0:384], preferred_element_type=F32)
            s0z = jnp.dot(mat[0, rows], x[:, 0:128], preferred_element_type=F32)
            s0w = jnp.dot(mat[0, rows], x[:, 384:512], preferred_element_type=F32)
            s1z = jnp.dot(mat[1, rows], x[:, 0:128], preferred_element_type=F32)
            s1w = jnp.dot(mat[1, rows], x[:, 512:640], preferred_element_type=F32)
            v = col[2, rows]
            s0w = s0w * low_part
            s1w = s1w * low_part
            s0w = s0w + roll_half(s0w)
            s1w = s1w + roll_half(s1w)
            act = jnp.where(low, s0w, s1w) + 256.0 * d[:, 128:256] + d[:, 256:384]
            tiles = (
                act * (v * w_scale),
                jnp.where(low, s0z, s1z) * (v * z_scale),
                d[:, 0:128] * (v * z_scale),
            )
            tiles = [nearest(jnp.minimum(jnp.maximum(t, -CODE), CODE)) for t in tiles]
            for m in range(BLOCK // HP):
                for j in range(3):
                    stage[m, j * hands : j * hands + HP] = tiles[j][m * HP : (m + 1) * HP]
                stage[m, 3 * hands : 3 * hands + 1] = w_power
                stage[m, 3 * hands + 1 : 3 * hands + 2] = z_power
                peer = i * (BLOCK // HP) + m
                out[peer] = code(stage[m, 0:ROWS])

                @pl.when(peer != leaf)
                def _():
                    out_copy(peer).start()

                @pl.when(peer == leaf)
                def _():
                    back[w_self] = out[peer]

            return carry

        lax.fori_loop(0, KP // BLOCK, block, 0)

    def values_of(k):
        pair = lax.rem(z_self // 2 - far_first(k // 6, 2) + 8, 4)
        w = 6 * pair + lax.rem(k, 6)
        slot = lax.rem(k, 2)
        stage[slot, 0:ROWS] = decode(back[w])
        w_scale = jnp.exp2(stage[slot, 3 * hands : 3 * hands + 1]) * (1.0 / CODE)
        z_scale = jnp.exp2(stage[slot, 3 * hands + 1 : 3 * hands + 2]) * (1.0 / CODE)
        act = stage[slot, 0:hands] * w_scale
        sz = stage[slot, hands : 2 * hands] * z_scale
        dz = stage[slot, 2 * hands : 3 * hands] * z_scale
        node = action_sum(kept[w, 4, 0:hands] * act, lane)
        regrets = [kept[w, b, 0:hands] for b in range(MOVES_ONE)]
        leaf_one = [show[b] * sz - fold[b] * dz for b in range(MOVES_ONE)]
        node_one = regrets[0] * leaf_one[0] + regrets[1] * leaf_one[1] + regrets[2] * leaf_one[2]
        return w, act, node, regrets, leaf_one, node_one * kept[w, 3, 0:hands]

    def collect(k, carry):
        pair = lax.rem(z_self // 2 - far_first(k // 6, 2) + 8, 4)
        w = 6 * pair + lax.rem(k, 6)
        peer = worker_leaf(w, line)

        @pl.when(peer != leaf)
        def _():
            pltpu.make_async_remote_copy(
                src_ref=out.at[0],
                dst_ref=back.at[w],
                send_sem=out_send.at[0],
                recv_sem=out_recv.at[w],
                device_id=(line, peer),
                device_id_type=MESH,
            ).wait_recv()

        return carry

    def renew(values):
        w, act, node, regrets, leaf_one, node_one = values
        r = rz[pl.ds(w, hands, stride=WORKERS)]
        new_rz[pl.ds(w, hands, stride=WORKERS)] = jnp.maximum(r + act - node, 0.0)
        new = [jnp.maximum(regrets[b] + leaf_one[b] - node_one, 0.0) for b in range(MOVES_ONE)]
        native = join_moves(new, lane)
        for v in range(3):
            new_ro[pl.ds(3 * w + v, hands, stride=3 * WORKERS)] = native[v]

    def update(k, carry):
        collect(k, 0)
        values = values_of(k)
        renew(values)
        return (carry[0] + values[2], carry[1] + values[5])

    def sum_only(k, carry):
        collect(k, 0)
        values = values_of(k)
        return (carry[0] + values[2], carry[1] + values[5])

    def finish(k, carry):
        renew(values_of(k))
        return carry

    zero = jnp.zeros((hands, 128), F32)
    sums = lax.fori_loop(0, EARLY, update, (zero, zero))
    sum_zero, sum_one = lax.fori_loop(EARLY, WORKERS, sum_only, sums)
    sum_zero = jnp.where(lane % 64 < SUBGAMES, sum_zero, 0.0)
    values = [
        CHANCE
        * lax.dot_general(
            tile_selector(),
            total,
            (((1,), (1,)), ((), ())),
            precision=lax.Precision.HIGHEST,
            preferred_element_type=F32,
        )
        for total in (sum_zero, sum_one)
    ]
    own[0] = turn_share * values[0]
    own[1] = values[1]
    line_start(own, parts, root_send, root_recv)
    lax.fori_loop(EARLY, WORKERS, finish, 0)
    stores = [
        pltpu.make_async_copy(new_rz, rz_out, load_sem.at[2]),
        pltpu.make_async_copy(new_ro, ro_out, load_sem.at[3]),
    ]
    for store in stores:
        store.start()
    total = line_sum(own, parts, root_send, root_recv)
    roots[...] = total
    new_turn[...] = jnp.maximum(turn_regret[...] + values[0] - total[0], 0.0)

    def y_sent(k, carry):
        w = forward_worker(k)
        peer = worker_leaf(w, line)

        @pl.when(peer != leaf)
        def _():
            y_copy(0, w, peer, leaf).wait_send()
            y_copy(1, w, peer, leaf).wait_send()

        return carry

    lax.fori_loop(0, WORKERS, y_sent, 0)

    @pl.when(is_worker)
    def _():
        def sent(k, carry):
            out_copy(lax.rem(leaf + k, PEERS)).wait_send()
            return carry

        lax.fori_loop(1, PEERS, sent, 0)

    line_sent(turn_regret, turns, turn_send, turn_recv)
    line_sent(own, parts, root_send, root_recv)
    for store in stores:
        store.wait()


def place_kernel(*refs):
    count = (len(refs) - 2) // 3
    srcs, dsts, held = refs[:count], refs[count : 2 * count], refs[2 * count : 3 * count]
    load_sem, store_sem = refs[-2], refs[-1]
    loads, stores = [], []
    for k in range(count):
        loads.append(pltpu.make_async_copy(srcs[k], held[k], load_sem.at[k]))
        stores.append(pltpu.make_async_copy(held[k], dsts[k], store_sem.at[k]))
        loads[k].start()
    for k in range(count):
        loads[k].wait()
        stores[k].start()
    for k in range(count):
        stores[k].wait()


VM = pl.BlockSpec(memory_space=pltpu.VMEM)
SM = pl.BlockSpec(memory_space=pltpu.SMEM)
HB = pl.BlockSpec(memory_space=pl.ANY)
LIMIT = 56 << 20


def local(
    range_zero,
    range_one,
    turn_regret,
    river_regret_zero,
    river_regret_one,
    hand_cards,
    dealt_cards,
    hand_ranks,
    leaf_pots,
    leaf_kinds,
):
    hands = range_zero.shape[1]
    lines = lax.axis_size("river")
    tr = turn_regret[0]
    rz = river_regret_zero.reshape(hands * WORKERS, 128)
    ro = river_regret_one.reshape(hands * 3 * WORKERS, 128)
    dma = pltpu.SemaphoreType.DMA
    i16 = jnp.int16
    new_turn, new_rz, new_ro, roots = pl.pallas_call(
        kernel,
        out_shape=(
            jax.ShapeDtypeStruct(tr.shape, F32),
            jax.ShapeDtypeStruct(rz.shape, F32),
            jax.ShapeDtypeStruct(ro.shape, F32),
            jax.ShapeDtypeStruct((2,) + tr.shape, F32),
        ),
        in_specs=[HB, HB, VM, VM, VM, VM, VM, SM, SM, SM],
        out_specs=(VM, HB, HB, VM),
        scratch_shapes=[
            pltpu.VMEM(rz.shape, F32),
            pltpu.VMEM(ro.shape, F32),
            pltpu.VMEM(rz.shape, F32),
            pltpu.VMEM(ro.shape, F32),
            pltpu.VMEM((lines,) + tr.shape, F32),
            pltpu.VMEM((WORKERS, ROWS, 128), i16),
            pltpu.VMEM((PEERS, ROWS, 128), i16),
            pltpu.VMEM((WORKERS, 5, HP, 128), F32),
            pltpu.VMEM((WORKERS, ROWS, 128), F32),
            pltpu.VMEM((BLOCK // HP, STAGE, 128), F32),
            pltpu.VMEM((PEERS * hands, KP), BF16),
            pltpu.VMEM((8, PEERS * hands), F32),
            pltpu.VMEM((8, KP), F32),
            pltpu.VMEM((KP, 640), BF16),
            pltpu.VMEM((3, KP, KP), BF16),
            pltpu.VMEM((3, KP, 128), F32),
            pltpu.VMEM((KP, 128), BF16),
            pltpu.VMEM((PEERS, ROWS, 128), i16),
            pltpu.VMEM((WORKERS, ROWS, 128), i16),
            pltpu.VMEM((2,) + tr.shape, F32),
            pltpu.VMEM((lines, 2) + tr.shape, F32),
            dma((4,)),
            dma((lines,)),
            dma((lines,)),
            dma((2, WORKERS)),
            dma((2, PEERS)),
            dma((PEERS,)),
            dma((WORKERS,)),
            dma((lines,)),
            dma((lines,)),
        ],
        compiler_params=pltpu.CompilerParams(
            collective_id=1, has_side_effects=True, vmem_limit_bytes=LIMIT
        ),
    )(
        rz,
        ro,
        range_zero,
        range_one,
        tr,
        hand_cards.T,
        hand_ranks,
        dealt_cards,
        leaf_pots,
        leaf_kinds,
    )
    results = (new_turn, new_rz, new_ro, roots)
    new_turn, new_rz, new_ro, roots = pl.pallas_call(
        place_kernel,
        out_shape=tuple(jax.ShapeDtypeStruct(r.shape, F32) for r in results),
        in_specs=[HB] * 4,
        out_specs=(HB,) * 4,
        scratch_shapes=[pltpu.VMEM(r.shape, F32) for r in results] + [dma((4,)), dma((4,))],
    )(*results)
    return (
        new_turn[None],
        new_rz.reshape(river_regret_zero.shape),
        new_ro.reshape(river_regret_one.shape),
        roots,
    )


def solution(mesh):
    placed = (
        P(None, "leaf"),
        P(None, "leaf"),
        P("river", None, "leaf"),
        P("river", "leaf", None),
        P("river", "leaf", None),
        P(),
        P(),
        P(),
        P("river", None),
        P("river", None),
    )
    return jax.shard_map(
        local,
        mesh=mesh,
        in_specs=placed,
        out_specs=(
            P("river", None, "leaf"),
            P("river", "leaf", None),
            P("river", "leaf", None),
            P(None, None, "leaf"),
        ),
        check_vma=False,
    )
```

```python
import jax
import jax.numpy as jnp
from jax import lax
from jax.experimental import pallas as pl
from jax.experimental.pallas import tpu as pltpu
from jax.sharding import PartitionSpec as P

MESH = pl.DeviceIdType.MESH
F32 = jnp.float32
BF16 = jnp.bfloat16
RIVERS = 48
MOVES_ZERO = 4
MOVES_ONE = 3
SUBGAMES = 16
WORKERS = 24
PEERS = 32
HP = 48
KP = PEERS * HP
MB = 384
BLOCK = 384
CHANCE = 1.0 / 44.0


def worker_leaf(w, line):
    z = w // 3
    x = lax.rem(w - 3 * z + 1 + z + 2 * lax.rem(line, 2), 4)
    return 4 * z + x


def leaf_worker(leaf, line):
    z = leaf // 4
    x = leaf - 4 * z
    k = lax.rem(x - 1 - z - 2 * lax.rem(line, 2) + 16, 4)
    return k, 3 * z + k


def far_first(k, half):
    h = (k + 1) // 2
    return half + h * (1 - 2 * lax.rem(k, 2))


def lanes(rows):
    return lax.broadcasted_iota(jnp.int32, (rows, 128), 1)


def gather_lanes(x, index):
    return jnp.take_along_axis(x, index, axis=1, mode="promise_in_bounds")


def roll_half(x):
    return pltpu.roll(x, 64, 1)


def action_sum(x, lane):
    x = x + gather_lanes(x, (lane & 64) | ((lane + 16) & 63))
    return x + gather_lanes(x, (lane & 64) | ((lane + 32) & 63))


def split_moves(tiles, lane):
    slot, sub = lane // 16, lane % 16
    out = []
    for b in range(MOVES_ONE):
        group = (3 * (slot - b + 8)) % 8
        tile = (3 * group + b) // 8
        picked = jnp.where(tile == 0, tiles[0], jnp.where(tile == 1, tiles[1], tiles[2]))
        out.append(gather_lanes(picked, ((3 * slot + b) % 8) * 16 + sub))
    return out


def join_moves(parts, lane):
    slot, sub = lane // 16, lane % 16
    moved = []
    for b in range(MOVES_ONE):
        group = (3 * (slot - b + 8)) % 8
        moved.append(gather_lanes(parts[b], group * 16 + sub))
    out = []
    for v in range(3):
        b = (8 * v + slot) % 3
        out.append(jnp.where(b == 0, moved[0], jnp.where(b == 1, moved[1], moved[2])))
    return out


def tile_selector():
    sub = lax.broadcasted_iota(jnp.int32, (SUBGAMES, 128), 0)
    lane = lanes(SUBGAMES)
    return (lane % SUBGAMES == sub).astype(F32)


def to_lanes(x):
    return lax.dot_general(
        x,
        tile_selector(),
        (((0,), (0,)), ((), ())),
        precision=lax.Precision.HIGHEST,
        preferred_element_type=F32,
    )


def leaf_scales(pots, kinds, rows):
    action = (lanes(rows) // SUBGAMES) % MOVES_ZERO
    show, fold = [], []
    for b in range(MOVES_ONE):
        s = jnp.zeros((rows, 128), F32)
        f = jnp.zeros((rows, 128), F32)
        for a in range(MOVES_ZERO):
            pot = pots[0, a * MOVES_ONE + b].astype(F32)
            kind = kinds[0, a * MOVES_ONE + b]
            here = action == a
            s = jnp.where(here, jnp.where(kind == 0, pot, 0.0), s)
            f = jnp.where(here, jnp.where(kind == 0, 0.0, jnp.where(kind == 1, pot, -pot)), f)
        show.append(s)
        fold.append(f)
    return show, fold


ONE_TOP = 64.0 * 0.001 * 1.005
CODE = 32760.0
ROWS = 128
STAGE = 136
SPLIT = 80
EARLY = 5
PLANE = 4
TRIO = 3


def column(rows, select):
    return lax.dot_general(
        rows, select, (((0,), (0,)), ((), ())), preferred_element_type=F32
    )


def code(x):
    return x.astype(jnp.int32).astype(jnp.int16)


def decode(x):
    return x.astype(jnp.int32).astype(F32)


def nearest(x):
    return jnp.floor(x + 0.5)


def power_above(x):
    return jnp.floor(jnp.log2(jnp.maximum(x, 1e-30))) + 1.0


def zero_shares(rz, w, lane, hands):
    x = rz[pl.ds(w, hands, stride=WORKERS)]
    return x, x / action_sum(x, lane)


def one_regrets(ro, w, lane, hands):
    tiles = [ro[pl.ds(3 * w + v, hands, stride=3 * WORKERS)] for v in range(3)]
    regrets = split_moves(tiles, lane)
    return regrets, 1.0 / (regrets[0] + regrets[1] + regrets[2])


def kernel(
    turn_hbm,
    ro_hbm,
    range_one_hbm,
    pots_hbm,
    kinds_hbm,
    rz_hbm,
    range_zero_hbm,
    cards_hbm,
    ranks_hbm,
    dealt_hbm,
    new_turn,
    rz_out,
    ro_out,
    roots,
    turn_regret,
    ro,
    range_one,
    pots,
    kinds,
    rz,
    range_zero,
    cards,
    all_ranks,
    dealt,
    new_rz,
    new_ro,
    turns,
    yq,
    recv,
    kept,
    y_stage,
    stage,
    spread,
    card_pad,
    rank_row,
    x,
    mat,
    col,
    inc,
    out,
    back,
    own,
    parts,
    load_sem,
    store_sem,
    turn_send,
    turn_recv,
    y_send,
    y_recv,
    out_send,
    out_recv,
    root_send,
    root_recv,
):
    line, leaf = lax.axis_index("river"), lax.axis_index("leaf")
    lines = turns.shape[0]
    k_self, w_self = leaf_worker(leaf, line)
    is_worker = k_self < 3
    hands = turn_regret.shape[1]
    z_self = leaf // 4
    x_self = leaf - 4 * z_self

    def forward_worker(k):
        step = far_first(k // 3, 4)
        return 3 * lax.rem(z_self + step, 8) + lax.rem(k + x_self, 3)

    sources = (
        turn_hbm,
        ro_hbm,
        range_one_hbm,
        pots_hbm,
        kinds_hbm,
        rz_hbm,
        range_zero_hbm,
        cards_hbm,
        ranks_hbm,
        dealt_hbm,
    )
    places = (turn_regret, ro, range_one, pots, kinds, rz, range_zero, cards, all_ranks, dealt)
    loads = [
        pltpu.make_async_copy(a, b, load_sem.at[k]) for k, (a, b) in enumerate(zip(sources, places))
    ]

    barrier = pltpu.get_barrier_semaphore()

    for load in loads[:2]:
        load.start()
    for k in range(1, lines):
        peer = lax.rem(line + k, lines)
        pl.semaphore_signal(barrier, inc=1, device_id=(peer, leaf), device_id_type=MESH)
    for k in range(1, PEERS):
        peer = lax.rem(leaf + k, PEERS)
        pl.semaphore_signal(barrier, inc=1, device_id=(line, peer), device_id_type=MESH)
    for load in loads[2:]:
        load.start()
    for load in loads:
        load.wait()

    lane = lanes(hands)
    weight_one = to_lanes(range_one[...])
    show, fold = leaf_scales(pots, kinds, 8)
    show = [s[0:1] for s in show]
    fold = [f[0:1] for f in fold]
    unit = CODE / ONE_TOP
    stage[...] = jnp.zeros_like(stage)
    y_stage[:, 120:ROWS] = jnp.zeros((WORKERS, ROWS - 120, 128), F32)
    pl.semaphore_wait(barrier, PEERS - 1 + lines - 1)

    def line_copy(src, dst, sends, recvs, peer, slot):
        return pltpu.make_async_remote_copy(
            src_ref=src,
            dst_ref=dst.at[slot],
            send_sem=sends.at[peer],
            recv_sem=recvs.at[slot],
            device_id=(peer, leaf),
            device_id_type=MESH,
        )

    def line_start(src, dst, sends, recvs):
        def start(k, carry):
            line_copy(src, dst, sends, recvs, lax.rem(line + k, lines), line).start()
            return carry

        lax.fori_loop(1, lines, start, 0)

    def line_sum(src, dst, sends, recvs):
        dst[line] = src[...]

        def wait(k, carry):
            peer = lax.rem(line + k, lines)
            line_copy(src, dst, sends, recvs, peer, peer).wait_recv()
            return carry

        lax.fori_loop(1, lines, wait, 0)
        total = dst[0]
        for t in range(1, lines):
            total = total + dst[t]
        return total

    def line_sent(src, dst, sends, recvs):
        def wait(k, carry):
            line_copy(src, dst, sends, recvs, lax.rem(line + k, lines), line).wait_send()
            return carry

        lax.fori_loop(1, lines, wait, 0)

    line_start(turn_regret, turns, turn_send, turn_recv)

    def y_copy(part, w, peer, slot):
        rows = (pl.ds(0, SPLIT), pl.ds(SPLIT, ROWS - SPLIT))[part]
        return pltpu.make_async_remote_copy(
            src_ref=yq.at[w, rows],
            dst_ref=recv.at[slot, rows],
            send_sem=y_send.at[part, w],
            recv_sem=y_recv.at[part, slot],
            device_id=(line, peer),
            device_id_type=MESH,
        )

    def hand_over(part, w):
        peer = worker_leaf(w, line)
        rows = (pl.ds(0, SPLIT), pl.ds(SPLIT, ROWS - SPLIT))[part]
        yq[w, rows] = code(y_stage[w, rows])

        @pl.when(peer != leaf)
        def _():
            y_copy(part, w, peer, leaf).start()

        @pl.when(peer == leaf)
        def _():
            recv[leaf, rows] = yq[w, rows]

    def prepare_one(k, carry):
        workers = [forward_worker(TRIO * k + m) for m in range(TRIO)]
        for w in workers:
            regrets, scale = one_regrets(ro, w, lane, hands)
            for b in range(MOVES_ONE):
                kept[w, b, 0:hands] = regrets[b]
            kept[w, 3, 0:hands] = scale
            o = [(weight_one * (r * scale)).astype(BF16).astype(F32) for r in regrets]
            for j, pot in enumerate((show, fold)):
                mixed = o[0] * pot[0] + o[1] * pot[1] + o[2] * pot[2]
                y_stage[w, j * hands : (j + 1) * hands] = nearest(mixed * unit)
        for w in workers:
            hand_over(0, w)
        return carry

    lax.fori_loop(0, WORKERS // TRIO, prepare_one, 0)
    turn_share = turn_regret[...] / line_sum(turn_regret, turns, turn_send, turn_recv)
    weight_zero = to_lanes(range_zero[...] * turn_share)

    def prepare_zero(k, carry):
        w = forward_worker(k)
        _, zs = zero_shares(rz, w, lane, hands)
        kept[w, 4, 0:hands] = zs
        z = (weight_zero * zs).astype(BF16).astype(F32)
        power = power_above(jnp.max(z, axis=0, keepdims=True))
        y_stage[w, 2 * hands : 3 * hands] = nearest(z * (CODE * jnp.exp2(-power)))
        y_stage[w, 3 * hands : 3 * hands + 1] = power
        hand_over(1, w)
        return carry

    lax.fori_loop(0, WORKERS, prepare_zero, 0)

    def out_copy(peer):
        return pltpu.make_async_remote_copy(
            src_ref=out.at[peer],
            dst_ref=back.at[w_self],
            send_sem=out_send.at[peer],
            recv_sem=out_recv.at[w_self],
            device_id=(line, peer),
            device_id_type=MESH,
        )

    @pl.when(is_worker)
    def _():
        low = lanes(8)[0:1] < 64
        source_hand = lax.broadcasted_iota(jnp.int32, (PEERS * hands, 128), 0)
        place = source_hand + (HP - hands) * (source_hand // hands)
        for j in range(KP // 128):
            here = lanes(PEERS * hands) + 128 * j
            spread[:, pl.ds(128 * j, 128)] = (place == here).astype(F32).astype(BF16)
        card_pad[...] = jnp.zeros_like(card_pad)
        card_pad[0:2] = (cards[...] + 1).astype(F32)
        eight = pl.ds(pl.multiple_of(8 * (w_self // 4), 8), 8)
        ranks = all_ranks[eight].astype(F32)
        high = jnp.floor(ranks * (1.0 / 64.0))
        rest = ranks - 64.0 * high

        def spread_rows(v):
            return jnp.dot(v.astype(BF16), spread[...], preferred_element_type=F32)

        card_rows = spread_rows(card_pad[...]).astype(BF16)
        high_rows = spread_rows(high)
        rest_rows = spread_rows(rest)
        one_row = lax.broadcasted_iota(jnp.int32, (8, 128), 0)
        pick = lambda r, scale: jnp.where(one_row == r, scale, 0.0).astype(BF16)
        first = column(card_rows, pick(0, 1.0)) - 1.0
        second = column(card_rows, pick(1, 1.0)) - 1.0
        usable = (first < 52.0) & (second < 52.0) & (first >= 0.0)
        for k in range(4):
            board = dealt[k].astype(F32)
            usable = usable & (first != board) & (second != board)
        rivers = [dealt[4 + 2 * w_self + c].astype(F32) for c in range(2)]
        river = jnp.where(low, rivers[0], rivers[1])
        col[2] = (usable & (first != river) & (second != river)).astype(F32)
        card = lanes(KP).astype(F32)
        inc[...] = ((first == card) | (second == card)).astype(F32).astype(BF16)
        rank_rows = 64.0 * high_rows + rest_rows
        wide_row = lax.broadcasted_iota(jnp.int32, (8, KP), 0)
        for c in range(2):
            r = 2 * lax.rem(w_self, 4) + c
            rank_row[c : c + 1] = jnp.sum(
                jnp.where(wide_row == r, rank_rows, 0.0), axis=0, keepdims=True
            )
            col[c] = column(high_rows.astype(BF16), pick(r, 64.0)) + column(
                rest_rows.astype(BF16), pick(r, 1.0)
            )

        def build(i, carry):
            rows = pl.ds(pl.multiple_of(i * MB, MB), MB)
            for j in range(KP // 128):
                js = pl.ds(128 * j, 128)
                shared = lax.dot_general(
                    inc[rows], inc[js], (((1,), (1,)), ((), ())), preferred_element_type=F32
                )
                apart = jnp.maximum(1.0 - shared, 0.0)
                mat[2, rows, js] = apart.astype(BF16)
                for c in range(2):
                    gap = col[c, rows] - rank_row[c : c + 1, js]
                    sign = jnp.minimum(jnp.maximum(gap, -1.0), 1.0)
                    mat[c, rows, js] = (sign * apart).astype(BF16)
            return carry

        lax.fori_loop(0, KP // MB, build, 0)

        def arrival(part, k):
            source_z = lax.rem(z_self - far_first(k, 4) + 16, 8)
            for m in range(PLANE):
                source = PLANE * source_z + m

                @pl.when(source != leaf)
                def _():
                    y_copy(part, 0, source, source).wait_recv()

            rows = pl.ds(pl.multiple_of(source_z * (PLANE * HP), PLANE * HP), PLANE * HP)
            return pl.ds(PLANE * source_z, PLANE), rows, col[2, rows]

        def flat(v):
            return v.reshape(PLANE * HP, 128)

        def arrive_one(k, w_sum):
            sources, rows, v = arrival(0, k)
            ws = flat(decode(recv[sources, 0:HP])) * v
            s_high = jnp.floor(ws * (1.0 / 256.0))
            s_low = ws - 256.0 * s_high
            x[rows, 384:512] = jnp.where(low, s_high, roll_half(s_low)).astype(BF16)
            x[rows, 512:640] = jnp.where(low, roll_half(s_high), s_low).astype(BF16)
            return w_sum + ws

        def arrive_two(k, carry):
            z_sum, w_sum = carry
            sources, rows, v = arrival(1, k)
            stage[0:PLANE, 32:ROWS] = decode(recv[sources, 32:ROWS])
            scale = jnp.exp2(stage[0:PLANE, 3 * hands : 3 * hands + 1]) * (1.0 / CODE)
            wf = flat(stage[0:PLANE, hands : hands + HP]) * v
            z = (flat(stage[0:PLANE, 2 * hands : 2 * hands + HP] * scale) * v).astype(BF16)
            f_high = jnp.floor(wf * (1.0 / 256.0))
            f_low = wf - 256.0 * f_high
            x[rows, 0:128] = z
            x[rows, 128:256] = f_high.astype(BF16)
            x[rows, 256:384] = f_low.astype(BF16)
            return (z_sum + z.astype(F32), w_sum + jnp.abs(wf))

        empty = jnp.zeros((PLANE * HP, 128), F32)
        w_sum = lax.fori_loop(0, PEERS // PLANE, arrive_one, empty)
        z_sum, w_sum = lax.fori_loop(0, PEERS // PLANE, arrive_two, (empty, w_sum))
        z_power = power_above(jnp.sum(z_sum, axis=0, keepdims=True))
        w_power = power_above(jnp.sum(w_sum, axis=0, keepdims=True) * (1.0 / unit))
        z_scale = CODE * jnp.exp2(-z_power)
        w_scale = (CODE / unit) * jnp.exp2(-w_power)
        low_part = jnp.where(low, 256.0, 1.0)

        def block(k, carry):
            i = lax.rem(z_self // 2 + far_first(k, 2), 4)
            rows = pl.ds(pl.multiple_of(i * BLOCK, BLOCK), BLOCK)
            d = jnp.dot(mat[2, rows], x[:, 0:384], preferred_element_type=F32)
            s0z = jnp.dot(mat[0, rows], x[:, 0:128], preferred_element_type=F32)
            s0w = jnp.dot(mat[0, rows], x[:, 384:512], preferred_element_type=F32)
            s1z = jnp.dot(mat[1, rows], x[:, 0:128], preferred_element_type=F32)
            s1w = jnp.dot(mat[1, rows], x[:, 512:640], preferred_element_type=F32)
            v = col[2, rows]
            s0w = s0w * low_part
            s1w = s1w * low_part
            s0w = s0w + roll_half(s0w)
            s1w = s1w + roll_half(s1w)
            act = jnp.where(low, s0w, s1w) + 256.0 * d[:, 128:256] + d[:, 256:384]
            tiles = (
                act * (v * w_scale),
                jnp.where(low, s0z, s1z) * (v * z_scale),
                d[:, 0:128] * (v * z_scale),
            )
            tiles = [nearest(jnp.minimum(jnp.maximum(t, -CODE), CODE)) for t in tiles]
            for m in range(BLOCK // HP):
                for j in range(3):
                    stage[m, j * hands : j * hands + HP] = tiles[j][m * HP : (m + 1) * HP]
                stage[m, 3 * hands : 3 * hands + 1] = w_power
                stage[m, 3 * hands + 1 : 3 * hands + 2] = z_power
                peer = i * (BLOCK // HP) + m
                out[peer] = code(stage[m, 0:ROWS])

                @pl.when(peer != leaf)
                def _():
                    out_copy(peer).start()

                @pl.when(peer == leaf)
                def _():
                    back[w_self] = out[peer]

            return carry

        lax.fori_loop(0, KP // BLOCK, block, 0)

    def first_of(k):
        pair = lax.rem(z_self // 2 - far_first(k // 2, 2) + 8, 4)
        return TRIO * (2 * pair + lax.rem(k, 2))

    def values_of(w, slot):
        stage[slot, 0:ROWS] = decode(back[w])
        w_scale = jnp.exp2(stage[slot, 3 * hands : 3 * hands + 1]) * (1.0 / CODE)
        z_scale = jnp.exp2(stage[slot, 3 * hands + 1 : 3 * hands + 2]) * (1.0 / CODE)
        act = stage[slot, 0:hands] * w_scale
        sz = stage[slot, hands : 2 * hands] * z_scale
        dz = stage[slot, 2 * hands : 3 * hands] * z_scale
        node = action_sum(kept[w, 4, 0:hands] * act, lane)
        regrets = [kept[w, b, 0:hands] for b in range(MOVES_ONE)]
        leaf_one = [show[b] * sz - fold[b] * dz for b in range(MOVES_ONE)]
        node_one = regrets[0] * leaf_one[0] + regrets[1] * leaf_one[1] + regrets[2] * leaf_one[2]
        return w, act, node, regrets, leaf_one, node_one * kept[w, 3, 0:hands]

    def collect(w):
        peer = worker_leaf(w, line)

        @pl.when(peer != leaf)
        def _():
            pltpu.make_async_remote_copy(
                src_ref=out.at[0],
                dst_ref=back.at[w],
                send_sem=out_send.at[0],
                recv_sem=out_recv.at[w],
                device_id=(line, peer),
                device_id_type=MESH,
            ).wait_recv()

    def renew(values):
        w, act, node, regrets, leaf_one, node_one = values
        r = rz[pl.ds(w, hands, stride=WORKERS)]
        new_rz[pl.ds(w, hands, stride=WORKERS)] = jnp.maximum(r + act - node, 0.0)
        new = [jnp.maximum(regrets[b] + leaf_one[b] - node_one, 0.0) for b in range(MOVES_ONE)]
        native = join_moves(new, lane)
        for v in range(3):
            new_ro[pl.ds(3 * w + v, hands, stride=3 * WORKERS)] = native[v]

    def trio_values(k, arriving):
        first = first_of(k)
        if arriving:
            for m in range(TRIO):
                collect(first + m)
        return [values_of(first + m, m) for m in range(TRIO)]

    def added(carry, trio):
        sum_zero, sum_one = carry
        for values in trio:
            sum_zero = sum_zero + values[2]
            sum_one = sum_one + values[5]
        return sum_zero, sum_one

    def update(k, carry):
        trio = trio_values(k, True)
        for values in trio:
            renew(values)
        return added(carry, trio)

    def sum_only(k, carry):
        return added(carry, trio_values(k, True))

    def finish(k, carry):
        for values in trio_values(k, False):
            renew(values)
        return carry

    zero = jnp.zeros((hands, 128), F32)
    sums = lax.fori_loop(0, EARLY, update, (zero, zero))
    sum_zero, sum_one = lax.fori_loop(EARLY, WORKERS // TRIO, sum_only, sums)
    sum_zero = jnp.where(lane % 64 < SUBGAMES, sum_zero, 0.0)
    values = [
        CHANCE
        * lax.dot_general(
            tile_selector(),
            total,
            (((1,), (1,)), ((), ())),
            precision=lax.Precision.HIGHEST,
            preferred_element_type=F32,
        )
        for total in (sum_zero, sum_one)
    ]
    own[0] = turn_share * values[0]
    own[1] = values[1]
    line_start(own, parts, root_send, root_recv)
    lax.fori_loop(EARLY, WORKERS // TRIO, finish, 0)
    stores = [
        pltpu.make_async_copy(new_rz, rz_out, store_sem.at[0]),
        pltpu.make_async_copy(new_ro, ro_out, store_sem.at[1]),
    ]
    for store in stores:
        store.start()
    total = line_sum(own, parts, root_send, root_recv)
    roots[...] = total
    new_turn[...] = jnp.maximum(turn_regret[...] + values[0] - total[0], 0.0)

    def y_sent(k, carry):
        w = forward_worker(k)
        peer = worker_leaf(w, line)

        @pl.when(peer != leaf)
        def _():
            y_copy(0, w, peer, leaf).wait_send()
            y_copy(1, w, peer, leaf).wait_send()

        return carry

    lax.fori_loop(0, WORKERS, y_sent, 0)

    @pl.when(is_worker)
    def _():
        def sent(k, carry):
            out_copy(lax.rem(leaf + k, PEERS)).wait_send()
            return carry

        lax.fori_loop(1, PEERS, sent, 0)

    line_sent(turn_regret, turns, turn_send, turn_recv)
    line_sent(own, parts, root_send, root_recv)
    for store in stores:
        store.wait()


def place_kernel(*refs):
    count = (len(refs) - 2) // 3
    srcs, dsts, held = refs[:count], refs[count : 2 * count], refs[2 * count : 3 * count]
    load_sem, store_sem = refs[-2], refs[-1]
    loads, stores = [], []
    for k in range(count):
        loads.append(pltpu.make_async_copy(srcs[k], held[k], load_sem.at[k]))
        stores.append(pltpu.make_async_copy(held[k], dsts[k], store_sem.at[k]))
        loads[k].start()
    for k in range(count):
        loads[k].wait()
        stores[k].start()
    for k in range(count):
        stores[k].wait()


VM = pl.BlockSpec(memory_space=pltpu.VMEM)
HB = pl.BlockSpec(memory_space=pl.ANY)
LIMIT = 56 << 20


def local(
    range_zero,
    range_one,
    turn_regret,
    river_regret_zero,
    river_regret_one,
    hand_cards,
    dealt_cards,
    hand_ranks,
    leaf_pots,
    leaf_kinds,
):
    hands = range_zero.shape[1]
    lines = lax.axis_size("river")
    tr = turn_regret[0]
    rz = river_regret_zero.reshape(hands * WORKERS, 128)
    ro = river_regret_one.reshape(hands * 3 * WORKERS, 128)
    dma = pltpu.SemaphoreType.DMA
    i16 = jnp.int16
    new_turn, new_rz, new_ro, roots = pl.pallas_call(
        kernel,
        out_shape=(
            jax.ShapeDtypeStruct(tr.shape, F32),
            jax.ShapeDtypeStruct(rz.shape, F32),
            jax.ShapeDtypeStruct(ro.shape, F32),
            jax.ShapeDtypeStruct((2,) + tr.shape, F32),
        ),
        in_specs=[HB] * 10,
        out_specs=(VM, HB, HB, VM),
        scratch_shapes=[
            pltpu.VMEM(tr.shape, F32),
            pltpu.VMEM(ro.shape, F32),
            pltpu.VMEM(tr.shape, F32),
            pltpu.SMEM(leaf_pots.shape, jnp.int32),
            pltpu.SMEM(leaf_kinds.shape, jnp.int32),
            pltpu.VMEM(rz.shape, F32),
            pltpu.VMEM(tr.shape, F32),
            pltpu.VMEM((2, PEERS * hands), jnp.int32),
            pltpu.VMEM(hand_ranks.shape, jnp.int32),
            pltpu.SMEM(dealt_cards.shape, jnp.int32),
            pltpu.VMEM(rz.shape, F32),
            pltpu.VMEM(ro.shape, F32),
            pltpu.VMEM((lines,) + tr.shape, F32),
            pltpu.VMEM((WORKERS, ROWS, 128), i16),
            pltpu.VMEM((PEERS, ROWS, 128), i16),
            pltpu.VMEM((WORKERS, 5, HP, 128), F32),
            pltpu.VMEM((WORKERS, ROWS, 128), F32),
            pltpu.VMEM((BLOCK // HP, STAGE, 128), F32),
            pltpu.VMEM((PEERS * hands, KP), BF16),
            pltpu.VMEM((8, PEERS * hands), F32),
            pltpu.VMEM((8, KP), F32),
            pltpu.VMEM((KP, 640), BF16),
            pltpu.VMEM((3, KP, KP), BF16),
            pltpu.VMEM((3, KP, 128), F32),
            pltpu.VMEM((KP, 128), BF16),
            pltpu.VMEM((PEERS, ROWS, 128), i16),
            pltpu.VMEM((WORKERS, ROWS, 128), i16),
            pltpu.VMEM((2,) + tr.shape, F32),
            pltpu.VMEM((lines, 2) + tr.shape, F32),
            dma((10,)),
            dma((2,)),
            dma((lines,)),
            dma((lines,)),
            dma((2, WORKERS)),
            dma((2, PEERS)),
            dma((PEERS,)),
            dma((WORKERS,)),
            dma((lines,)),
            dma((lines,)),
        ],
        compiler_params=pltpu.CompilerParams(
            collective_id=1, has_side_effects=True, vmem_limit_bytes=LIMIT
        ),
    )(
        tr,
        ro,
        range_one,
        leaf_pots,
        leaf_kinds,
        rz,
        range_zero,
        hand_cards.T,
        hand_ranks,
        dealt_cards,
    )
    results = (new_turn, new_rz, new_ro, roots)
    new_turn, new_rz, new_ro, roots = pl.pallas_call(
        place_kernel,
        out_shape=tuple(jax.ShapeDtypeStruct(r.shape, F32) for r in results),
        in_specs=[HB] * 4,
        out_specs=(HB,) * 4,
        scratch_shapes=[pltpu.VMEM(r.shape, F32) for r in results] + [dma((4,)), dma((4,))],
    )(*results)
    return (
        new_turn[None],
        new_rz.reshape(river_regret_zero.shape),
        new_ro.reshape(river_regret_one.shape),
        roots,
    )


def solution(mesh):
    placed = (
        P(None, "leaf"),
        P(None, "leaf"),
        P("river", None, "leaf"),
        P("river", "leaf", None),
        P("river", "leaf", None),
        P(),
        P(),
        P(),
        P("river", None),
        P("river", None),
    )
    return jax.shard_map(
        local,
        mesh=mesh,
        in_specs=placed,
        out_specs=(
            P("river", None, "leaf"),
            P("river", "leaf", None),
            P("river", "leaf", None),
            P(None, None, "leaf"),
        ),
        check_vma=False,
    )
```

```python
import jax
import jax.numpy as jnp
from jax import lax
from jax.experimental import pallas as pl
from jax.experimental.pallas import tpu as pltpu
from jax.sharding import PartitionSpec as P

MESH = pl.DeviceIdType.MESH
F32 = jnp.float32
BF16 = jnp.bfloat16
RIVERS = 48
MOVES_ZERO = 4
MOVES_ONE = 3
SUBGAMES = 16
WORKERS = 24
PEERS = 32
HP = 48
KP = PEERS * HP
MB = 384
BLOCK = 384
CHANCE = 1.0 / 44.0


def worker_leaf(w, line):
    z = w // 3
    x = lax.rem(w - 3 * z + 1 + z + 2 * lax.rem(line, 2), 4)
    return 4 * z + x


def leaf_worker(leaf, line):
    z = leaf // 4
    x = leaf - 4 * z
    k = lax.rem(x - 1 - z - 2 * lax.rem(line, 2) + 16, 4)
    return k, 3 * z + k


def far_first(k, half):
    h = (k + 1) // 2
    return half + h * (1 - 2 * lax.rem(k, 2))


def lanes(rows):
    return lax.broadcasted_iota(jnp.int32, (rows, 128), 1)


def gather_lanes(x, index):
    return jnp.take_along_axis(x, index, axis=1, mode="promise_in_bounds")


def roll_half(x):
    return pltpu.roll(x, 64, 1)


def action_sum(x, lane):
    x = x + gather_lanes(x, (lane & 64) | ((lane + 16) & 63))
    return x + gather_lanes(x, (lane & 64) | ((lane + 32) & 63))


def split_moves(tiles, lane):
    slot, sub = lane // 16, lane % 16
    out = []
    for b in range(MOVES_ONE):
        group = (3 * (slot - b + 8)) % 8
        tile = (3 * group + b) // 8
        picked = jnp.where(tile == 0, tiles[0], jnp.where(tile == 1, tiles[1], tiles[2]))
        out.append(gather_lanes(picked, ((3 * slot + b) % 8) * 16 + sub))
    return out


def join_moves(parts, lane):
    slot, sub = lane // 16, lane % 16
    moved = []
    for b in range(MOVES_ONE):
        group = (3 * (slot - b + 8)) % 8
        moved.append(gather_lanes(parts[b], group * 16 + sub))
    out = []
    for v in range(3):
        b = (8 * v + slot) % 3
        out.append(jnp.where(b == 0, moved[0], jnp.where(b == 1, moved[1], moved[2])))
    return out


def tile_selector():
    sub = lax.broadcasted_iota(jnp.int32, (SUBGAMES, 128), 0)
    lane = lanes(SUBGAMES)
    return (lane % SUBGAMES == sub).astype(F32)


def to_lanes(x):
    return lax.dot_general(
        x,
        tile_selector(),
        (((0,), (0,)), ((), ())),
        precision=lax.Precision.HIGHEST,
        preferred_element_type=F32,
    )


def leaf_scales(pots, kinds, rows):
    action = (lanes(rows) // SUBGAMES) % MOVES_ZERO
    show, fold = [], []
    for b in range(MOVES_ONE):
        s = jnp.zeros((rows, 128), F32)
        f = jnp.zeros((rows, 128), F32)
        for a in range(MOVES_ZERO):
            pot = pots[0, a * MOVES_ONE + b].astype(F32)
            kind = kinds[0, a * MOVES_ONE + b]
            here = action == a
            s = jnp.where(here, jnp.where(kind == 0, pot, 0.0), s)
            f = jnp.where(here, jnp.where(kind == 0, 0.0, jnp.where(kind == 1, pot, -pot)), f)
        show.append(s)
        fold.append(f)
    return show, fold


ONE_TOP = 64.0 * 0.001 * 1.005
CODE = 32760.0
ROWS = 128
STAGE = 136
SPLIT = 80
EARLY = 5
PLANE = 4
TRIO = 3
PIECES = 3


def column(rows, select):
    return lax.dot_general(
        rows, select, (((0,), (0,)), ((), ())), preferred_element_type=F32
    )


def code(x):
    return x.astype(jnp.int32).astype(jnp.int16)


def decode(x):
    return x.astype(jnp.int32).astype(F32)


def nearest(x):
    return jnp.floor(x + 0.5)


def power_above(x):
    return jnp.floor(jnp.log2(jnp.maximum(x, 1e-30))) + 1.0


def zero_shares(rz, w, lane, hands):
    x = rz[pl.ds(w, hands, stride=WORKERS)]
    return x, x / action_sum(x, lane)


def one_regrets(ro, w, lane, hands):
    tiles = [ro[pl.ds(3 * w + v, hands, stride=3 * WORKERS)] for v in range(3)]
    regrets = split_moves(tiles, lane)
    return regrets, 1.0 / (regrets[0] + regrets[1] + regrets[2])


def kernel(
    turn_hbm,
    ro_hbm,
    range_one_hbm,
    pots_hbm,
    kinds_hbm,
    rz_hbm,
    range_zero_hbm,
    cards_hbm,
    ranks_hbm,
    dealt_hbm,
    new_turn,
    rz_out,
    ro_out,
    roots,
    turn_regret,
    ro,
    range_one,
    pots,
    kinds,
    rz,
    range_zero,
    cards,
    all_ranks,
    dealt,
    new_rz,
    new_ro,
    turns,
    yq,
    recv,
    kept,
    y_stage,
    stage,
    spread,
    card_pad,
    rank_row,
    x,
    mat,
    col,
    inc,
    out,
    back,
    own,
    parts,
    load_sem,
    store_sem,
    turn_send,
    turn_recv,
    y_send,
    y_recv,
    out_send,
    out_recv,
    root_send,
    root_recv,
):
    line, leaf = lax.axis_index("river"), lax.axis_index("leaf")
    lines = turns.shape[0]
    k_self, w_self = leaf_worker(leaf, line)
    is_worker = k_self < 3
    hands = turn_regret.shape[1]
    z_self = leaf // 4
    x_self = leaf - 4 * z_self

    def forward_worker(k):
        step = far_first(k // 3, 4)
        return 3 * lax.rem(z_self + step, 8) + lax.rem(k + x_self, 3)

    sources = (
        turn_hbm,
        ro_hbm,
        range_one_hbm,
        pots_hbm,
        kinds_hbm,
        rz_hbm,
        range_zero_hbm,
        cards_hbm,
        ranks_hbm,
        dealt_hbm,
    )
    places = (turn_regret, ro, range_one, pots, kinds, rz, range_zero, cards, all_ranks, dealt)
    loads = [
        pltpu.make_async_copy(a, b, load_sem.at[k]) for k, (a, b) in enumerate(zip(sources, places))
    ]

    barrier = pltpu.get_barrier_semaphore()

    for load in loads[:2]:
        load.start()
    for k in range(1, lines):
        peer = lax.rem(line + k, lines)
        pl.semaphore_signal(barrier, inc=1, device_id=(peer, leaf), device_id_type=MESH)
    for k in range(1, PEERS):
        peer = lax.rem(leaf + k, PEERS)
        pl.semaphore_signal(barrier, inc=1, device_id=(line, peer), device_id_type=MESH)
    for load in loads[2:]:
        load.start()
    for load in loads:
        load.wait()

    lane = lanes(hands)
    weight_one = to_lanes(range_one[...])
    show, fold = leaf_scales(pots, kinds, 8)
    show = [s[0:1] for s in show]
    fold = [f[0:1] for f in fold]
    unit = CODE / ONE_TOP
    stage[...] = jnp.zeros_like(stage)
    y_stage[:, 120:ROWS] = jnp.zeros((WORKERS, ROWS - 120, 128), F32)
    pl.semaphore_wait(barrier, PEERS - 1 + lines - 1)

    def line_copy(src, dst, sends, recvs, peer, slot):
        return pltpu.make_async_remote_copy(
            src_ref=src,
            dst_ref=dst.at[slot],
            send_sem=sends.at[peer],
            recv_sem=recvs.at[slot],
            device_id=(peer, leaf),
            device_id_type=MESH,
        )

    def line_start(src, dst, sends, recvs):
        def start(k, carry):
            line_copy(src, dst, sends, recvs, lax.rem(line + k, lines), line).start()
            return carry

        lax.fori_loop(1, lines, start, 0)

    def line_sum(src, dst, sends, recvs):
        dst[line] = src[...]

        def wait(k, carry):
            peer = lax.rem(line + k, lines)
            line_copy(src, dst, sends, recvs, peer, peer).wait_recv()
            return carry

        lax.fori_loop(1, lines, wait, 0)
        total = dst[0]
        for t in range(1, lines):
            total = total + dst[t]
        return total

    def line_sent(src, dst, sends, recvs):
        def wait(k, carry):
            line_copy(src, dst, sends, recvs, lax.rem(line + k, lines), line).wait_send()
            return carry

        lax.fori_loop(1, lines, wait, 0)

    line_start(turn_regret, turns, turn_send, turn_recv)

    def y_copy(part, w, peer, slot):
        rows = (pl.ds(0, SPLIT), pl.ds(SPLIT, ROWS - SPLIT))[part]
        return pltpu.make_async_remote_copy(
            src_ref=yq.at[w, rows],
            dst_ref=recv.at[slot, rows],
            send_sem=y_send.at[part, w],
            recv_sem=y_recv.at[part, slot],
            device_id=(line, peer),
            device_id_type=MESH,
        )

    def hand_over(part, w):
        peer = worker_leaf(w, line)
        rows = (pl.ds(0, SPLIT), pl.ds(SPLIT, ROWS - SPLIT))[part]
        yq[w, rows] = code(y_stage[w, rows])

        @pl.when(peer != leaf)
        def _():
            y_copy(part, w, peer, leaf).start()

        @pl.when(peer == leaf)
        def _():
            recv[leaf, rows] = yq[w, rows]

    def prepare_one(k, carry):
        workers = [forward_worker(TRIO * k + m) for m in range(TRIO)]
        for w in workers:
            regrets, scale = one_regrets(ro, w, lane, hands)
            for b in range(MOVES_ONE):
                kept[w, b, 0:hands] = regrets[b]
            kept[w, 3, 0:hands] = scale
            o = [(weight_one * (r * scale)).astype(BF16).astype(F32) for r in regrets]
            for j, pot in enumerate((show, fold)):
                mixed = o[0] * pot[0] + o[1] * pot[1] + o[2] * pot[2]
                y_stage[w, j * hands : (j + 1) * hands] = nearest(mixed * unit)
        for w in workers:
            hand_over(0, w)
        return carry

    lax.fori_loop(0, WORKERS // TRIO, prepare_one, 0)
    turn_share = turn_regret[...] / line_sum(turn_regret, turns, turn_send, turn_recv)
    weight_zero = to_lanes(range_zero[...] * turn_share)

    def prepare_zero(k, carry):
        workers = [forward_worker(TRIO * k + m) for m in range(TRIO)]
        for w in workers:
            _, zs = zero_shares(rz, w, lane, hands)
            kept[w, 4, 0:hands] = zs
            z = (weight_zero * zs).astype(BF16).astype(F32)
            power = power_above(jnp.max(z, axis=0, keepdims=True))
            y_stage[w, 2 * hands : 3 * hands] = nearest(z * (CODE * jnp.exp2(-power)))
            y_stage[w, 3 * hands : 3 * hands + 1] = power
        for w in workers:
            hand_over(1, w)
        return carry

    lax.fori_loop(0, WORKERS // TRIO, prepare_zero, 0)

    def out_copy(peer):
        return pltpu.make_async_remote_copy(
            src_ref=out.at[peer],
            dst_ref=back.at[w_self],
            send_sem=out_send.at[peer],
            recv_sem=out_recv.at[w_self],
            device_id=(line, peer),
            device_id_type=MESH,
        )

    @pl.when(is_worker)
    def _():
        low = lanes(8)[0:1] < 64
        source_hand = lax.broadcasted_iota(jnp.int32, (PEERS * hands, 128), 0)
        place = source_hand + (HP - hands) * (source_hand // hands)
        for j in range(KP // 128):
            here = lanes(PEERS * hands) + 128 * j
            spread[:, pl.ds(128 * j, 128)] = (place == here).astype(F32).astype(BF16)
        card_pad[...] = jnp.zeros_like(card_pad)
        card_pad[0:2] = (cards[...] + 1).astype(F32)
        eight = pl.ds(pl.multiple_of(8 * (w_self // 4), 8), 8)
        ranks = all_ranks[eight].astype(F32)
        high = jnp.floor(ranks * (1.0 / 64.0))
        rest = ranks - 64.0 * high

        def spread_rows(v):
            return jnp.dot(v.astype(BF16), spread[...], preferred_element_type=F32)

        card_rows = spread_rows(card_pad[...]).astype(BF16)
        high_rows = spread_rows(high)
        rest_rows = spread_rows(rest)
        one_row = lax.broadcasted_iota(jnp.int32, (8, 128), 0)
        pick = lambda r, scale: jnp.where(one_row == r, scale, 0.0).astype(BF16)
        first = column(card_rows, pick(0, 1.0)) - 1.0
        second = column(card_rows, pick(1, 1.0)) - 1.0
        usable = (first < 52.0) & (second < 52.0) & (first >= 0.0)
        for k in range(4):
            board = dealt[k].astype(F32)
            usable = usable & (first != board) & (second != board)
        rivers = [dealt[4 + 2 * w_self + c].astype(F32) for c in range(2)]
        river = jnp.where(low, rivers[0], rivers[1])
        col[2] = (usable & (first != river) & (second != river)).astype(F32)
        card = lanes(KP).astype(F32)
        inc[...] = ((first == card) | (second == card)).astype(F32).astype(BF16)
        rank_rows = 64.0 * high_rows + rest_rows
        wide_row = lax.broadcasted_iota(jnp.int32, (8, KP), 0)
        for c in range(2):
            r = 2 * lax.rem(w_self, 4) + c
            rank_row[c : c + 1] = jnp.sum(
                jnp.where(wide_row == r, rank_rows, 0.0), axis=0, keepdims=True
            )
            col[c] = column(high_rows.astype(BF16), pick(r, 64.0)) + column(
                rest_rows.astype(BF16), pick(r, 1.0)
            )

        def build(i, carry):
            rows = pl.ds(pl.multiple_of(i * MB, MB), MB)
            for j in range(KP // 128):
                js = pl.ds(128 * j, 128)
                shared = lax.dot_general(
                    inc[rows], inc[js], (((1,), (1,)), ((), ())), preferred_element_type=F32
                )
                apart = jnp.maximum(1.0 - shared, 0.0)
                mat[2, rows, js] = apart.astype(BF16)
                for c in range(2):
                    gap = col[c, rows] - rank_row[c : c + 1, js]
                    sign = jnp.minimum(jnp.maximum(gap, -1.0), 1.0)
                    mat[c, rows, js] = (sign * apart).astype(BF16)
            return carry

        lax.fori_loop(0, KP // MB, build, 0)

        def arrival(part, k):
            source_z = lax.rem(z_self - far_first(k, 4) + 16, 8)
            for m in range(PLANE):
                source = PLANE * source_z + m

                @pl.when(source != leaf)
                def _():
                    y_copy(part, 0, source, source).wait_recv()

            rows = pl.ds(pl.multiple_of(source_z * (PLANE * HP), PLANE * HP), PLANE * HP)
            return pl.ds(PLANE * source_z, PLANE), rows, col[2, rows]

        def flat(v):
            return v.reshape(PLANE * HP, 128)

        def arrive_one(k, w_sum):
            sources, rows, v = arrival(0, k)
            ws = flat(decode(recv[sources, 0:HP])) * v
            s_high = jnp.floor(ws * (1.0 / 256.0))
            s_low = ws - 256.0 * s_high
            x[rows, 384:512] = jnp.where(low, s_high, roll_half(s_low)).astype(BF16)
            x[rows, 640:768] = jnp.where(low, roll_half(s_high), s_low).astype(BF16)
            return w_sum + ws

        def arrive_two(k, carry):
            z_sum, w_sum = carry
            sources, rows, v = arrival(1, k)
            stage[0:PLANE, 32:ROWS] = decode(recv[sources, 32:ROWS])
            scale = jnp.exp2(stage[0:PLANE, 3 * hands : 3 * hands + 1]) * (1.0 / CODE)
            wf = flat(stage[0:PLANE, hands : hands + HP]) * v
            z = (flat(stage[0:PLANE, 2 * hands : 2 * hands + HP] * scale) * v).astype(BF16)
            f_high = jnp.floor(wf * (1.0 / 256.0))
            f_low = wf - 256.0 * f_high
            x[rows, 0:128] = f_high.astype(BF16)
            x[rows, 128:256] = f_low.astype(BF16)
            x[rows, 256:384] = z
            x[rows, 512:640] = z
            return (z_sum + z.astype(F32), w_sum + jnp.abs(wf))

        empty = jnp.zeros((PLANE * HP, 128), F32)
        w_sum = lax.fori_loop(0, PEERS // PLANE, arrive_one, empty)
        z_sum, w_sum = lax.fori_loop(0, PEERS // PLANE, arrive_two, (empty, w_sum))
        z_power = power_above(jnp.sum(z_sum, axis=0, keepdims=True))
        w_power = power_above(jnp.sum(w_sum, axis=0, keepdims=True) * (1.0 / unit))
        z_scale = CODE * jnp.exp2(-z_power)
        w_scale = (CODE / unit) * jnp.exp2(-w_power)
        low_part = jnp.where(low, 256.0, 1.0)

        def block(k, carry):
            i = lax.rem(z_self // 2 + far_first(k, 2), 4)
            rows = pl.ds(pl.multiple_of(i * BLOCK, BLOCK), BLOCK)
            d = jnp.dot(mat[2, rows], x[:, 0:384], preferred_element_type=F32)
            s0 = jnp.dot(mat[0, rows], x[:, 256:512], preferred_element_type=F32)
            s1 = jnp.dot(mat[1, rows], x[:, 512:768], preferred_element_type=F32)
            s0z, s0w = s0[:, 0:128], s0[:, 128:256]
            s1z, s1w = s1[:, 0:128], s1[:, 128:256]
            v = col[2, rows]
            s0w = s0w * low_part
            s1w = s1w * low_part
            s0w = s0w + roll_half(s0w)
            s1w = s1w + roll_half(s1w)
            act = jnp.where(low, s0w, s1w) + 256.0 * d[:, 0:128] + d[:, 128:256]
            tiles = (
                act * (v * w_scale),
                jnp.where(low, s0z, s1z) * (v * z_scale),
                d[:, 256:384] * (v * z_scale),
            )
            tiles = [nearest(jnp.minimum(jnp.maximum(t, -CODE), CODE)) for t in tiles]
            for m in range(BLOCK // HP):
                for j in range(3):
                    stage[m, j * hands : j * hands + HP] = tiles[j][m * HP : (m + 1) * HP]
                stage[m, 3 * hands : 3 * hands + 1] = w_power
                stage[m, 3 * hands + 1 : 3 * hands + 2] = z_power
                peer = i * (BLOCK // HP) + m
                out[peer] = code(stage[m, 0:ROWS])

                @pl.when(peer != leaf)
                def _():
                    out_copy(peer).start()

                @pl.when(peer == leaf)
                def _():
                    back[w_self] = out[peer]

            return carry

        lax.fori_loop(0, KP // BLOCK, block, 0)

    def first_of(k):
        pair = lax.rem(z_self // 2 - far_first(k // 2, 2) + 8, 4)
        return TRIO * (2 * pair + lax.rem(k, 2))

    def values_of(w, slot):
        stage[slot, 0:ROWS] = decode(back[w])
        w_scale = jnp.exp2(stage[slot, 3 * hands : 3 * hands + 1]) * (1.0 / CODE)
        z_scale = jnp.exp2(stage[slot, 3 * hands + 1 : 3 * hands + 2]) * (1.0 / CODE)
        act = stage[slot, 0:hands] * w_scale
        sz = stage[slot, hands : 2 * hands] * z_scale
        dz = stage[slot, 2 * hands : 3 * hands] * z_scale
        node = action_sum(kept[w, 4, 0:hands] * act, lane)
        regrets = [kept[w, b, 0:hands] for b in range(MOVES_ONE)]
        leaf_one = [show[b] * sz - fold[b] * dz for b in range(MOVES_ONE)]
        node_one = regrets[0] * leaf_one[0] + regrets[1] * leaf_one[1] + regrets[2] * leaf_one[2]
        return w, act, node, regrets, leaf_one, node_one * kept[w, 3, 0:hands]

    def collect(w):
        peer = worker_leaf(w, line)

        @pl.when(peer != leaf)
        def _():
            pltpu.make_async_remote_copy(
                src_ref=out.at[0],
                dst_ref=back.at[w],
                send_sem=out_send.at[0],
                recv_sem=out_recv.at[w],
                device_id=(line, peer),
                device_id_type=MESH,
            ).wait_recv()

    def renew(values):
        w, act, node, regrets, leaf_one, node_one = values
        r = rz[pl.ds(w, hands, stride=WORKERS)]
        new_rz[pl.ds(w, hands, stride=WORKERS)] = jnp.maximum(r + act - node, 0.0)
        new = [jnp.maximum(regrets[b] + leaf_one[b] - node_one, 0.0) for b in range(MOVES_ONE)]
        native = join_moves(new, lane)
        for v in range(3):
            new_ro[pl.ds(3 * w + v, hands, stride=3 * WORKERS)] = native[v]

    def trio_values(k, arriving):
        first = first_of(k)
        if arriving:
            for m in range(TRIO):
                collect(first + m)
        return [values_of(first + m, m) for m in range(TRIO)]

    def added(carry, trio):
        sum_zero, sum_one = carry
        for values in trio:
            sum_zero = sum_zero + values[2]
            sum_one = sum_one + values[5]
        return sum_zero, sum_one

    def update(k, carry):
        trio = trio_values(k, True)
        for values in trio:
            renew(values)
        return added(carry, trio)

    def sum_only(k, carry):
        return added(carry, trio_values(k, True))

    def finish(k, carry):
        for values in trio_values(k, False):
            renew(values)
        return carry

    zero = jnp.zeros((hands, 128), F32)
    sums = lax.fori_loop(0, EARLY, update, (zero, zero))
    sum_zero, sum_one = lax.fori_loop(EARLY, WORKERS // TRIO, sum_only, sums)
    sum_zero = jnp.where(lane % 64 < SUBGAMES, sum_zero, 0.0)
    values = [
        CHANCE
        * lax.dot_general(
            tile_selector(),
            total,
            (((1,), (1,)), ((), ())),
            precision=lax.Precision.HIGHEST,
            preferred_element_type=F32,
        )
        for total in (sum_zero, sum_one)
    ]
    own[0] = turn_share * values[0]
    own[1] = values[1]
    line_start(own, parts, root_send, root_recv)
    lax.fori_loop(EARLY, WORKERS // TRIO, finish, 0)
    stores = [
        pltpu.make_async_copy(new_rz, rz_out, store_sem.at[0]),
        pltpu.make_async_copy(new_ro, ro_out, store_sem.at[1]),
    ]
    for store in stores:
        store.start()
    total = line_sum(own, parts, root_send, root_recv)
    roots[...] = total
    new_turn[...] = jnp.maximum(turn_regret[...] + values[0] - total[0], 0.0)

    def y_sent(k, carry):
        w = forward_worker(k)
        peer = worker_leaf(w, line)

        @pl.when(peer != leaf)
        def _():
            y_copy(0, w, peer, leaf).wait_send()
            y_copy(1, w, peer, leaf).wait_send()

        return carry

    lax.fori_loop(0, WORKERS, y_sent, 0)

    @pl.when(is_worker)
    def _():
        def sent(k, carry):
            out_copy(lax.rem(leaf + k, PEERS)).wait_send()
            return carry

        lax.fori_loop(1, PEERS, sent, 0)

    line_sent(turn_regret, turns, turn_send, turn_recv)
    line_sent(own, parts, root_send, root_recv)
    for store in stores:
        store.wait()


def place_kernel(*refs):
    count = (len(refs) - 2) // 3
    srcs, dsts, held = refs[:count], refs[count : 2 * count], refs[2 * count : 3 * count]
    load_sem, store_sem = refs[-2], refs[-1]
    pieces = []
    for k in range(count):
        rows = srcs[k].shape[0]
        parts = PIECES if rows % (8 * PIECES) == 0 else 1
        for m in range(parts):
            piece = pl.ds(m * (rows // parts), rows // parts)
            pieces.append((srcs[k].at[piece], held[k].at[piece], dsts[k].at[piece]))
    loads = [pltpu.make_async_copy(p[0], p[1], load_sem.at[n]) for n, p in enumerate(pieces)]
    stores = [pltpu.make_async_copy(p[1], p[2], store_sem.at[n]) for n, p in enumerate(pieces)]
    for load in loads:
        load.start()
    for load, store in zip(loads, stores):
        load.wait()
        store.start()
    for store in stores:
        store.wait()


VM = pl.BlockSpec(memory_space=pltpu.VMEM)
HB = pl.BlockSpec(memory_space=pl.ANY)
LIMIT = 56 << 20


def local(
    range_zero,
    range_one,
    turn_regret,
    river_regret_zero,
    river_regret_one,
    hand_cards,
    dealt_cards,
    hand_ranks,
    leaf_pots,
    leaf_kinds,
):
    hands = range_zero.shape[1]
    lines = lax.axis_size("river")
    tr = turn_regret[0]
    rz = river_regret_zero.reshape(hands * WORKERS, 128)
    ro = river_regret_one.reshape(hands * 3 * WORKERS, 128)
    dma = pltpu.SemaphoreType.DMA
    i16 = jnp.int16
    new_turn, new_rz, new_ro, roots = pl.pallas_call(
        kernel,
        out_shape=(
            jax.ShapeDtypeStruct(tr.shape, F32),
            jax.ShapeDtypeStruct(rz.shape, F32),
            jax.ShapeDtypeStruct(ro.shape, F32),
            jax.ShapeDtypeStruct((2,) + tr.shape, F32),
        ),
        in_specs=[HB] * 10,
        out_specs=(VM, HB, HB, VM),
        scratch_shapes=[
            pltpu.VMEM(tr.shape, F32),
            pltpu.VMEM(ro.shape, F32),
            pltpu.VMEM(tr.shape, F32),
            pltpu.SMEM(leaf_pots.shape, jnp.int32),
            pltpu.SMEM(leaf_kinds.shape, jnp.int32),
            pltpu.VMEM(rz.shape, F32),
            pltpu.VMEM(tr.shape, F32),
            pltpu.VMEM((2, PEERS * hands), jnp.int32),
            pltpu.VMEM(hand_ranks.shape, jnp.int32),
            pltpu.SMEM(dealt_cards.shape, jnp.int32),
            pltpu.VMEM(rz.shape, F32),
            pltpu.VMEM(ro.shape, F32),
            pltpu.VMEM((lines,) + tr.shape, F32),
            pltpu.VMEM((WORKERS, ROWS, 128), i16),
            pltpu.VMEM((PEERS, ROWS, 128), i16),
            pltpu.VMEM((WORKERS, 5, HP, 128), F32),
            pltpu.VMEM((WORKERS, ROWS, 128), F32),
            pltpu.VMEM((BLOCK // HP, STAGE, 128), F32),
            pltpu.VMEM((PEERS * hands, KP), BF16),
            pltpu.VMEM((8, PEERS * hands), F32),
            pltpu.VMEM((8, KP), F32),
            pltpu.VMEM((KP, 768), BF16),
            pltpu.VMEM((3, KP, KP), BF16),
            pltpu.VMEM((3, KP, 128), F32),
            pltpu.VMEM((KP, 128), BF16),
            pltpu.VMEM((PEERS, ROWS, 128), i16),
            pltpu.VMEM((WORKERS, ROWS, 128), i16),
            pltpu.VMEM((2,) + tr.shape, F32),
            pltpu.VMEM((lines, 2) + tr.shape, F32),
            dma((10,)),
            dma((2,)),
            dma((lines,)),
            dma((lines,)),
            dma((2, WORKERS)),
            dma((2, PEERS)),
            dma((PEERS,)),
            dma((WORKERS,)),
            dma((lines,)),
            dma((lines,)),
        ],
        compiler_params=pltpu.CompilerParams(
            collective_id=1, has_side_effects=True, vmem_limit_bytes=LIMIT
        ),
    )(
        tr,
        ro,
        range_one,
        leaf_pots,
        leaf_kinds,
        rz,
        range_zero,
        hand_cards.T,
        hand_ranks,
        dealt_cards,
    )
    results = (new_turn, new_rz, new_ro, roots)
    new_turn, new_rz, new_ro, roots = pl.pallas_call(
        place_kernel,
        out_shape=tuple(jax.ShapeDtypeStruct(r.shape, F32) for r in results),
        in_specs=[HB] * 4,
        out_specs=(HB,) * 4,
        scratch_shapes=[pltpu.VMEM(r.shape, F32) for r in results] + [dma((4 * PIECES,)), dma((4 * PIECES,))],
    )(*results)
    return (
        new_turn[None],
        new_rz.reshape(river_regret_zero.shape),
        new_ro.reshape(river_regret_one.shape),
        roots,
    )


def solution(mesh):
    placed = (
        P(None, "leaf"),
        P(None, "leaf"),
        P("river", None, "leaf"),
        P("river", "leaf", None),
        P("river", "leaf", None),
        P(),
        P(),
        P(),
        P("river", None),
        P("river", None),
    )
    return jax.shard_map(
        local,
        mesh=mesh,
        in_specs=placed,
        out_specs=(
            P("river", None, "leaf"),
            P("river", "leaf", None),
            P("river", "leaf", None),
            P(None, None, "leaf"),
        ),
        check_vma=False,
    )
```

```python
import jax
import jax.numpy as jnp
from jax import lax
from jax.experimental import pallas as pl
from jax.experimental.pallas import tpu as pltpu
from jax.sharding import PartitionSpec as P

MESH = pl.DeviceIdType.MESH
F32 = jnp.float32
BF16 = jnp.bfloat16
RIVERS = 48
MOVES_ZERO = 4
MOVES_ONE = 3
SUBGAMES = 16
WORKERS = 24
PEERS = 32
HP = 48
KP = PEERS * HP
MB = 384
BLOCK = 384
CHANCE = 1.0 / 44.0


def worker_leaf(w, line):
    z = w // 3
    x = lax.rem(w - 3 * z + 1 + z + 2 * lax.rem(line, 2), 4)
    return 4 * z + x


def leaf_worker(leaf, line):
    z = leaf // 4
    x = leaf - 4 * z
    k = lax.rem(x - 1 - z - 2 * lax.rem(line, 2) + 16, 4)
    return k, 3 * z + k


def far_first(k, half):
    h = (k + 1) // 2
    return half + h * (1 - 2 * lax.rem(k, 2))


def lanes(rows):
    return lax.broadcasted_iota(jnp.int32, (rows, 128), 1)


def gather_lanes(x, index):
    return jnp.take_along_axis(x, index, axis=1, mode="promise_in_bounds")


def roll_half(x):
    return pltpu.roll(x, 64, 1)


def action_sum(x, lane):
    x = x + gather_lanes(x, (lane & 64) | ((lane + 16) & 63))
    return x + gather_lanes(x, (lane & 64) | ((lane + 32) & 63))


def split_moves(tiles, lane):
    slot, sub = lane // 16, lane % 16
    out = []
    for b in range(MOVES_ONE):
        group = (3 * (slot - b + 8)) % 8
        tile = (3 * group + b) // 8
        picked = jnp.where(tile == 0, tiles[0], jnp.where(tile == 1, tiles[1], tiles[2]))
        out.append(gather_lanes(picked, ((3 * slot + b) % 8) * 16 + sub))
    return out


def join_moves(parts, lane):
    slot, sub = lane // 16, lane % 16
    moved = []
    for b in range(MOVES_ONE):
        group = (3 * (slot - b + 8)) % 8
        moved.append(gather_lanes(parts[b], group * 16 + sub))
    out = []
    for v in range(3):
        b = (8 * v + slot) % 3
        out.append(jnp.where(b == 0, moved[0], jnp.where(b == 1, moved[1], moved[2])))
    return out


def tile_selector():
    sub = lax.broadcasted_iota(jnp.int32, (SUBGAMES, 128), 0)
    lane = lanes(SUBGAMES)
    return (lane % SUBGAMES == sub).astype(F32)


def to_lanes(x):
    return lax.dot_general(
        x,
        tile_selector(),
        (((0,), (0,)), ((), ())),
        precision=lax.Precision.HIGHEST,
        preferred_element_type=F32,
    )


def leaf_scales(pots, kinds, rows):
    action = (lanes(rows) // SUBGAMES) % MOVES_ZERO
    show, fold = [], []
    for b in range(MOVES_ONE):
        s = jnp.zeros((rows, 128), F32)
        f = jnp.zeros((rows, 128), F32)
        for a in range(MOVES_ZERO):
            pot = pots[0, a * MOVES_ONE + b].astype(F32)
            kind = kinds[0, a * MOVES_ONE + b]
            here = action == a
            s = jnp.where(here, jnp.where(kind == 0, pot, 0.0), s)
            f = jnp.where(here, jnp.where(kind == 0, 0.0, jnp.where(kind == 1, pot, -pot)), f)
        show.append(s)
        fold.append(f)
    return show, fold


ONE_TOP = 64.0 * 0.001 * 1.005
CODE = 32760.0
ROWS = 128
STAGE = 136
SPLIT = 80
EARLY = 4
PLANE = 4
TRIO = 3
PIECES = 3


def column(rows, select):
    return lax.dot_general(
        rows, select, (((0,), (0,)), ((), ())), preferred_element_type=F32
    )


def code(x):
    return x.astype(jnp.int32).astype(jnp.int16)


def decode(x):
    return x.astype(jnp.int32).astype(F32)


def nearest(x):
    return jnp.floor(x + 0.5)


def power_above(x):
    return jnp.floor(jnp.log2(jnp.maximum(x, 1e-30))) + 1.0


def zero_shares(rz, w, lane, hands):
    x = rz[pl.ds(w, hands, stride=WORKERS)]
    return x, x / action_sum(x, lane)


def one_regrets(ro, w, lane, hands):
    tiles = [ro[pl.ds(3 * w + v, hands, stride=3 * WORKERS)] for v in range(3)]
    regrets = split_moves(tiles, lane)
    return regrets, 1.0 / (regrets[0] + regrets[1] + regrets[2])


def kernel(
    turn_hbm,
    ro_hbm,
    range_one_hbm,
    pots_hbm,
    kinds_hbm,
    rz_hbm,
    range_zero_hbm,
    cards_hbm,
    ranks_hbm,
    dealt_hbm,
    new_turn,
    rz_out,
    ro_out,
    roots,
    turn_regret,
    ro,
    range_one,
    pots,
    kinds,
    rz,
    range_zero,
    cards,
    all_ranks,
    dealt,
    new_rz,
    new_ro,
    turns,
    yq,
    recv,
    kept,
    y_stage,
    stage,
    spread,
    card_pad,
    rank_row,
    x,
    mat,
    col,
    inc,
    out,
    back,
    own,
    parts,
    load_sem,
    store_sem,
    turn_send,
    turn_recv,
    y_send,
    y_recv,
    out_send,
    out_recv,
    root_send,
    root_recv,
):
    line, leaf = lax.axis_index("river"), lax.axis_index("leaf")
    lines = turns.shape[0]
    k_self, w_self = leaf_worker(leaf, line)
    is_worker = k_self < 3
    hands = turn_regret.shape[1]
    z_self = leaf // 4
    x_self = leaf - 4 * z_self

    def forward_worker(k):
        step = far_first(k // 3, 4)
        return 3 * lax.rem(z_self + step, 8) + lax.rem(k + x_self, 3)

    sources = (
        turn_hbm,
        ro_hbm,
        range_one_hbm,
        pots_hbm,
        kinds_hbm,
        rz_hbm,
        range_zero_hbm,
        cards_hbm,
        ranks_hbm,
        dealt_hbm,
    )
    places = (turn_regret, ro, range_one, pots, kinds, rz, range_zero, cards, all_ranks, dealt)
    loads = [
        pltpu.make_async_copy(a, b, load_sem.at[k]) for k, (a, b) in enumerate(zip(sources, places))
    ]

    barrier = pltpu.get_barrier_semaphore()

    for load in loads[:2]:
        load.start()
    for k in range(1, lines):
        peer = lax.rem(line + k, lines)
        pl.semaphore_signal(barrier, inc=1, device_id=(peer, leaf), device_id_type=MESH)
    for k in range(1, PEERS):
        peer = lax.rem(leaf + k, PEERS)
        pl.semaphore_signal(barrier, inc=1, device_id=(line, peer), device_id_type=MESH)
    for load in loads[2:]:
        load.start()
    for load in loads:
        load.wait()

    lane = lanes(hands)
    weight_one = to_lanes(range_one[...])
    show, fold = leaf_scales(pots, kinds, 8)
    show = [s[0:1] for s in show]
    fold = [f[0:1] for f in fold]
    unit = CODE / ONE_TOP
    stage[...] = jnp.zeros_like(stage)
    y_stage[:, 120:ROWS] = jnp.zeros((WORKERS, ROWS - 120, 128), F32)
    pl.semaphore_wait(barrier, PEERS - 1 + lines - 1)

    def line_copy(src, dst, sends, recvs, peer, slot):
        return pltpu.make_async_remote_copy(
            src_ref=src,
            dst_ref=dst.at[slot],
            send_sem=sends.at[peer],
            recv_sem=recvs.at[slot],
            device_id=(peer, leaf),
            device_id_type=MESH,
        )

    def line_start(src, dst, sends, recvs):
        for k in range(1, lines):
            line_copy(src, dst, sends, recvs, lax.rem(line + k, lines), line).start()

    def line_sum(src, dst, sends, recvs):
        dst[line] = src[...]

        for k in range(1, lines):
            peer = lax.rem(line + k, lines)
            line_copy(src, dst, sends, recvs, peer, peer).wait_recv()
        total = dst[0]
        for t in range(1, lines):
            total = total + dst[t]
        return total

    def line_sent(src, dst, sends, recvs):
        def wait(k, carry):
            line_copy(src, dst, sends, recvs, lax.rem(line + k, lines), line).wait_send()
            return carry

        lax.fori_loop(1, lines, wait, 0)

    line_start(turn_regret, turns, turn_send, turn_recv)

    def y_copy(part, w, peer, slot):
        rows = (pl.ds(0, SPLIT), pl.ds(SPLIT, ROWS - SPLIT))[part]
        return pltpu.make_async_remote_copy(
            src_ref=yq.at[w, rows],
            dst_ref=recv.at[slot, rows],
            send_sem=y_send.at[part, w],
            recv_sem=y_recv.at[part, slot],
            device_id=(line, peer),
            device_id_type=MESH,
        )

    def hand_over(part, w):
        peer = worker_leaf(w, line)
        rows = (pl.ds(0, SPLIT), pl.ds(SPLIT, ROWS - SPLIT))[part]
        yq[w, rows] = code(y_stage[w, rows])

        @pl.when(peer != leaf)
        def _():
            y_copy(part, w, peer, leaf).start()

        @pl.when(peer == leaf)
        def _():
            recv[leaf, rows] = yq[w, rows]

    def prepare_one(k, carry):
        workers = [forward_worker(TRIO * k + m) for m in range(TRIO)]
        for w in workers:
            regrets, scale = one_regrets(ro, w, lane, hands)
            for b in range(MOVES_ONE):
                kept[w, b, 0:hands] = regrets[b]
            kept[w, 3, 0:hands] = scale
            o = [(weight_one * (r * scale)).astype(BF16).astype(F32) for r in regrets]
            for j, pot in enumerate((show, fold)):
                mixed = o[0] * pot[0] + o[1] * pot[1] + o[2] * pot[2]
                y_stage[w, j * hands : (j + 1) * hands] = nearest(mixed * unit)
        for w in workers:
            hand_over(0, w)
        return carry

    lax.fori_loop(0, WORKERS // TRIO, prepare_one, 0)
    turn_share = turn_regret[...] / line_sum(turn_regret, turns, turn_send, turn_recv)
    weight_zero = to_lanes(range_zero[...] * turn_share)

    def prepare_zero(k, carry):
        workers = [forward_worker(TRIO * k + m) for m in range(TRIO)]
        for w in workers:
            _, zs = zero_shares(rz, w, lane, hands)
            kept[w, 4, 0:hands] = zs
            z = (weight_zero * zs).astype(BF16).astype(F32)
            power = power_above(jnp.max(z, axis=0, keepdims=True))
            y_stage[w, 2 * hands : 3 * hands] = nearest(z * (CODE * jnp.exp2(-power)))
            y_stage[w, 3 * hands : 3 * hands + 1] = power
        for w in workers:
            hand_over(1, w)
        return carry

    lax.fori_loop(0, WORKERS // TRIO, prepare_zero, 0)

    def out_copy(peer):
        return pltpu.make_async_remote_copy(
            src_ref=out.at[peer],
            dst_ref=back.at[w_self],
            send_sem=out_send.at[peer],
            recv_sem=out_recv.at[w_self],
            device_id=(line, peer),
            device_id_type=MESH,
        )

    @pl.when(is_worker)
    def _():
        low = lanes(8)[0:1] < 64
        source_hand = lax.broadcasted_iota(jnp.int32, (PEERS * hands, 128), 0)
        place = source_hand + (HP - hands) * (source_hand // hands)
        for j in range(KP // 128):
            here = lanes(PEERS * hands) + 128 * j
            spread[:, pl.ds(128 * j, 128)] = (place == here).astype(F32).astype(BF16)
        card_pad[...] = jnp.zeros_like(card_pad)
        card_pad[0:2] = (cards[...] + 1).astype(F32)
        eight = pl.ds(pl.multiple_of(8 * (w_self // 4), 8), 8)
        ranks = all_ranks[eight].astype(F32)
        high = jnp.floor(ranks * (1.0 / 64.0))
        rest = ranks - 64.0 * high

        def spread_rows(v):
            return jnp.dot(v.astype(BF16), spread[...], preferred_element_type=F32)

        card_rows = spread_rows(card_pad[...]).astype(BF16)
        high_rows = spread_rows(high)
        rest_rows = spread_rows(rest)
        one_row = lax.broadcasted_iota(jnp.int32, (8, 128), 0)
        pick = lambda r, scale: jnp.where(one_row == r, scale, 0.0).astype(BF16)
        first = column(card_rows, pick(0, 1.0)) - 1.0
        second = column(card_rows, pick(1, 1.0)) - 1.0
        usable = (first < 52.0) & (second < 52.0) & (first >= 0.0)
        for k in range(4):
            board = dealt[k].astype(F32)
            usable = usable & (first != board) & (second != board)
        rivers = [dealt[4 + 2 * w_self + c].astype(F32) for c in range(2)]
        river = jnp.where(low, rivers[0], rivers[1])
        col[2] = (usable & (first != river) & (second != river)).astype(F32)
        card = lanes(KP).astype(F32)
        inc[...] = ((first == card) | (second == card)).astype(F32).astype(BF16)
        rank_rows = 64.0 * high_rows + rest_rows
        wide_row = lax.broadcasted_iota(jnp.int32, (8, KP), 0)
        for c in range(2):
            r = 2 * lax.rem(w_self, 4) + c
            rank_row[c : c + 1] = jnp.sum(
                jnp.where(wide_row == r, rank_rows, 0.0), axis=0, keepdims=True
            )
            col[c] = column(high_rows.astype(BF16), pick(r, 64.0)) + column(
                rest_rows.astype(BF16), pick(r, 1.0)
            )

        def build(i, carry):
            rows = pl.ds(pl.multiple_of(i * MB, MB), MB)
            for j in range(KP // 128):
                js = pl.ds(128 * j, 128)
                shared = lax.dot_general(
                    inc[rows], inc[js], (((1,), (1,)), ((), ())), preferred_element_type=F32
                )
                apart = jnp.maximum(1.0 - shared, 0.0)
                mat[2, rows, js] = apart.astype(BF16)
                for c in range(2):
                    gap = col[c, rows] - rank_row[c : c + 1, js]
                    sign = jnp.minimum(jnp.maximum(gap, -1.0), 1.0)
                    mat[c, rows, js] = (sign * apart).astype(BF16)
            return carry

        lax.fori_loop(0, KP // MB, build, 0)

        def arrival(part, k):
            source_z = lax.rem(z_self - far_first(k, 4) + 16, 8)
            for m in range(PLANE):
                source = PLANE * source_z + m

                @pl.when(source != leaf)
                def _():
                    y_copy(part, 0, source, source).wait_recv()

            rows = pl.ds(pl.multiple_of(source_z * (PLANE * HP), PLANE * HP), PLANE * HP)
            return pl.ds(PLANE * source_z, PLANE), rows, col[2, rows]

        def flat(v):
            return v.reshape(PLANE * HP, 128)

        def arrive_one(k, w_sum):
            sources, rows, v = arrival(0, k)
            ws = flat(decode(recv[sources, 0:HP])) * v
            s_high = jnp.floor(ws * (1.0 / 256.0))
            s_low = ws - 256.0 * s_high
            x[rows, 384:512] = jnp.where(low, s_high, roll_half(s_low)).astype(BF16)
            x[rows, 640:768] = jnp.where(low, roll_half(s_high), s_low).astype(BF16)
            return w_sum + ws

        def arrive_two(k, carry):
            z_sum, w_sum = carry
            sources, rows, v = arrival(1, k)
            stage[0:PLANE, 32:ROWS] = decode(recv[sources, 32:ROWS])
            scale = jnp.exp2(stage[0:PLANE, 3 * hands : 3 * hands + 1]) * (1.0 / CODE)
            wf = flat(stage[0:PLANE, hands : hands + HP]) * v
            z = (flat(stage[0:PLANE, 2 * hands : 2 * hands + HP] * scale) * v).astype(BF16)
            f_high = jnp.floor(wf * (1.0 / 256.0))
            f_low = wf - 256.0 * f_high
            x[rows, 0:128] = f_high.astype(BF16)
            x[rows, 128:256] = f_low.astype(BF16)
            x[rows, 256:384] = z
            x[rows, 512:640] = z
            return (z_sum + z.astype(F32), w_sum + jnp.abs(wf))

        empty = jnp.zeros((PLANE * HP, 128), F32)
        w_sum = lax.fori_loop(0, PEERS // PLANE, arrive_one, empty)
        z_sum, w_sum = lax.fori_loop(0, PEERS // PLANE, arrive_two, (empty, w_sum))
        z_power = power_above(jnp.sum(z_sum, axis=0, keepdims=True))
        w_power = power_above(jnp.sum(w_sum, axis=0, keepdims=True) * (1.0 / unit))
        z_scale = CODE * jnp.exp2(-z_power)
        w_scale = (CODE / unit) * jnp.exp2(-w_power)
        low_part = jnp.where(low, 256.0, 1.0)

        def block(k, carry):
            i = lax.rem(z_self // 2 + far_first(k, 2), 4)
            rows = pl.ds(pl.multiple_of(i * BLOCK, BLOCK), BLOCK)
            d = jnp.dot(mat[2, rows], x[:, 0:384], preferred_element_type=F32)
            s0 = jnp.dot(mat[0, rows], x[:, 256:512], preferred_element_type=F32)
            s1 = jnp.dot(mat[1, rows], x[:, 512:768], preferred_element_type=F32)
            s0z, s0w = s0[:, 0:128], s0[:, 128:256]
            s1z, s1w = s1[:, 0:128], s1[:, 128:256]
            v = col[2, rows]
            s0w = s0w * low_part
            s1w = s1w * low_part
            s0w = s0w + roll_half(s0w)
            s1w = s1w + roll_half(s1w)
            act = jnp.where(low, s0w, s1w) + 256.0 * d[:, 0:128] + d[:, 128:256]
            tiles = (
                act * (v * w_scale),
                jnp.where(low, s0z, s1z) * (v * z_scale),
                d[:, 256:384] * (v * z_scale),
            )
            tiles = [nearest(jnp.minimum(jnp.maximum(t, -CODE), CODE)) for t in tiles]
            for m in range(BLOCK // HP):
                for j in range(3):
                    stage[m, j * hands : j * hands + HP] = tiles[j][m * HP : (m + 1) * HP]
                stage[m, 3 * hands : 3 * hands + 1] = w_power
                stage[m, 3 * hands + 1 : 3 * hands + 2] = z_power
                peer = i * (BLOCK // HP) + m
                out[peer] = code(stage[m, 0:ROWS])

                @pl.when(peer != leaf)
                def _():
                    out_copy(peer).start()

                @pl.when(peer == leaf)
                def _():
                    back[w_self] = out[peer]

            return carry

        lax.fori_loop(0, KP // BLOCK, block, 0)

    def first_of(k):
        pair = lax.rem(z_self // 2 - far_first(k // 2, 2) + 8, 4)
        return TRIO * (2 * pair + lax.rem(k, 2))

    def values_of(w, slot):
        stage[slot, 0:ROWS] = decode(back[w])
        w_scale = jnp.exp2(stage[slot, 3 * hands : 3 * hands + 1]) * (1.0 / CODE)
        z_scale = jnp.exp2(stage[slot, 3 * hands + 1 : 3 * hands + 2]) * (1.0 / CODE)
        act = stage[slot, 0:hands] * w_scale
        sz = stage[slot, hands : 2 * hands] * z_scale
        dz = stage[slot, 2 * hands : 3 * hands] * z_scale
        node = action_sum(kept[w, 4, 0:hands] * act, lane)
        regrets = [kept[w, b, 0:hands] for b in range(MOVES_ONE)]
        leaf_one = [show[b] * sz - fold[b] * dz for b in range(MOVES_ONE)]
        node_one = regrets[0] * leaf_one[0] + regrets[1] * leaf_one[1] + regrets[2] * leaf_one[2]
        return w, act, node, regrets, leaf_one, node_one * kept[w, 3, 0:hands]

    def collect(w):
        peer = worker_leaf(w, line)

        @pl.when(peer != leaf)
        def _():
            pltpu.make_async_remote_copy(
                src_ref=out.at[0],
                dst_ref=back.at[w],
                send_sem=out_send.at[0],
                recv_sem=out_recv.at[w],
                device_id=(line, peer),
                device_id_type=MESH,
            ).wait_recv()

    def renew(values):
        w, act, node, regrets, leaf_one, node_one = values
        r = rz[pl.ds(w, hands, stride=WORKERS)]
        new_rz[pl.ds(w, hands, stride=WORKERS)] = jnp.maximum(r + act - node, 0.0)
        new = [jnp.maximum(regrets[b] + leaf_one[b] - node_one, 0.0) for b in range(MOVES_ONE)]
        native = join_moves(new, lane)
        for v in range(3):
            new_ro[pl.ds(3 * w + v, hands, stride=3 * WORKERS)] = native[v]

    def trio_values(k, arriving):
        first = first_of(k)
        if arriving:
            for m in range(TRIO):
                collect(first + m)
        return [values_of(first + m, m) for m in range(TRIO)]

    def added(carry, trio):
        sum_zero, sum_one = carry
        for values in trio:
            sum_zero = sum_zero + values[2]
            sum_one = sum_one + values[5]
        return sum_zero, sum_one

    def update(k, carry):
        trio = trio_values(k, True)
        for values in trio:
            renew(values)
        return added(carry, trio)

    def sum_only(k, carry):
        return added(carry, trio_values(k, True))

    def finish(k, carry):
        for values in trio_values(k, False):
            renew(values)
        return carry

    zero = jnp.zeros((hands, 128), F32)
    sums = lax.fori_loop(0, EARLY, update, (zero, zero))
    sum_zero, sum_one = lax.fori_loop(EARLY, WORKERS // TRIO, sum_only, sums)
    sum_zero = jnp.where(lane % 64 < SUBGAMES, sum_zero, 0.0)
    values = [
        CHANCE
        * lax.dot_general(
            tile_selector(),
            total,
            (((1,), (1,)), ((), ())),
            precision=lax.Precision.HIGHEST,
            preferred_element_type=F32,
        )
        for total in (sum_zero, sum_one)
    ]
    own[0] = turn_share * values[0]
    own[1] = values[1]
    line_start(own, parts, root_send, root_recv)
    lax.fori_loop(EARLY, WORKERS // TRIO, finish, 0)
    stores = [
        pltpu.make_async_copy(new_rz, rz_out, store_sem.at[0]),
        pltpu.make_async_copy(new_ro, ro_out, store_sem.at[1]),
    ]
    for store in stores:
        store.start()
    total = line_sum(own, parts, root_send, root_recv)
    roots[...] = total
    new_turn[...] = jnp.maximum(turn_regret[...] + values[0] - total[0], 0.0)

    def y_sent(k, carry):
        w = forward_worker(k)
        peer = worker_leaf(w, line)

        @pl.when(peer != leaf)
        def _():
            y_copy(0, w, peer, leaf).wait_send()
            y_copy(1, w, peer, leaf).wait_send()

        return carry

    lax.fori_loop(0, WORKERS, y_sent, 0)

    @pl.when(is_worker)
    def _():
        def sent(k, carry):
            out_copy(lax.rem(leaf + k, PEERS)).wait_send()
            return carry

        lax.fori_loop(1, PEERS, sent, 0)

    line_sent(turn_regret, turns, turn_send, turn_recv)
    line_sent(own, parts, root_send, root_recv)
    for store in stores:
        store.wait()


def place_kernel(*refs):
    count = (len(refs) - 2) // 3
    srcs, dsts, held = refs[:count], refs[count : 2 * count], refs[2 * count : 3 * count]
    load_sem, store_sem = refs[-2], refs[-1]
    pieces = []
    for k in range(count):
        rows = srcs[k].shape[0]
        parts = PIECES if rows % (8 * PIECES) == 0 else 1
        for m in range(parts):
            piece = pl.ds(m * (rows // parts), rows // parts)
            pieces.append((srcs[k].at[piece], held[k].at[piece], dsts[k].at[piece]))
    loads = [pltpu.make_async_copy(p[0], p[1], load_sem.at[n]) for n, p in enumerate(pieces)]
    stores = [pltpu.make_async_copy(p[1], p[2], store_sem.at[n]) for n, p in enumerate(pieces)]
    for load in loads:
        load.start()
    for load, store in zip(loads, stores):
        load.wait()
        store.start()
    for store in stores:
        store.wait()


VM = pl.BlockSpec(memory_space=pltpu.VMEM)
HB = pl.BlockSpec(memory_space=pl.ANY)
LIMIT = 56 << 20


def local(
    range_zero,
    range_one,
    turn_regret,
    river_regret_zero,
    river_regret_one,
    hand_cards,
    dealt_cards,
    hand_ranks,
    leaf_pots,
    leaf_kinds,
):
    hands = range_zero.shape[1]
    lines = lax.axis_size("river")
    tr = turn_regret[0]
    rz = river_regret_zero.reshape(hands * WORKERS, 128)
    ro = river_regret_one.reshape(hands * 3 * WORKERS, 128)
    dma = pltpu.SemaphoreType.DMA
    i16 = jnp.int16
    new_turn, new_rz, new_ro, roots = pl.pallas_call(
        kernel,
        out_shape=(
            jax.ShapeDtypeStruct(tr.shape, F32),
            jax.ShapeDtypeStruct(rz.shape, F32),
            jax.ShapeDtypeStruct(ro.shape, F32),
            jax.ShapeDtypeStruct((2,) + tr.shape, F32),
        ),
        in_specs=[HB] * 10,
        out_specs=(VM, HB, HB, VM),
        scratch_shapes=[
            pltpu.VMEM(tr.shape, F32),
            pltpu.VMEM(ro.shape, F32),
            pltpu.VMEM(tr.shape, F32),
            pltpu.SMEM(leaf_pots.shape, jnp.int32),
            pltpu.SMEM(leaf_kinds.shape, jnp.int32),
            pltpu.VMEM(rz.shape, F32),
            pltpu.VMEM(tr.shape, F32),
            pltpu.VMEM((2, PEERS * hands), jnp.int32),
            pltpu.VMEM(hand_ranks.shape, jnp.int32),
            pltpu.SMEM(dealt_cards.shape, jnp.int32),
            pltpu.VMEM(rz.shape, F32),
            pltpu.VMEM(ro.shape, F32),
            pltpu.VMEM((lines,) + tr.shape, F32),
            pltpu.VMEM((WORKERS, ROWS, 128), i16),
            pltpu.VMEM((PEERS, ROWS, 128), i16),
            pltpu.VMEM((WORKERS, 5, HP, 128), F32),
            pltpu.VMEM((WORKERS, ROWS, 128), F32),
            pltpu.VMEM((BLOCK // HP, STAGE, 128), F32),
            pltpu.VMEM((PEERS * hands, KP), BF16),
            pltpu.VMEM((8, PEERS * hands), F32),
            pltpu.VMEM((8, KP), F32),
            pltpu.VMEM((KP, 768), BF16),
            pltpu.VMEM((3, KP, KP), BF16),
            pltpu.VMEM((3, KP, 128), F32),
            pltpu.VMEM((KP, 128), BF16),
            pltpu.VMEM((PEERS, ROWS, 128), i16),
            pltpu.VMEM((WORKERS, ROWS, 128), i16),
            pltpu.VMEM((2,) + tr.shape, F32),
            pltpu.VMEM((lines, 2) + tr.shape, F32),
            dma((10,)),
            dma((2,)),
            dma((lines,)),
            dma((lines,)),
            dma((2, WORKERS)),
            dma((2, PEERS)),
            dma((PEERS,)),
            dma((WORKERS,)),
            dma((lines,)),
            dma((lines,)),
        ],
        compiler_params=pltpu.CompilerParams(
            collective_id=1, has_side_effects=True, vmem_limit_bytes=LIMIT
        ),
    )(
        tr,
        ro,
        range_one,
        leaf_pots,
        leaf_kinds,
        rz,
        range_zero,
        hand_cards.T,
        hand_ranks,
        dealt_cards,
    )
    results = (new_turn, new_rz, new_ro, roots)
    new_turn, new_rz, new_ro, roots = pl.pallas_call(
        place_kernel,
        out_shape=tuple(jax.ShapeDtypeStruct(r.shape, F32) for r in results),
        in_specs=[HB] * 4,
        out_specs=(HB,) * 4,
        scratch_shapes=[pltpu.VMEM(r.shape, F32) for r in results] + [dma((4 * PIECES,)), dma((4 * PIECES,))],
    )(*results)
    return (
        new_turn[None],
        new_rz.reshape(river_regret_zero.shape),
        new_ro.reshape(river_regret_one.shape),
        roots,
    )


def solution(mesh):
    placed = (
        P(None, "leaf"),
        P(None, "leaf"),
        P("river", None, "leaf"),
        P("river", "leaf", None),
        P("river", "leaf", None),
        P(),
        P(),
        P(),
        P("river", None),
        P("river", None),
    )
    return jax.shard_map(
        local,
        mesh=mesh,
        in_specs=placed,
        out_specs=(
            P("river", None, "leaf"),
            P("river", "leaf", None),
            P("river", "leaf", None),
            P(None, None, "leaf"),
        ),
        check_vma=False,
    )
```
